128 devices in a mesh: comp: 8 (over z, core), sub: 16 (over y, x).
Axes of the slice: x: 4, y: 4, z: 4, core: 2. Of those that a mesh axis runs over, the one named last changes fastest.
Arguments:
- atmos_profiles: bfloat16 [4, 72, 1048576], P(None, None, ('comp', 'sub')), may hold values from -6 to 6
- atmos_mixing: bfloat16 [72, 72], replicated
- drag_factor: float32 [1048576], P(('comp', 'sub')), may hold values from 0.5 to 1.5
- surface_before: float32 [4, 1048576], P(None, ('comp', 'sub')), may hold values from -6 to 6
- downward_fluxes: float32 [4, 1048576], P(None, ('comp', 'sub')), may hold values from -6 to 6
- land_weight: float32 [1048576], P(('comp', 'sub')), may hold values from 0.05 to 1
- land_surface: float32 [4, 1048576], P(None, ('comp', 'sub')), may hold values from -6 to 6
- ocean_state: float32 [4, 60, 1048576], P(None, None, ('comp', 'sub')), may hold values from -6 to 6
- ocean_mixing: float32 [60, 60], replicated
- sea_mask: int32 [1048576], P(('comp', 'sub')), may hold values 0 or 1
- exchange_slot: int32 [4, 1048576], P(None, ('comp', 'sub')), may hold values from 0 to 65535, as said below
- parent_column: int32 [4, 1048576], P(None, ('comp', 'sub')), may hold values from 0 to 8191, as said below
- ocean_weight: float32 [4, 1048576], P(None, ('comp', 'sub')), may hold values from 0.1 to 1
- atmos_weight: float32 [4, 1048576], P(None, ('comp', 'sub')), may hold values from 0.05 to 0.5
Outputs:
- atmos_updated: bfloat16 [4, 72, 1048576], P(None, None, ('comp', 'sub'))
- ocean_updated: float32 [4, 60, 1048576], P(None, None, ('comp', 'sub'))
- surface_state: float32 [4, 1048576], P(None, ('comp', 'sub'))
The draws below stay inside these ranges and needn't reach their ends.
Inputs may be any that keep to these rules, and one draw needn't show every extreme that they name: Within the 8192 cells of one device block along the second dimension, all 32768 values are distinct, at most 512 of them share one value of exchange_slot // 512, and in every block some value of exchange_slot // 512 is shared by exactly 512 of them. In every aligned group of 128 cells along the second dimension (one k), the values are t * 128 + 0, 1, ..., 127 in order, for one t. In every aligned group of 128 cells along the second dimension (one k), all values share one value of parent_column // 128.
All inputs are finite; a program needn't handle non-finite values. No bound on the sum of `sea_mask` on one device may be relied on, other than what follows from the above.
Results may differ from the reference program's by a relative error of at most 0.001.
Values sent between devices are 32-bit elements; how exact they have to be, the bound alone decides.
A program may use at most 128 MiB of HBM per device.

```python
import math
import jax
import jax.numpy as jnp
from jax import lax

LEVELS_ATMOS = 72
LEVELS_OCEAN = 60
INTERSECTIONS = 4
COLUMNS_DEV = 8192
CELLS_DEV = 8192
CAPACITY = 512
TILE = 128
COLUMNS = 1048576
CELLS = 1048576
DEVICES = 128


def mixing_matrix(key, extent):
    main_key, rest_key = jax.random.split(key)
    main = jax.random.uniform(main_key, (extent,), jnp.float32, 0.5, 1.0)
    spread = jax.random.normal(rest_key, (extent, extent), jnp.float32) * (0.25 / math.sqrt(extent))
    return jnp.diag(main) + spread


def draw_atmos_mixing(key, part):
    return mixing_matrix(jax.random.fold_in(key, 3), LEVELS_ATMOS).astype(jnp.bfloat16)


def draw_ocean_mixing(key, part):
    return mixing_matrix(jax.random.fold_in(key, 5), LEVELS_OCEAN)


def slot_tables(key):
    tile_slots = DEVICES * CAPACITY // TILE
    tiles_dev = INTERSECTIONS * CELLS_DEV // TILE
    per_owner = CAPACITY // TILE

    def one_device(device_key):
        bias_key, full_key, score_key, order_key = jax.random.split(device_key, 4)
        source = jnp.arange(tile_slots, dtype=jnp.int32) // per_owner
        favour = jax.random.randint(bias_key, (DEVICES,), 0, 4) * 16384
        chosen = jax.random.randint(full_key, (), 0, DEVICES)
        scores = jax.random.randint(score_key, (tile_slots,), 0, 16384) + favour[source]
        scores = scores + jnp.where(source == chosen, 131072, 0)
        picked = jnp.argsort(-scores, stable=True)[:tiles_dev]
        shuffle = jax.random.permutation(order_key, tiles_dev)
        starts = picked[shuffle].astype(jnp.int32) * TILE
        lanes = jnp.arange(TILE, dtype=jnp.int32)
        return (starts[:, None] + lanes[None, :]).reshape(INTERSECTIONS, CELLS_DEV)
    tables = jax.vmap(one_device)(jax.random.split(key, DEVICES))
    return tables.transpose(1, 0, 2).reshape(INTERSECTIONS, DEVICES * CELLS_DEV)


def draw_exchange_slot(key, part):
    return slot_tables(jax.random.fold_in(key, 11))


def draw_parent_column(key, part):
    window_key, lane_key = jax.random.split(jax.random.fold_in(key, 13))
    window = jax.random.randint(window_key, (INTERSECTIONS, CELLS // TILE), 0, COLUMNS_DEV // TILE)
    lanes = jax.random.randint(lane_key, (INTERSECTIONS, CELLS), 0, TILE)
    return (jnp.repeat(window, TILE, axis=1) * TILE + lanes).astype(jnp.int32)


def set_ends(array, key, least, largest):
    index_at = [jax.random.randint(jax.random.fold_in(key, axis), (), 0, length) for axis, length in enumerate(array.shape)]
    widest = array.shape.index(max(array.shape))
    beside = index_at[:widest] + [(index_at[widest] + 1) % array.shape[widest]] + index_at[widest + 1:]
    return array.at[tuple(index_at)].set(least).at[tuple(beside)].set(largest)


def levels(stream_key, shape, cuts, least, top_value):
    loudness = 1.0
    for position, parts in cuts:
        draws = jax.random.uniform(jax.random.fold_in(jax.random.fold_in(stream_key, 6), position), (parts,), jnp.float32, least / len(cuts), top_value / len(cuts))
        loudness = loudness * jnp.repeat(jnp.exp(draws), shape[position] // parts).reshape((-1,) + (1,) * (len(shape) - 1 - position))
    return loudness


def normal_values(key, dims, deviation, bound, cuts=(), kind=jnp.bfloat16):
    values = deviation * jax.random.normal(key, dims, jnp.float32)
    if cuts:
        values = values * levels(key, dims, cuts, -0.22, 0.18)
    return jnp.clip(values, -bound, bound).astype(kind)


def setup_inputs(seed: int = 0) -> dict:
    streams_of = jax.random.split(jax.random.key(seed), 15)
    atmos_profiles = normal_values(streams_of[0], (4, LEVELS_ATMOS, COLUMNS), 1.0, 6.0, ((2, 128),))
    atmos_mixing = draw_atmos_mixing(jax.random.fold_in(streams_of[14], 71), 0)
    drag_factor = jnp.clip(jnp.exp(math.log(1.5) - 1.0986123 * jax.random.uniform(streams_of[2], (COLUMNS,), jnp.float32) ** levels(streams_of[2], (COLUMNS,), ((0, 128),), -0.2, 0.2)), 0.5, 1.5)
    surface_before = normal_values(streams_of[3], (4, COLUMNS), 1.0, 6.0, ((1, 128),), jnp.float32)
    downward_fluxes = normal_values(streams_of[4], (4, COLUMNS), 1.0, 6.0, ((1, 128),), jnp.float32)
    land_weight = jnp.clip(jnp.exp(math.log(1.0) - 2.9957323 * jax.random.uniform(streams_of[5], (COLUMNS,), jnp.float32) ** levels(streams_of[5], (COLUMNS,), ((0, 128),), -0.2, 0.2)), 0.05, 1.0)
    land_surface = normal_values(streams_of[6], (4, COLUMNS), 1.0, 6.0, ((1, 128),), jnp.float32)
    ocean_state = normal_values(streams_of[7], (4, LEVELS_OCEAN, CELLS), 1.0, 6.0, ((2, 128),), jnp.float32)
    ocean_mixing = draw_ocean_mixing(jax.random.fold_in(streams_of[14], 71), 0)
    sea_mask = set_ends((jax.random.randint(streams_of[9], (CELLS,), 0, 4) < 3).astype(jnp.int32), jax.random.fold_in(streams_of[9], 1), 0, 1)
    exchange_slot = draw_exchange_slot(jax.random.fold_in(streams_of[14], 71), 0)
    parent_column = draw_parent_column(jax.random.fold_in(streams_of[14], 71), 0)
    ocean_weight = jnp.clip(jnp.exp(math.log(1.0) - 2.3025851 * jax.random.uniform(streams_of[12], (INTERSECTIONS, CELLS), jnp.float32) ** levels(streams_of[12], (INTERSECTIONS, CELLS), ((1, 128),), -0.2, 0.2)), 0.1, 1.0)
    atmos_weight = jnp.clip(jnp.exp(math.log(0.5) - 2.3025851 * jax.random.uniform(streams_of[13], (INTERSECTIONS, CELLS), jnp.float32) ** levels(streams_of[13], (INTERSECTIONS, CELLS), ((1, 128),), -0.2, 0.2)), 0.05, 0.5)
    return {"atmos_profiles": atmos_profiles, "atmos_mixing": atmos_mixing, "drag_factor": drag_factor, "surface_before": surface_before, "downward_fluxes": downward_fluxes, "land_weight": land_weight, "land_surface": land_surface, "ocean_state": ocean_state, "ocean_mixing": ocean_mixing, "sea_mask": sea_mask, "exchange_slot": exchange_slot, "parent_column": parent_column, "ocean_weight": ocean_weight, "atmos_weight": atmos_weight}


couple_rate = 0.5

def surface_fluxes(atmos_profiles, drag_factor, surface_before, downward_fluxes):
    bottom = atmos_profiles[:, -1, :].astype(jnp.float32)
    east_gap = bottom[2] - surface_before[2]
    north_gap = bottom[3] - surface_before[3]
    wind_speed = jnp.sqrt(1.0 + east_gap * east_gap + north_gap * north_gap)
    transfer = drag_factor * wind_speed
    sensible = transfer * (surface_before[0] - bottom[0])
    latent = transfer * (surface_before[1] - bottom[1])
    return jnp.stack([sensible, latent, transfer * east_gap, transfer * north_gap, downward_fluxes[0], downward_fluxes[1], downward_fluxes[2], downward_fluxes[3]])

def diffuse_atmos(atmos_profiles, atmos_mixing, fluxes):
    lowest = atmos_mixing[:, -1].astype(jnp.float32)
    tendency = couple_rate * jnp.stack([fluxes[0], fluxes[1], -fluxes[2], -fluxes[3]])
    result = []
    for member in range(4):
        mixed_rows = jnp.dot(atmos_mixing, atmos_profiles[member], preferred_element_type=jnp.float32)
        result.append(mixed_rows + lowest[:, None] * tendency[member][None, :])
    return jnp.stack(result).astype(jnp.bfloat16)

def forcing_rows(fluxes):
    return couple_rate * jnp.stack([fluxes[4] + fluxes[5] - fluxes[0] - fluxes[1], fluxes[1] - fluxes[6] - fluxes[7], fluxes[2], fluxes[3]])

def reference(atmos_profiles, atmos_mixing, drag_factor, surface_before, downward_fluxes, land_weight, land_surface, ocean_state, ocean_mixing, sea_mask, exchange_slot, parent_column, ocean_weight, atmos_weight):
    fluxes = surface_fluxes(atmos_profiles, drag_factor, surface_before, downward_fluxes)
    atmos_updated = diffuse_atmos(atmos_profiles, atmos_mixing, fluxes)
    column_forcing = forcing_rows(fluxes)
    parent = exchange_slot // CAPACITY * COLUMNS_DEV + parent_column
    flat_parent = parent.reshape(-1).astype(jnp.int32)
    at_cells = jnp.take(column_forcing, flat_parent, axis=1).reshape(4, INTERSECTIONS, CELLS)
    forcing = lax.optimization_barrier(jnp.sum(ocean_weight[None] * at_cells, axis=1)) / lax.optimization_barrier(jnp.sum(ocean_weight, axis=0))[None]
    loaded = ocean_state.at[:, 0, :].add(forcing)
    mixed_state = jnp.stack([jnp.dot(ocean_mixing, loaded[member], precision=lax.Precision.HIGHEST) for member in range(4)])
    ocean_updated = jnp.where(sea_mask[None, None, :] == 1, mixed_state, ocean_state)
    sea_share = atmos_weight * sea_mask.astype(jnp.float32)[None, :]
    outgoing = jnp.concatenate([sea_share[None] * ocean_updated[:, 0, :][:, None, :], sea_share[None]], axis=0)
    summed = jnp.zeros((5, COLUMNS), jnp.float32).at[:, flat_parent].add(outgoing.reshape(5, -1))
    surface_state = (summed[:4] + land_weight[None] * land_surface) / (summed[4] + land_weight)[None]
    return (atmos_updated, ocean_updated, surface_state)
```

```python
import jax
import jax.numpy as jnp
from jax import lax
from jax.experimental import pallas as pl
from jax.experimental.pallas import tpu as pltpu
from jax.sharding import PartitionSpec as P

couple_rate = 0.5
highest = lax.Precision.HIGHEST
high = lax.Precision.HIGH


def surface_fluxes(atmos_profiles, drag_factor, surface_before, downward_fluxes):
    bottom = atmos_profiles[:, -1, :].astype(jnp.float32)
    east_gap = bottom[2] - surface_before[2]
    north_gap = bottom[3] - surface_before[3]
    wind_speed = jnp.sqrt(1.0 + east_gap * east_gap + north_gap * north_gap)
    transfer = drag_factor * wind_speed
    sensible = transfer * (surface_before[0] - bottom[0])
    latent = transfer * (surface_before[1] - bottom[1])
    return jnp.stack(
        [
            sensible,
            latent,
            transfer * east_gap,
            transfer * north_gap,
            downward_fluxes[0],
            downward_fluxes[1],
            downward_fluxes[2],
            downward_fluxes[3],
        ]
    )


def diffuse_atmos(atmos_profiles, atmos_mixing, fluxes):
    lowest = atmos_mixing[:, -1].astype(jnp.float32)
    tendency = couple_rate * jnp.stack([fluxes[0], fluxes[1], -fluxes[2], -fluxes[3]])
    result = []
    for member in range(4):
        mixed_rows = jnp.dot(
            atmos_mixing, atmos_profiles[member], preferred_element_type=jnp.float32
        )
        result.append(mixed_rows + lowest[:, None] * tendency[member][None, :])
    return jnp.stack(result).astype(jnp.bfloat16)


def forcing_rows(fluxes):
    return couple_rate * jnp.stack(
        [
            fluxes[4] + fluxes[5] - fluxes[0] - fluxes[1],
            fluxes[1] - fluxes[6] - fluxes[7],
            fluxes[2],
            fluxes[3],
        ]
    )


def lane_gather_kernel(win_ref, lanes_ref, out_ref):
    lanes = lanes_ref[...]
    for field in range(win_ref.shape[0]):
        out_ref[field] = jnp.take_along_axis(
            win_ref[field], lanes, axis=1, mode="promise_in_bounds"
        )


def lane_gather(win, lanes):
    return pl.pallas_call(
        lane_gather_kernel,
        out_shape=jax.ShapeDtypeStruct(win.shape, win.dtype),
        in_specs=[pl.BlockSpec(memory_space=pltpu.VMEM)] * 2,
        out_specs=pl.BlockSpec(memory_space=pltpu.VMEM),
    )(win, lanes)


def ocean_kernel(m_ref, m0_ref, x_ref, forcing_ref, sea_ref, out_ref, top_ref):
    m = m_ref[...]
    m0 = m0_ref[...]
    sea = sea_ref[...] == 1
    for field in range(x_ref.shape[1]):
        x = x_ref[:, field, :]
        mixed = jnp.dot(m, x, precision=highest, preferred_element_type=jnp.float32)
        mixed = mixed + m0 * forcing_ref[field : field + 1, :]
        updated = jnp.where(sea, mixed, x)
        out_ref[:, field, :] = updated
        top_ref[field : field + 1, :] = updated[0:1, :]


def ocean_update(ocean_mixing, state_by_level, forcing, sea_mask, block=1024):
    levels, fields, cells = state_by_level.shape
    return pl.pallas_call(
        ocean_kernel,
        grid=(cells // block,),
        out_shape=(
            jax.ShapeDtypeStruct(state_by_level.shape, jnp.float32),
            jax.ShapeDtypeStruct((fields, cells), jnp.float32),
        ),
        in_specs=[
            pl.BlockSpec((levels, levels), lambda i: (0, 0)),
            pl.BlockSpec((levels, 1), lambda i: (0, 0)),
            pl.BlockSpec((levels, fields, block), lambda i: (0, 0, i)),
            pl.BlockSpec((fields, block), lambda i: (0, i)),
            pl.BlockSpec((1, block), lambda i: (0, i)),
        ],
        out_specs=(
            pl.BlockSpec((levels, fields, block), lambda i: (0, 0, i)),
            pl.BlockSpec((fields, block), lambda i: (0, i)),
        ),
    )(ocean_mixing, ocean_mixing[:, 0:1], state_by_level, forcing, sea_mask.reshape(1, cells))


def per_device(
    atmos_profiles,
    atmos_mixing,
    drag_factor,
    surface_before,
    downward_fluxes,
    land_weight,
    land_surface,
    ocean_state,
    ocean_mixing,
    sea_mask,
    exchange_slot,
    parent_column,
    ocean_weight,
    atmos_weight,
):
    comp_count = lax.axis_size("comp")
    sub_count = lax.axis_size("sub")
    devices = comp_count * sub_count
    columns = atmos_profiles.shape[2]
    intersections = exchange_slot.shape[0]
    ocean_cells = exchange_slot.shape[1]
    capacity = 2 * intersections * ocean_cells // devices
    width = min(128, capacity)
    tile_count = intersections * ocean_cells // width
    slot_tiles = devices * capacity // width
    windows = columns // width
    tile_place = exchange_slot.reshape(tile_count, width)[:, 0] // width
    placement = (tile_place[None, :] == jnp.arange(slot_tiles, dtype=jnp.int32)[:, None]).astype(
        jnp.float32
    )
    tiles_pc = parent_column.reshape(tile_count, width)
    window_of_tile = tiles_pc[:, 0] // width
    lanes = tiles_pc % width

    request = jnp.dot(placement, window_of_tile.astype(jnp.float32), precision=highest)
    request = (request + 0.5).astype(jnp.int32).reshape(devices, slot_tiles // devices)
    asked = lax.all_to_all(request, ("comp", "sub"), split_axis=0, concat_axis=0, tiled=True)
    asked = asked.reshape(slot_tiles)
    window_hot = (asked[:, None] == jnp.arange(windows, dtype=jnp.int32)[None, :]).astype(
        jnp.float32
    )

    fluxes = surface_fluxes(atmos_profiles, drag_factor, surface_before, downward_fluxes)
    column_forcing = forcing_rows(fluxes)
    served = jnp.einsum(
        "qw,fwl->fql", window_hot, column_forcing.reshape(4, windows, width), precision=highest
    )
    arrived = lax.all_to_all(
        served.reshape(4, devices, capacity),
        ("comp", "sub"),
        split_axis=1,
        concat_axis=1,
        tiled=True,
    )
    atmos_updated = diffuse_atmos(atmos_profiles, atmos_mixing, fluxes)
    win_local = jnp.einsum(
        "qt,fql->ftl", placement, arrived.reshape(4, slot_tiles, width), precision=highest
    )
    at_cells = lane_gather(win_local, lanes).reshape(4, intersections, ocean_cells)
    forcing = jnp.sum(ocean_weight[None] * at_cells, axis=1) / jnp.sum(ocean_weight, axis=0)[None]

    state_by_level = jnp.transpose(ocean_state, (1, 0, 2))
    updated_by_level, top = ocean_update(ocean_mixing, state_by_level, forcing, sea_mask)
    ocean_updated = jnp.transpose(updated_by_level, (1, 0, 2))

    sea_share = atmos_weight * sea_mask.astype(jnp.float32)[None, :]
    outgoing = jnp.concatenate([sea_share[None] * top[:, None, :], sea_share[None]], axis=0)
    lane_hot = (lanes[:, :, None] == jnp.arange(width, dtype=jnp.int32)[None, None, :]).astype(
        jnp.float32
    )
    partial = jnp.einsum(
        "ftl,tlc->ftc", outgoing.reshape(5, tile_count, width), lane_hot, precision=high
    )
    send_buffer = jnp.einsum("qt,ftc->fqc", placement, partial, precision=highest)
    returned = lax.all_to_all(
        send_buffer.reshape(5, devices, capacity),
        ("comp", "sub"),
        split_axis=1,
        concat_axis=1,
        tiled=True,
    )
    summed = jnp.einsum(
        "qw,fqc->fwc", window_hot, returned.reshape(5, slot_tiles, width), precision=highest
    ).reshape(5, columns)
    surface_state = (summed[:4] + land_weight[None] * land_surface) / (summed[4] + land_weight)[
        None
    ]
    return (atmos_updated, ocean_updated, surface_state)


def solution(mesh):
    return jax.shard_map(
        per_device,
        mesh=mesh,
        in_specs=(
            P(None, None, ("comp", "sub")),
            P(),
            P(("comp", "sub")),
            P(None, ("comp", "sub")),
            P(None, ("comp", "sub")),
            P(("comp", "sub")),
            P(None, ("comp", "sub")),
            P(None, None, ("comp", "sub")),
            P(),
            P(("comp", "sub")),
            P(None, ("comp", "sub")),
            P(None, ("comp", "sub")),
            P(None, ("comp", "sub")),
            P(None, ("comp", "sub")),
        ),
        out_specs=(
            P(None, None, ("comp", "sub")),
            P(None, None, ("comp", "sub")),
            P(None, ("comp", "sub")),
        ),
        check_vma=False,
    )
```

```python
import functools

import jax
import jax.numpy as jnp
from jax import lax
from jax.experimental import pallas as pl
from jax.experimental.pallas import tpu as pltpu
from jax.sharding import PartitionSpec as P

MESH = pl.DeviceIdType.MESH
couple_rate = 0.5
highest = lax.Precision.HIGHEST
high = lax.Precision.HIGH


def surface_fluxes(atmos_profiles, drag_factor, surface_before, downward_fluxes):
    bottom = atmos_profiles[:, -1, :].astype(jnp.float32)
    east_gap = bottom[2] - surface_before[2]
    north_gap = bottom[3] - surface_before[3]
    wind_speed = jnp.sqrt(1.0 + east_gap * east_gap + north_gap * north_gap)
    transfer = drag_factor * wind_speed
    sensible = transfer * (surface_before[0] - bottom[0])
    latent = transfer * (surface_before[1] - bottom[1])
    return jnp.stack(
        [
            sensible,
            latent,
            transfer * east_gap,
            transfer * north_gap,
            downward_fluxes[0],
            downward_fluxes[1],
            downward_fluxes[2],
            downward_fluxes[3],
        ]
    )


def diffuse_atmos(atmos_profiles, atmos_mixing, fluxes):
    lowest = atmos_mixing[:, -1].astype(jnp.float32)
    tendency = couple_rate * jnp.stack([fluxes[0], fluxes[1], -fluxes[2], -fluxes[3]])
    result = []
    for member in range(4):
        mixed_rows = jnp.dot(
            atmos_mixing, atmos_profiles[member], preferred_element_type=jnp.float32
        )
        result.append(mixed_rows + lowest[:, None] * tendency[member][None, :])
    return jnp.stack(result).astype(jnp.bfloat16)


def forcing_rows(fluxes):
    return couple_rate * jnp.stack(
        [
            fluxes[4] + fluxes[5] - fluxes[0] - fluxes[1],
            fluxes[1] - fluxes[6] - fluxes[7],
            fluxes[2],
            fluxes[3],
        ]
    )


def lane_gather_kernel(win_ref, lanes_ref, out_ref):
    lanes = lanes_ref[...]
    for field in range(win_ref.shape[0]):
        out_ref[field] = jnp.take_along_axis(
            win_ref[field], lanes, axis=1, mode="promise_in_bounds"
        )


def lane_gather(win, lanes):
    return pl.pallas_call(
        lane_gather_kernel,
        out_shape=jax.ShapeDtypeStruct(win.shape, win.dtype),
        in_specs=[pl.BlockSpec(memory_space=pltpu.VMEM)] * 2,
        out_specs=pl.BlockSpec(memory_space=pltpu.VMEM),
    )(win, lanes)


def ocean_kernel(m_ref, m0_ref, x_ref, forcing_ref, sea_ref, out_ref, top_ref):
    m = m_ref[...]
    m0 = m0_ref[...]
    sea = sea_ref[...] == 1
    for field in range(x_ref.shape[1]):
        x = x_ref[:, field, :]
        mixed = jnp.dot(m, x, precision=highest, preferred_element_type=jnp.float32)
        mixed = mixed + m0 * forcing_ref[field : field + 1, :]
        updated = jnp.where(sea, mixed, x)
        out_ref[:, field, :] = updated
        top_ref[field : field + 1, :] = updated[0:1, :]


def ocean_update(ocean_mixing, state_by_level, forcing, sea_mask, block=1024):
    levels, fields, cells = state_by_level.shape
    return pl.pallas_call(
        ocean_kernel,
        grid=(cells // block,),
        out_shape=(
            jax.ShapeDtypeStruct(state_by_level.shape, jnp.float32),
            jax.ShapeDtypeStruct((fields, cells), jnp.float32),
        ),
        in_specs=[
            pl.BlockSpec((levels, levels), lambda i: (0, 0)),
            pl.BlockSpec((levels, 1), lambda i: (0, 0)),
            pl.BlockSpec((levels, fields, block), lambda i: (0, 0, i)),
            pl.BlockSpec((fields, block), lambda i: (0, i)),
            pl.BlockSpec((1, block), lambda i: (0, i)),
        ],
        out_specs=(
            pl.BlockSpec((levels, fields, block), lambda i: (0, 0, i)),
            pl.BlockSpec((fields, block), lambda i: (0, i)),
        ),
    )(ocean_mixing, ocean_mixing[:, 0:1], state_by_level, forcing, sea_mask.reshape(1, cells))


def exchange_kernel(n_sub, x_ref, out_ref, send_sem, recv_sem):
    n = x_ref.shape[0]
    me = lax.axis_index("comp") * n_sub + lax.axis_index("sub")

    def device_of(peer):
        return (peer // n_sub, peer % n_sub)

    barrier = pltpu.get_barrier_semaphore()

    def greet(step, carry):
        peer = lax.rem(me + step, n)
        pl.semaphore_signal(barrier, 1, device_id=device_of(peer), device_id_type=MESH)
        return carry

    lax.fori_loop(1, n, greet, 0)
    pl.semaphore_wait(barrier, n - 1)

    def send(step, carry):
        peer = lax.rem(me + step, n)
        pltpu.make_async_remote_copy(
            src_ref=x_ref.at[peer],
            dst_ref=out_ref.at[me],
            send_sem=send_sem,
            recv_sem=recv_sem,
            device_id=device_of(peer),
            device_id_type=MESH,
        ).start()
        return carry

    lax.fori_loop(1, n, send, 0)
    out_ref[me] = x_ref[me]
    everyone = pltpu.make_async_remote_copy(
        src_ref=x_ref.at[pl.ds(0, n - 1)],
        dst_ref=out_ref.at[pl.ds(0, n - 1)],
        send_sem=send_sem,
        recv_sem=recv_sem,
        device_id=device_of(lax.rem(me + 1, n)),
        device_id_type=MESH,
    )
    everyone.wait_send()
    everyone.wait_recv()


def exchange(x, n_sub, collective_id):
    return pl.pallas_call(
        functools.partial(exchange_kernel, n_sub),
        out_shape=jax.ShapeDtypeStruct(x.shape, x.dtype),
        in_specs=[pl.BlockSpec(memory_space=pltpu.VMEM)],
        out_specs=pl.BlockSpec(memory_space=pltpu.VMEM),
        scratch_shapes=[pltpu.SemaphoreType.DMA, pltpu.SemaphoreType.DMA],
        compiler_params=pltpu.CompilerParams(
            collective_id=collective_id, has_side_effects=True
        ),
    )(x)


def per_device(
    atmos_profiles,
    atmos_mixing,
    drag_factor,
    surface_before,
    downward_fluxes,
    land_weight,
    land_surface,
    ocean_state,
    ocean_mixing,
    sea_mask,
    exchange_slot,
    parent_column,
    ocean_weight,
    atmos_weight,
):
    comp_count = lax.axis_size("comp")
    sub_count = lax.axis_size("sub")
    devices = comp_count * sub_count
    columns = atmos_profiles.shape[2]
    intersections = exchange_slot.shape[0]
    ocean_cells = exchange_slot.shape[1]
    capacity = 2 * intersections * ocean_cells // devices
    width = min(128, capacity)
    tile_count = intersections * ocean_cells // width
    slot_tiles = devices * capacity // width
    windows = columns // width
    tile_place = exchange_slot.reshape(tile_count, width)[:, 0] // width
    placement = (tile_place[None, :] == jnp.arange(slot_tiles, dtype=jnp.int32)[:, None]).astype(
        jnp.float32
    )
    tiles_pc = parent_column.reshape(tile_count, width)
    window_of_tile = tiles_pc[:, 0] // width
    lanes = tiles_pc % width

    request = jnp.dot(placement, window_of_tile.astype(jnp.float32), precision=highest)
    request = (request + 0.5).astype(jnp.int32).reshape(devices, 1, slot_tiles // devices)
    request = jnp.pad(request, ((0, 0), (0, 0), (0, width - slot_tiles // devices)))
    asked = exchange(request, sub_count, 0)[:, 0, : slot_tiles // devices]
    asked = asked.reshape(slot_tiles)
    window_hot = (asked[:, None] == jnp.arange(windows, dtype=jnp.int32)[None, :]).astype(
        jnp.float32
    )

    fluxes = surface_fluxes(atmos_profiles, drag_factor, surface_before, downward_fluxes)
    column_forcing = forcing_rows(fluxes)
    served = jnp.einsum(
        "qw,fwl->qfl", window_hot, column_forcing.reshape(4, windows, width), precision=highest
    )
    arrived = exchange(served.reshape(devices, -1, width), sub_count, 1)
    atmos_updated = diffuse_atmos(atmos_profiles, atmos_mixing, fluxes)
    win_local = jnp.einsum(
        "qt,qfl->ftl", placement, arrived.reshape(slot_tiles, 4, width), precision=highest
    )
    at_cells = lane_gather(win_local, lanes).reshape(4, intersections, ocean_cells)
    forcing = jnp.sum(ocean_weight[None] * at_cells, axis=1) / jnp.sum(ocean_weight, axis=0)[None]

    state_by_level = jnp.transpose(ocean_state, (1, 0, 2))
    updated_by_level, top = ocean_update(ocean_mixing, state_by_level, forcing, sea_mask)
    ocean_updated = jnp.transpose(updated_by_level, (1, 0, 2))

    sea_share = atmos_weight * sea_mask.astype(jnp.float32)[None, :]
    outgoing = jnp.concatenate([sea_share[None] * top[:, None, :], sea_share[None]], axis=0)
    lane_hot = (lanes[:, :, None] == jnp.arange(width, dtype=jnp.int32)[None, None, :]).astype(
        jnp.float32
    )
    partial = jnp.einsum(
        "ftl,tlc->ftc", outgoing.reshape(5, tile_count, width), lane_hot, precision=high
    )
    send_buffer = jnp.einsum("qt,ftc->qfc", placement, partial, precision=highest)
    returned = exchange(send_buffer.reshape(devices, -1, width), sub_count, 2)
    summed = jnp.einsum(
        "qw,qfc->fwc", window_hot, returned.reshape(slot_tiles, 5, width), precision=highest
    ).reshape(5, columns)
    surface_state = (summed[:4] + land_weight[None] * land_surface) / (summed[4] + land_weight)[
        None
    ]
    return (atmos_updated, ocean_updated, surface_state)


def solution(mesh):
    return jax.shard_map(
        per_device,
        mesh=mesh,
        in_specs=(
            P(None, None, ("comp", "sub")),
            P(),
            P(("comp", "sub")),
            P(None, ("comp", "sub")),
            P(None, ("comp", "sub")),
            P(("comp", "sub")),
            P(None, ("comp", "sub")),
            P(None, None, ("comp", "sub")),
            P(),
            P(("comp", "sub")),
            P(None, ("comp", "sub")),
            P(None, ("comp", "sub")),
            P(None, ("comp", "sub")),
            P(None, ("comp", "sub")),
        ),
        out_specs=(
            P(None, None, ("comp", "sub")),
            P(None, None, ("comp", "sub")),
            P(None, ("comp", "sub")),
        ),
        check_vma=False,
    )
```

```python
import jax
import jax.numpy as jnp
from jax import lax
from jax.experimental import pallas as pl
from jax.experimental.pallas import tpu as pltpu
from jax.sharding import PartitionSpec as P

couple_rate = 0.5
highest = lax.Precision.HIGHEST
high = lax.Precision.HIGH


def surface_fluxes(atmos_profiles, drag_factor, surface_before, downward_fluxes):
    bottom = atmos_profiles[:, -1, :].astype(jnp.float32)
    east_gap = bottom[2] - surface_before[2]
    north_gap = bottom[3] - surface_before[3]
    wind_speed = jnp.sqrt(1.0 + east_gap * east_gap + north_gap * north_gap)
    transfer = drag_factor * wind_speed
    sensible = transfer * (surface_before[0] - bottom[0])
    latent = transfer * (surface_before[1] - bottom[1])
    return jnp.stack(
        [
            sensible,
            latent,
            transfer * east_gap,
            transfer * north_gap,
            downward_fluxes[0],
            downward_fluxes[1],
            downward_fluxes[2],
            downward_fluxes[3],
        ]
    )


def diffuse_atmos(atmos_profiles, atmos_mixing, fluxes):
    lowest = atmos_mixing[:, -1].astype(jnp.float32)
    tendency = couple_rate * jnp.stack([fluxes[0], fluxes[1], -fluxes[2], -fluxes[3]])
    result = []
    for member in range(4):
        mixed_rows = jnp.dot(
            atmos_mixing, atmos_profiles[member], preferred_element_type=jnp.float32
        )
        result.append(mixed_rows + lowest[:, None] * tendency[member][None, :])
    return jnp.stack(result).astype(jnp.bfloat16)


def forcing_rows(fluxes):
    return couple_rate * jnp.stack(
        [
            fluxes[4] + fluxes[5] - fluxes[0] - fluxes[1],
            fluxes[1] - fluxes[6] - fluxes[7],
            fluxes[2],
            fluxes[3],
        ]
    )


def lane_gather_kernel(win_ref, lanes_ref, out_ref):
    lanes = lanes_ref[...]
    for field in range(win_ref.shape[0]):
        out_ref[field] = jnp.take_along_axis(
            win_ref[field], lanes, axis=1, mode="promise_in_bounds"
        )


def lane_gather(win, lanes):
    return pl.pallas_call(
        lane_gather_kernel,
        out_shape=jax.ShapeDtypeStruct(win.shape, win.dtype),
        in_specs=[pl.BlockSpec(memory_space=pltpu.VMEM)] * 2,
        out_specs=pl.BlockSpec(memory_space=pltpu.VMEM),
    )(win, lanes)


def split_bf16(values):
    upper = values.astype(jnp.bfloat16)
    return upper, (values - upper.astype(jnp.float32)).astype(jnp.bfloat16)


def split_kept(values):
    upper = lax.reduce_precision(values, exponent_bits=8, mantissa_bits=7)
    return upper.astype(jnp.bfloat16), (values - upper).astype(jnp.bfloat16)


def ocean_kernel(m_hi_ref, m_lo_ref, m0_ref, x_ref, forcing_ref, sea_ref, out_ref, top_ref):
    m_hi = m_hi_ref[...]
    m_lo = m_lo_ref[...]
    m0 = m0_ref[...]
    sea = sea_ref[...] == 1
    for field in range(x_ref.shape[1]):
        x = x_ref[:, field, :]
        x_hi, x_lo = split_bf16(x)
        mixed = jnp.dot(m_hi, x_hi, preferred_element_type=jnp.float32)
        mixed = mixed + jnp.dot(m_hi, x_lo, preferred_element_type=jnp.float32)
        mixed = mixed + jnp.dot(m_lo, x_hi, preferred_element_type=jnp.float32)
        mixed = mixed + m0 * forcing_ref[field : field + 1, :]
        updated = jnp.where(sea, mixed, x)
        out_ref[:, field, :] = updated
        top_ref[field : field + 1, :] = updated[0:1, :]


def ocean_update(ocean_mixing, state_by_level, forcing, sea_mask, block=1024):
    levels, fields, cells = state_by_level.shape
    return pl.pallas_call(
        ocean_kernel,
        grid=(cells // block,),
        out_shape=(
            jax.ShapeDtypeStruct(state_by_level.shape, jnp.float32),
            jax.ShapeDtypeStruct((fields, cells), jnp.float32),
        ),
        in_specs=[
            pl.BlockSpec((levels, levels), lambda i: (0, 0)),
            pl.BlockSpec((levels, levels), lambda i: (0, 0)),
            pl.BlockSpec((levels, 1), lambda i: (0, 0)),
            pl.BlockSpec((levels, fields, block), lambda i: (0, 0, i)),
            pl.BlockSpec((fields, block), lambda i: (0, i)),
            pl.BlockSpec((1, block), lambda i: (0, i)),
        ],
        out_specs=(
            pl.BlockSpec((levels, fields, block), lambda i: (0, 0, i)),
            pl.BlockSpec((fields, block), lambda i: (0, i)),
        ),
    )(*split_kept(ocean_mixing), ocean_mixing[:, 0:1], state_by_level, forcing, sea_mask.reshape(1, cells))


def per_device(
    atmos_profiles,
    atmos_mixing,
    drag_factor,
    surface_before,
    downward_fluxes,
    land_weight,
    land_surface,
    ocean_state,
    ocean_mixing,
    sea_mask,
    exchange_slot,
    parent_column,
    ocean_weight,
    atmos_weight,
):
    comp_count = lax.axis_size("comp")
    sub_count = lax.axis_size("sub")
    devices = comp_count * sub_count
    columns = atmos_profiles.shape[2]
    intersections = exchange_slot.shape[0]
    ocean_cells = exchange_slot.shape[1]
    capacity = 2 * intersections * ocean_cells // devices
    width = min(128, capacity)
    tile_count = intersections * ocean_cells // width
    slot_tiles = devices * capacity // width
    windows = columns // width
    tile_place = exchange_slot.reshape(tile_count, width)[:, 0] // width
    placement = (tile_place[None, :] == jnp.arange(slot_tiles, dtype=jnp.int32)[:, None]).astype(
        jnp.float32
    )
    tiles_pc = parent_column.reshape(tile_count, width)
    window_of_tile = tiles_pc[:, 0] // width
    lanes = tiles_pc % width

    request = jnp.dot(placement, window_of_tile.astype(jnp.float32), precision=highest)
    request = (request + 0.5).astype(jnp.int32).reshape(devices, slot_tiles // devices)
    asked = lax.all_to_all(request, ("comp", "sub"), split_axis=0, concat_axis=0, tiled=True)
    asked = asked.reshape(slot_tiles)
    window_hot = (asked[:, None] == jnp.arange(windows, dtype=jnp.int32)[None, :]).astype(
        jnp.float32
    )

    fluxes = surface_fluxes(atmos_profiles, drag_factor, surface_before, downward_fluxes)
    column_forcing = forcing_rows(fluxes)
    served = jnp.einsum(
        "qw,fwl->fql", window_hot, column_forcing.reshape(4, windows, width), precision=highest
    )
    arrived = lax.all_to_all(
        served.reshape(4, devices, capacity),
        ("comp", "sub"),
        split_axis=1,
        concat_axis=1,
        tiled=True,
    )
    atmos_updated = diffuse_atmos(atmos_profiles, atmos_mixing, fluxes)
    win_local = jnp.einsum(
        "qt,fql->ftl", placement, arrived.reshape(4, slot_tiles, width), precision=highest
    )
    at_cells = lane_gather(win_local, lanes).reshape(4, intersections, ocean_cells)
    forcing = jnp.sum(ocean_weight[None] * at_cells, axis=1) / jnp.sum(ocean_weight, axis=0)[None]

    state_by_level = jnp.transpose(ocean_state, (1, 0, 2))
    updated_by_level, top = ocean_update(ocean_mixing, state_by_level, forcing, sea_mask)
    ocean_updated = jnp.transpose(updated_by_level, (1, 0, 2))

    sea_share = atmos_weight * sea_mask.astype(jnp.float32)[None, :]
    outgoing = jnp.concatenate([sea_share[None] * top[:, None, :], sea_share[None]], axis=0)
    lane_hot = (lanes[:, :, None] == jnp.arange(width, dtype=jnp.int32)[None, None, :]).astype(
        jnp.bfloat16
    )
    pieces = jnp.concatenate(split_kept(outgoing.reshape(5, tile_count, width)), axis=0)
    partial = jnp.einsum("ftl,tlc->ftc", pieces, lane_hot, preferred_element_type=jnp.float32)
    partial = partial[:5] + partial[5:]
    send_buffer = jnp.einsum("qt,ftc->fqc", placement, partial, precision=highest)
    returned = lax.all_to_all(
        send_buffer.reshape(5, devices, capacity),
        ("comp", "sub"),
        split_axis=1,
        concat_axis=1,
        tiled=True,
    )
    summed = jnp.einsum(
        "qw,fqc->fwc", window_hot, returned.reshape(5, slot_tiles, width), precision=highest
    ).reshape(5, columns)
    surface_state = (summed[:4] + land_weight[None] * land_surface) / (summed[4] + land_weight)[
        None
    ]
    return (atmos_updated, ocean_updated, surface_state)


def solution(mesh):
    return jax.shard_map(
        per_device,
        mesh=mesh,
        in_specs=(
            P(None, None, ("comp", "sub")),
            P(),
            P(("comp", "sub")),
            P(None, ("comp", "sub")),
            P(None, ("comp", "sub")),
            P(("comp", "sub")),
            P(None, ("comp", "sub")),
            P(None, None, ("comp", "sub")),
            P(),
            P(("comp", "sub")),
            P(None, ("comp", "sub")),
            P(None, ("comp", "sub")),
            P(None, ("comp", "sub")),
            P(None, ("comp", "sub")),
        ),
        out_specs=(
            P(None, None, ("comp", "sub")),
            P(None, None, ("comp", "sub")),
            P(None, ("comp", "sub")),
        ),
        check_vma=False,
    )
```

```python
import jax
import jax.numpy as jnp
from jax import lax
from jax.experimental import pallas as pl
from jax.experimental.pallas import tpu as pltpu
from jax.sharding import PartitionSpec as P

couple_rate = 0.5
highest = lax.Precision.HIGHEST
high = lax.Precision.HIGH


def surface_fluxes(atmos_profiles, drag_factor, surface_before, downward_fluxes):
    bottom = atmos_profiles[:, -1, :].astype(jnp.float32)
    east_gap = bottom[2] - surface_before[2]
    north_gap = bottom[3] - surface_before[3]
    wind_speed = jnp.sqrt(1.0 + east_gap * east_gap + north_gap * north_gap)
    transfer = drag_factor * wind_speed
    sensible = transfer * (surface_before[0] - bottom[0])
    latent = transfer * (surface_before[1] - bottom[1])
    return jnp.stack(
        [
            sensible,
            latent,
            transfer * east_gap,
            transfer * north_gap,
            downward_fluxes[0],
            downward_fluxes[1],
            downward_fluxes[2],
            downward_fluxes[3],
        ]
    )


def diffuse_atmos(atmos_profiles, atmos_mixing, fluxes):
    lowest = atmos_mixing[:, -1].astype(jnp.float32)
    tendency = couple_rate * jnp.stack([fluxes[0], fluxes[1], -fluxes[2], -fluxes[3]])
    result = []
    for member in range(4):
        mixed_rows = jnp.dot(
            atmos_mixing, atmos_profiles[member], preferred_element_type=jnp.float32
        )
        result.append(mixed_rows + lowest[:, None] * tendency[member][None, :])
    return jnp.stack(result).astype(jnp.bfloat16)


def forcing_rows(fluxes):
    return couple_rate * jnp.stack(
        [
            fluxes[4] + fluxes[5] - fluxes[0] - fluxes[1],
            fluxes[1] - fluxes[6] - fluxes[7],
            fluxes[2],
            fluxes[3],
        ]
    )


def lane_gather_kernel(win_ref, lanes_ref, out_ref):
    lanes = lanes_ref[...]
    for field in range(win_ref.shape[0]):
        out_ref[field] = jnp.take_along_axis(
            win_ref[field], lanes, axis=1, mode="promise_in_bounds"
        )


def lane_gather(win, lanes):
    return pl.pallas_call(
        lane_gather_kernel,
        out_shape=jax.ShapeDtypeStruct(win.shape, win.dtype),
        in_specs=[pl.BlockSpec(memory_space=pltpu.VMEM)] * 2,
        out_specs=pl.BlockSpec(memory_space=pltpu.VMEM),
    )(win, lanes)


def split_kept(values):
    upper = lax.reduce_precision(values, exponent_bits=8, mantissa_bits=7)
    return upper.astype(jnp.bfloat16), (values - upper).astype(jnp.bfloat16)


def ocean_kernel(m_ref, m0_ref, x_ref, forcing_ref, sea_ref, out_ref):
    m = m_ref[...]
    m0 = m0_ref[...]
    sea = sea_ref[...] == 1
    for field in range(x_ref.shape[1]):
        x = x_ref[:, field, :]
        mixed = jnp.dot(m, x, precision=highest, preferred_element_type=jnp.float32)
        mixed = mixed + m0 * forcing_ref[field : field + 1, :]
        out_ref[:, field, :] = jnp.where(sea, mixed, x)


def ocean_update(ocean_mixing, state_by_level, forcing, sea_mask, block=1024):
    levels, fields, cells = state_by_level.shape
    return pl.pallas_call(
        ocean_kernel,
        grid=(cells // block,),
        out_shape=jax.ShapeDtypeStruct(state_by_level.shape, jnp.float32),
        in_specs=[
            pl.BlockSpec((levels, levels), lambda i: (0, 0)),
            pl.BlockSpec((levels, 1), lambda i: (0, 0)),
            pl.BlockSpec((levels, fields, block), lambda i: (0, 0, i)),
            pl.BlockSpec((fields, block), lambda i: (0, i)),
            pl.BlockSpec((1, block), lambda i: (0, i)),
        ],
        out_specs=pl.BlockSpec((levels, fields, block), lambda i: (0, 0, i)),
        cost_estimate=pl.CostEstimate(
            flops=12 * levels * levels * fields * cells,
            bytes_accessed=8 * levels * fields * cells,
            transcendentals=0,
        ),
    )(ocean_mixing, ocean_mixing[:, 0:1], state_by_level, forcing, sea_mask.reshape(1, cells))


def per_device(
    atmos_profiles,
    atmos_mixing,
    drag_factor,
    surface_before,
    downward_fluxes,
    land_weight,
    land_surface,
    ocean_state,
    ocean_mixing,
    sea_mask,
    exchange_slot,
    parent_column,
    ocean_weight,
    atmos_weight,
):
    comp_count = lax.axis_size("comp")
    sub_count = lax.axis_size("sub")
    devices = comp_count * sub_count
    columns = atmos_profiles.shape[2]
    intersections = exchange_slot.shape[0]
    ocean_cells = exchange_slot.shape[1]
    capacity = 2 * intersections * ocean_cells // devices
    width = min(128, capacity)
    tile_count = intersections * ocean_cells // width
    slot_tiles = devices * capacity // width
    windows = columns // width
    tile_place = exchange_slot.reshape(tile_count, width)[:, 0] // width
    placement = (tile_place[None, :] == jnp.arange(slot_tiles, dtype=jnp.int32)[:, None]).astype(
        jnp.float32
    )
    tiles_pc = parent_column.reshape(tile_count, width)
    window_of_tile = tiles_pc[:, 0] // width
    lanes = tiles_pc % width

    state_by_level = jnp.transpose(ocean_state, (1, 0, 2))
    base_top = jnp.einsum("m,mfc->fc", ocean_mixing[0], state_by_level, precision=highest)

    request = jnp.dot(placement, window_of_tile.astype(jnp.float32), precision=highest)
    request = (request + 0.5).astype(jnp.int32).reshape(devices, slot_tiles // devices)
    asked = lax.all_to_all(request, ("comp", "sub"), split_axis=0, concat_axis=0, tiled=True)
    asked = asked.reshape(slot_tiles)
    window_hot = (asked[:, None] == jnp.arange(windows, dtype=jnp.int32)[None, :]).astype(
        jnp.float32
    )

    fluxes = surface_fluxes(atmos_profiles, drag_factor, surface_before, downward_fluxes)
    column_forcing = forcing_rows(fluxes)
    served = jnp.einsum(
        "qw,fwl->fql", window_hot, column_forcing.reshape(4, windows, width), precision=highest
    )
    arrived = lax.all_to_all(
        served.reshape(4, devices, capacity),
        ("comp", "sub"),
        split_axis=1,
        concat_axis=1,
        tiled=True,
    )
    atmos_updated = diffuse_atmos(atmos_profiles, atmos_mixing, fluxes)
    win_local = jnp.einsum(
        "qt,fql->ftl", placement, arrived.reshape(4, slot_tiles, width), precision=highest
    )
    at_cells = lane_gather(win_local, lanes).reshape(4, intersections, ocean_cells)
    forcing = jnp.sum(ocean_weight[None] * at_cells, axis=1) / jnp.sum(ocean_weight, axis=0)[None]

    sea = sea_mask[None, :] == 1
    top = jnp.where(sea, base_top + ocean_mixing[0, 0] * forcing, state_by_level[0])
    sea_share = atmos_weight * sea_mask.astype(jnp.float32)[None, :]
    outgoing = jnp.concatenate([sea_share[None] * top[:, None, :], sea_share[None]], axis=0)
    lane_hot = (lanes[:, :, None] == jnp.arange(width, dtype=jnp.int32)[None, None, :]).astype(
        jnp.bfloat16
    )
    pieces = jnp.concatenate(split_kept(outgoing.reshape(5, tile_count, width)), axis=0)
    partial = jnp.einsum("ftl,tlc->ftc", pieces, lane_hot, preferred_element_type=jnp.float32)
    partial = partial[:5] + partial[5:]
    send_buffer = jnp.einsum("qt,ftc->fqc", placement, partial, precision=highest)
    returned = lax.all_to_all(
        send_buffer.reshape(5, devices, capacity),
        ("comp", "sub"),
        split_axis=1,
        concat_axis=1,
        tiled=True,
    )
    summed = jnp.einsum(
        "qw,fqc->fwc", window_hot, returned.reshape(5, slot_tiles, width), precision=highest
    ).reshape(5, columns)
    updated_by_level = ocean_update(ocean_mixing, state_by_level, forcing, sea_mask)
    ocean_updated = jnp.transpose(updated_by_level, (1, 0, 2))
    surface_state = (summed[:4] + land_weight[None] * land_surface) / (summed[4] + land_weight)[
        None
    ]
    return (atmos_updated, ocean_updated, surface_state)


def solution(mesh):
    return jax.shard_map(
        per_device,
        mesh=mesh,
        in_specs=(
            P(None, None, ("comp", "sub")),
            P(),
            P(("comp", "sub")),
            P(None, ("comp", "sub")),
            P(None, ("comp", "sub")),
            P(("comp", "sub")),
            P(None, ("comp", "sub")),
            P(None, None, ("comp", "sub")),
            P(),
            P(("comp", "sub")),
            P(None, ("comp", "sub")),
            P(None, ("comp", "sub")),
            P(None, ("comp", "sub")),
            P(None, ("comp", "sub")),
        ),
        out_specs=(
            P(None, None, ("comp", "sub")),
            P(None, None, ("comp", "sub")),
            P(None, ("comp", "sub")),
        ),
        check_vma=False,
    )
```

```python
import jax
import jax.numpy as jnp
from jax import lax
from jax.experimental import pallas as pl
from jax.experimental.pallas import tpu as pltpu
from jax.sharding import PartitionSpec as P

couple_rate = 0.5
highest = lax.Precision.HIGHEST
high = lax.Precision.HIGH


def surface_fluxes(atmos_profiles, drag_factor, surface_before, downward_fluxes):
    bottom = atmos_profiles[:, -1, :].astype(jnp.float32)
    east_gap = bottom[2] - surface_before[2]
    north_gap = bottom[3] - surface_before[3]
    wind_speed = jnp.sqrt(1.0 + east_gap * east_gap + north_gap * north_gap)
    transfer = drag_factor * wind_speed
    sensible = transfer * (surface_before[0] - bottom[0])
    latent = transfer * (surface_before[1] - bottom[1])
    return jnp.stack(
        [
            sensible,
            latent,
            transfer * east_gap,
            transfer * north_gap,
            downward_fluxes[0],
            downward_fluxes[1],
            downward_fluxes[2],
            downward_fluxes[3],
        ]
    )


def diffuse_atmos(atmos_profiles, atmos_mixing, fluxes):
    lowest = atmos_mixing[:, -1].astype(jnp.float32)
    tendency = couple_rate * jnp.stack([fluxes[0], fluxes[1], -fluxes[2], -fluxes[3]])
    result = []
    for member in range(4):
        mixed_rows = jnp.dot(
            atmos_mixing, atmos_profiles[member], preferred_element_type=jnp.float32
        )
        result.append(mixed_rows + lowest[:, None] * tendency[member][None, :])
    return jnp.stack(result).astype(jnp.bfloat16)


def forcing_rows(fluxes):
    return couple_rate * jnp.stack(
        [
            fluxes[4] + fluxes[5] - fluxes[0] - fluxes[1],
            fluxes[1] - fluxes[6] - fluxes[7],
            fluxes[2],
            fluxes[3],
        ]
    )


def lane_gather_kernel(win_ref, lanes_ref, out_ref):
    lanes = lanes_ref[...]
    for field in range(win_ref.shape[0]):
        out_ref[field] = jnp.take_along_axis(
            win_ref[field], lanes, axis=1, mode="promise_in_bounds"
        )


def lane_gather(win, lanes):
    return pl.pallas_call(
        lane_gather_kernel,
        out_shape=jax.ShapeDtypeStruct(win.shape, win.dtype),
        in_specs=[pl.BlockSpec(memory_space=pltpu.VMEM)] * 2,
        out_specs=pl.BlockSpec(memory_space=pltpu.VMEM),
    )(win, lanes)


def split_kept(values):
    upper = lax.reduce_precision(values, exponent_bits=8, mantissa_bits=7)
    return upper.astype(jnp.bfloat16), (values - upper).astype(jnp.bfloat16)


def ocean_kernel(m_ref, m0_ref, x_ref, forcing_ref, sea_ref, out_ref):
    m = m_ref[...]
    m0 = m0_ref[...]
    sea = sea_ref[...] == 1
    for field in range(x_ref.shape[1]):
        x = x_ref[:, field, :]
        mixed = jnp.dot(m, x, precision=highest, preferred_element_type=jnp.float32)
        mixed = mixed + m0 * forcing_ref[field : field + 1, :]
        out_ref[:, field, :] = jnp.where(sea, mixed, x)


def ocean_update(ocean_mixing, state_by_level, forcing, sea_mask, block=1024):
    levels, fields, cells = state_by_level.shape
    return pl.pallas_call(
        ocean_kernel,
        grid=(cells // block,),
        out_shape=jax.ShapeDtypeStruct(state_by_level.shape, jnp.float32),
        in_specs=[
            pl.BlockSpec((levels, levels), lambda i: (0, 0)),
            pl.BlockSpec((levels, 1), lambda i: (0, 0)),
            pl.BlockSpec((levels, fields, block), lambda i: (0, 0, i)),
            pl.BlockSpec((fields, block), lambda i: (0, i)),
            pl.BlockSpec((1, block), lambda i: (0, i)),
        ],
        out_specs=pl.BlockSpec((levels, fields, block), lambda i: (0, 0, i)),
        cost_estimate=pl.CostEstimate(
            flops=12 * levels * levels * fields * cells,
            bytes_accessed=8 * levels * fields * cells,
            transcendentals=0,
        ),
    )(ocean_mixing, ocean_mixing[:, 0:1], state_by_level, forcing, sea_mask.reshape(1, cells))


def top_level_kernel(row_ref, x_ref, out_ref):
    total = row_ref[0] * x_ref[0]
    for level in range(1, x_ref.shape[0]):
        total = total + row_ref[level] * x_ref[level]
    out_ref[...] = total


def top_level_mix(first_row, state_by_level, block=2048):
    levels, fields, cells = state_by_level.shape
    return pl.pallas_call(
        top_level_kernel,
        grid=(cells // block,),
        out_shape=jax.ShapeDtypeStruct((fields, cells), jnp.float32),
        in_specs=[
            pl.BlockSpec(memory_space=pltpu.SMEM),
            pl.BlockSpec((levels, fields, block), lambda i: (0, 0, i)),
        ],
        out_specs=pl.BlockSpec((fields, block), lambda i: (0, i)),
        cost_estimate=pl.CostEstimate(
            flops=2 * levels * fields * cells,
            bytes_accessed=4 * (levels + 1) * fields * cells,
            transcendentals=0,
        ),
    )(first_row, state_by_level)


def per_device(
    atmos_profiles,
    atmos_mixing,
    drag_factor,
    surface_before,
    downward_fluxes,
    land_weight,
    land_surface,
    ocean_state,
    ocean_mixing,
    sea_mask,
    exchange_slot,
    parent_column,
    ocean_weight,
    atmos_weight,
):
    comp_count = lax.axis_size("comp")
    sub_count = lax.axis_size("sub")
    devices = comp_count * sub_count
    columns = atmos_profiles.shape[2]
    intersections = exchange_slot.shape[0]
    ocean_cells = exchange_slot.shape[1]
    capacity = 2 * intersections * ocean_cells // devices
    width = min(128, capacity)
    tile_count = intersections * ocean_cells // width
    slot_tiles = devices * capacity // width
    windows = columns // width
    tile_place = exchange_slot.reshape(tile_count, width)[:, 0] // width
    placement = (tile_place[None, :] == jnp.arange(slot_tiles, dtype=jnp.int32)[:, None]).astype(
        jnp.float32
    )
    tiles_pc = parent_column.reshape(tile_count, width)
    window_of_tile = tiles_pc[:, 0] // width
    lanes = tiles_pc % width

    state_by_level = jnp.transpose(ocean_state, (1, 0, 2))
    base_top = top_level_mix(ocean_mixing[0], state_by_level)

    request = jnp.dot(placement, window_of_tile.astype(jnp.float32), precision=highest)
    request = (request + 0.5).astype(jnp.int32).reshape(devices, slot_tiles // devices)
    asked = lax.all_to_all(request, ("comp", "sub"), split_axis=0, concat_axis=0, tiled=True)
    asked = asked.reshape(slot_tiles)
    window_hot = (asked[:, None] == jnp.arange(windows, dtype=jnp.int32)[None, :]).astype(
        jnp.float32
    )

    fluxes = surface_fluxes(atmos_profiles, drag_factor, surface_before, downward_fluxes)
    column_forcing = forcing_rows(fluxes)
    served = jnp.einsum(
        "qw,fwl->fql", window_hot, column_forcing.reshape(4, windows, width), precision=highest
    )
    arrived = lax.all_to_all(
        served.reshape(4, devices, capacity),
        ("comp", "sub"),
        split_axis=1,
        concat_axis=1,
        tiled=True,
    )
    atmos_updated = diffuse_atmos(atmos_profiles, atmos_mixing, fluxes)
    win_local = jnp.einsum(
        "qt,fql->ftl", placement, arrived.reshape(4, slot_tiles, width), precision=highest
    )
    at_cells = lane_gather(win_local, lanes).reshape(4, intersections, ocean_cells)
    forcing = jnp.sum(ocean_weight[None] * at_cells, axis=1) / jnp.sum(ocean_weight, axis=0)[None]

    sea = sea_mask[None, :] == 1
    top = jnp.where(sea, base_top + ocean_mixing[0, 0] * forcing, state_by_level[0])
    sea_share = atmos_weight * sea_mask.astype(jnp.float32)[None, :]
    outgoing = jnp.concatenate([sea_share[None] * top[:, None, :], sea_share[None]], axis=0)
    lane_hot = (lanes[:, :, None] == jnp.arange(width, dtype=jnp.int32)[None, None, :]).astype(
        jnp.bfloat16
    )
    pieces = jnp.concatenate(split_kept(outgoing.reshape(5, tile_count, width)), axis=0)
    partial = jnp.einsum("ftl,tlc->ftc", pieces, lane_hot, preferred_element_type=jnp.float32)
    partial = partial[:5] + partial[5:]
    send_buffer = jnp.einsum("qt,ftc->fqc", placement, partial, precision=highest)
    returned = lax.all_to_all(
        send_buffer.reshape(5, devices, capacity),
        ("comp", "sub"),
        split_axis=1,
        concat_axis=1,
        tiled=True,
    )
    summed = jnp.einsum(
        "qw,fqc->fwc", window_hot, returned.reshape(5, slot_tiles, width), precision=highest
    ).reshape(5, columns)
    updated_by_level = ocean_update(ocean_mixing, state_by_level, forcing, sea_mask)
    ocean_updated = jnp.transpose(updated_by_level, (1, 0, 2))
    surface_state = (summed[:4] + land_weight[None] * land_surface) / (summed[4] + land_weight)[
        None
    ]
    return (atmos_updated, ocean_updated, surface_state)


def solution(mesh):
    return jax.shard_map(
        per_device,
        mesh=mesh,
        in_specs=(
            P(None, None, ("comp", "sub")),
            P(),
            P(("comp", "sub")),
            P(None, ("comp", "sub")),
            P(None, ("comp", "sub")),
            P(("comp", "sub")),
            P(None, ("comp", "sub")),
            P(None, None, ("comp", "sub")),
            P(),
            P(("comp", "sub")),
            P(None, ("comp", "sub")),
            P(None, ("comp", "sub")),
            P(None, ("comp", "sub")),
            P(None, ("comp", "sub")),
        ),
        out_specs=(
            P(None, None, ("comp", "sub")),
            P(None, None, ("comp", "sub")),
            P(None, ("comp", "sub")),
        ),
        check_vma=False,
    )
```

```python
import jax
import jax.numpy as jnp
from jax import lax
from jax.experimental import pallas as pl
from jax.experimental.pallas import tpu as pltpu
from jax.sharding import PartitionSpec as P

couple_rate = 0.5
highest = lax.Precision.HIGHEST
high = lax.Precision.HIGH


def surface_fluxes(atmos_profiles, drag_factor, surface_before, downward_fluxes):
    bottom = atmos_profiles[:, -1, :].astype(jnp.float32)
    east_gap = bottom[2] - surface_before[2]
    north_gap = bottom[3] - surface_before[3]
    wind_speed = jnp.sqrt(1.0 + east_gap * east_gap + north_gap * north_gap)
    transfer = drag_factor * wind_speed
    sensible = transfer * (surface_before[0] - bottom[0])
    latent = transfer * (surface_before[1] - bottom[1])
    return jnp.stack(
        [
            sensible,
            latent,
            transfer * east_gap,
            transfer * north_gap,
            downward_fluxes[0],
            downward_fluxes[1],
            downward_fluxes[2],
            downward_fluxes[3],
        ]
    )


def diffuse_atmos(atmos_profiles, atmos_mixing, fluxes):
    lowest = atmos_mixing[:, -1].astype(jnp.float32)
    tendency = couple_rate * jnp.stack([fluxes[0], fluxes[1], -fluxes[2], -fluxes[3]])
    result = []
    for member in range(4):
        mixed_rows = jnp.dot(
            atmos_mixing, atmos_profiles[member], preferred_element_type=jnp.float32
        )
        result.append(mixed_rows + lowest[:, None] * tendency[member][None, :])
    return jnp.stack(result).astype(jnp.bfloat16)


def forcing_rows(fluxes):
    return couple_rate * jnp.stack(
        [
            fluxes[4] + fluxes[5] - fluxes[0] - fluxes[1],
            fluxes[1] - fluxes[6] - fluxes[7],
            fluxes[2],
            fluxes[3],
        ]
    )


def lane_gather_kernel(win_ref, lanes_ref, out_ref):
    lanes = lanes_ref[...]
    for field in range(win_ref.shape[0]):
        out_ref[field] = jnp.take_along_axis(
            win_ref[field], lanes, axis=1, mode="promise_in_bounds"
        )


def lane_gather(win, lanes):
    return pl.pallas_call(
        lane_gather_kernel,
        out_shape=jax.ShapeDtypeStruct(win.shape, win.dtype),
        in_specs=[pl.BlockSpec(memory_space=pltpu.VMEM)] * 2,
        out_specs=pl.BlockSpec(memory_space=pltpu.VMEM),
    )(win, lanes)


def split_kept(values):
    upper = lax.reduce_precision(values, exponent_bits=8, mantissa_bits=7)
    return upper.astype(jnp.bfloat16), (values - upper).astype(jnp.bfloat16)


def ocean_kernel(m_ref, m0_ref, x_ref, forcing_ref, sea_ref, out_ref):
    m = m_ref[...]
    m0 = m0_ref[...]
    sea = sea_ref[...] == 1
    for field in range(x_ref.shape[1]):
        x = x_ref[:, field, :]
        mixed = jnp.dot(m, x, precision=highest, preferred_element_type=jnp.float32)
        mixed = mixed + m0 * forcing_ref[field : field + 1, :]
        out_ref[:, field, :] = jnp.where(sea, mixed, x)


def ocean_update(ocean_mixing, state_by_level, forcing, sea_mask, block=1024):
    levels, fields, cells = state_by_level.shape
    return pl.pallas_call(
        ocean_kernel,
        grid=(cells // block,),
        out_shape=jax.ShapeDtypeStruct(state_by_level.shape, jnp.float32),
        in_specs=[
            pl.BlockSpec((levels, levels), lambda i: (0, 0)),
            pl.BlockSpec((levels, 1), lambda i: (0, 0)),
            pl.BlockSpec((levels, fields, block), lambda i: (0, 0, i)),
            pl.BlockSpec((fields, block), lambda i: (0, i)),
            pl.BlockSpec((1, block), lambda i: (0, i)),
        ],
        out_specs=pl.BlockSpec((levels, fields, block), lambda i: (0, 0, i)),
        cost_estimate=pl.CostEstimate(
            flops=12 * levels * levels * fields * cells,
            bytes_accessed=8 * levels * fields * cells,
            transcendentals=0,
        ),
    )(ocean_mixing, ocean_mixing[:, 0:1], state_by_level, forcing, sea_mask.reshape(1, cells))


def top_level_kernel(row_ref, x_ref, out_ref):
    total = row_ref[0] * x_ref[0]
    for level in range(1, x_ref.shape[0]):
        total = total + row_ref[level] * x_ref[level]
    out_ref[...] = total


def top_level_mix(first_row, state_by_level, block=2048):
    levels, fields, cells = state_by_level.shape
    return pl.pallas_call(
        top_level_kernel,
        grid=(cells // block,),
        out_shape=jax.ShapeDtypeStruct((fields, cells), jnp.float32),
        in_specs=[
            pl.BlockSpec(memory_space=pltpu.SMEM),
            pl.BlockSpec((levels, fields, block), lambda i: (0, 0, i)),
        ],
        out_specs=pl.BlockSpec((fields, block), lambda i: (0, i)),
        cost_estimate=pl.CostEstimate(
            flops=2 * levels * fields * cells,
            bytes_accessed=4 * (levels + 1) * fields * cells,
            transcendentals=0,
        ),
    )(first_row, state_by_level)


def lane_scatter_kernel(order_ref, keys_ref, last_ref, present_ref, val_ref, out_ref):
    order = order_ref[...]
    keys = keys_ref[...]
    last = last_ref[...]
    present = present_ref[...] > 0
    position = lax.broadcasted_iota(jnp.int32, keys.shape, 1)
    links = []
    shift = 1
    while shift < keys.shape[1]:
        joined = (position >= shift) & (pltpu.roll(keys, shift, 1) == keys)
        links.append((shift, joined))
        shift *= 2
    for field in range(val_ref.shape[0]):
        run = jnp.take_along_axis(val_ref[field], order, axis=1, mode="promise_in_bounds")
        for shift, joined in links:
            run = jnp.where(joined, run + pltpu.roll(run, shift, 1), run)
        picked = jnp.take_along_axis(run, last, axis=1, mode="promise_in_bounds")
        out_ref[field] = jnp.where(present, picked, 0.0)


def lane_scatter(values, order, keys, last, present):
    return pl.pallas_call(
        lane_scatter_kernel,
        out_shape=jax.ShapeDtypeStruct(values.shape, values.dtype),
        in_specs=[pl.BlockSpec(memory_space=pltpu.VMEM)] * 5,
        out_specs=pl.BlockSpec(memory_space=pltpu.VMEM),
    )(order, keys, last, present, values)


def per_device(
    atmos_profiles,
    atmos_mixing,
    drag_factor,
    surface_before,
    downward_fluxes,
    land_weight,
    land_surface,
    ocean_state,
    ocean_mixing,
    sea_mask,
    exchange_slot,
    parent_column,
    ocean_weight,
    atmos_weight,
):
    comp_count = lax.axis_size("comp")
    sub_count = lax.axis_size("sub")
    devices = comp_count * sub_count
    columns = atmos_profiles.shape[2]
    intersections = exchange_slot.shape[0]
    ocean_cells = exchange_slot.shape[1]
    capacity = 2 * intersections * ocean_cells // devices
    width = min(128, capacity)
    tile_count = intersections * ocean_cells // width
    slot_tiles = devices * capacity // width
    windows = columns // width
    tile_place = exchange_slot.reshape(tile_count, width)[:, 0] // width
    placement = (tile_place[None, :] == jnp.arange(slot_tiles, dtype=jnp.int32)[:, None]).astype(
        jnp.float32
    )
    tiles_pc = parent_column.reshape(tile_count, width)
    window_of_tile = tiles_pc[:, 0] // width
    lanes = tiles_pc % width
    keys, order = lax.sort(
        (lanes, lax.broadcasted_iota(jnp.int32, lanes.shape, 1)), dimension=1, num_keys=1
    )
    at_most = jnp.sum(
        (lanes[:, None, :] <= jnp.arange(width, dtype=jnp.int32)[None, :, None]).astype(jnp.int32),
        axis=2,
    )
    present = at_most - jnp.pad(at_most[:, :-1], ((0, 0), (1, 0)))
    last = jnp.maximum(at_most - 1, 0)

    state_by_level = jnp.transpose(ocean_state, (1, 0, 2))
    base_top = top_level_mix(ocean_mixing[0], state_by_level)

    request = jnp.dot(placement, window_of_tile.astype(jnp.float32), precision=highest)
    request = (request + 0.5).astype(jnp.int32).reshape(devices, slot_tiles // devices)
    asked = lax.all_to_all(request, ("comp", "sub"), split_axis=0, concat_axis=0, tiled=True)
    asked = asked.reshape(slot_tiles)
    window_hot = (asked[:, None] == jnp.arange(windows, dtype=jnp.int32)[None, :]).astype(
        jnp.float32
    )

    fluxes = surface_fluxes(atmos_profiles, drag_factor, surface_before, downward_fluxes)
    column_forcing = forcing_rows(fluxes)
    served = jnp.einsum(
        "qw,fwl->fql", window_hot, column_forcing.reshape(4, windows, width), precision=highest
    )
    arrived = lax.all_to_all(
        served.reshape(4, devices, capacity),
        ("comp", "sub"),
        split_axis=1,
        concat_axis=1,
        tiled=True,
    )
    atmos_updated = diffuse_atmos(atmos_profiles, atmos_mixing, fluxes)
    win_local = jnp.einsum(
        "qt,fql->ftl", placement, arrived.reshape(4, slot_tiles, width), precision=highest
    )
    at_cells = lane_gather(win_local, lanes).reshape(4, intersections, ocean_cells)
    forcing = jnp.sum(ocean_weight[None] * at_cells, axis=1) / jnp.sum(ocean_weight, axis=0)[None]

    sea = sea_mask[None, :] == 1
    top = jnp.where(sea, base_top + ocean_mixing[0, 0] * forcing, state_by_level[0])
    sea_share = atmos_weight * sea_mask.astype(jnp.float32)[None, :]
    outgoing = jnp.concatenate([sea_share[None] * top[:, None, :], sea_share[None]], axis=0)
    partial = lane_scatter(outgoing.reshape(5, tile_count, width), order, keys, last, present)
    send_buffer = jnp.einsum("qt,ftc->fqc", placement, partial, precision=highest)
    returned = lax.all_to_all(
        send_buffer.reshape(5, devices, capacity),
        ("comp", "sub"),
        split_axis=1,
        concat_axis=1,
        tiled=True,
    )
    summed = jnp.einsum(
        "qw,fqc->fwc", window_hot, returned.reshape(5, slot_tiles, width), precision=highest
    ).reshape(5, columns)
    updated_by_level = ocean_update(ocean_mixing, state_by_level, forcing, sea_mask)
    ocean_updated = jnp.transpose(updated_by_level, (1, 0, 2))
    surface_state = (summed[:4] + land_weight[None] * land_surface) / (summed[4] + land_weight)[
        None
    ]
    return (atmos_updated, ocean_updated, surface_state)


def solution(mesh):
    return jax.shard_map(
        per_device,
        mesh=mesh,
        in_specs=(
            P(None, None, ("comp", "sub")),
            P(),
            P(("comp", "sub")),
            P(None, ("comp", "sub")),
            P(None, ("comp", "sub")),
            P(("comp", "sub")),
            P(None, ("comp", "sub")),
            P(None, None, ("comp", "sub")),
            P(),
            P(("comp", "sub")),
            P(None, ("comp", "sub")),
            P(None, ("comp", "sub")),
            P(None, ("comp", "sub")),
            P(None, ("comp", "sub")),
        ),
        out_specs=(
            P(None, None, ("comp", "sub")),
            P(None, None, ("comp", "sub")),
            P(None, ("comp", "sub")),
        ),
        check_vma=False,
    )
```

```python
import jax
import jax.numpy as jnp
from jax import lax
from jax.experimental import pallas as pl
from jax.experimental.pallas import tpu as pltpu
from jax.sharding import PartitionSpec as P

couple_rate = 0.5
highest = lax.Precision.HIGHEST
high = lax.Precision.HIGH


def surface_fluxes(atmos_profiles, drag_factor, surface_before, downward_fluxes):
    bottom = atmos_profiles[:, -1, :].astype(jnp.float32)
    east_gap = bottom[2] - surface_before[2]
    north_gap = bottom[3] - surface_before[3]
    wind_speed = jnp.sqrt(1.0 + east_gap * east_gap + north_gap * north_gap)
    transfer = drag_factor * wind_speed
    sensible = transfer * (surface_before[0] - bottom[0])
    latent = transfer * (surface_before[1] - bottom[1])
    return jnp.stack(
        [
            sensible,
            latent,
            transfer * east_gap,
            transfer * north_gap,
            downward_fluxes[0],
            downward_fluxes[1],
            downward_fluxes[2],
            downward_fluxes[3],
        ]
    )


def diffuse_atmos(atmos_profiles, atmos_mixing, fluxes):
    lowest = atmos_mixing[:, -1].astype(jnp.float32)
    tendency = couple_rate * jnp.stack([fluxes[0], fluxes[1], -fluxes[2], -fluxes[3]])
    result = []
    for member in range(4):
        mixed_rows = jnp.dot(
            atmos_mixing, atmos_profiles[member], preferred_element_type=jnp.float32
        )
        result.append(mixed_rows + lowest[:, None] * tendency[member][None, :])
    return jnp.stack(result).astype(jnp.bfloat16)


def forcing_rows(fluxes):
    return couple_rate * jnp.stack(
        [
            fluxes[4] + fluxes[5] - fluxes[0] - fluxes[1],
            fluxes[1] - fluxes[6] - fluxes[7],
            fluxes[2],
            fluxes[3],
        ]
    )


def lane_gather_kernel(win_ref, lanes_ref, out_ref):
    lanes = lanes_ref[...]
    for field in range(win_ref.shape[0]):
        out_ref[field] = jnp.take_along_axis(
            win_ref[field], lanes, axis=1, mode="promise_in_bounds"
        )


def lane_gather(win, lanes):
    return pl.pallas_call(
        lane_gather_kernel,
        out_shape=jax.ShapeDtypeStruct(win.shape, win.dtype),
        in_specs=[pl.BlockSpec(memory_space=pltpu.VMEM)] * 2,
        out_specs=pl.BlockSpec(memory_space=pltpu.VMEM),
    )(win, lanes)


def split_kept(values):
    upper = lax.reduce_precision(values, exponent_bits=8, mantissa_bits=7)
    return upper.astype(jnp.bfloat16), (values - upper).astype(jnp.bfloat16)


def ocean_kernel(m_ref, m0_ref, x_ref, forcing_ref, sea_ref, out_ref):
    m = m_ref[...]
    m0 = m0_ref[...]
    sea = sea_ref[...] == 1
    for field in range(x_ref.shape[1]):
        x = x_ref[:, field, :]
        mixed = jnp.dot(m, x, precision=highest, preferred_element_type=jnp.float32)
        mixed = mixed + m0 * forcing_ref[field : field + 1, :]
        out_ref[:, field, :] = jnp.where(sea, mixed, x)


def ocean_update(ocean_mixing, state_by_level, forcing, sea_mask, block=1024):
    levels, fields, cells = state_by_level.shape
    return pl.pallas_call(
        ocean_kernel,
        grid=(cells // block,),
        out_shape=jax.ShapeDtypeStruct(state_by_level.shape, jnp.float32),
        in_specs=[
            pl.BlockSpec((levels, levels), lambda i: (0, 0)),
            pl.BlockSpec((levels, 1), lambda i: (0, 0)),
            pl.BlockSpec((levels, fields, block), lambda i: (0, 0, i)),
            pl.BlockSpec((fields, block), lambda i: (0, i)),
            pl.BlockSpec((1, block), lambda i: (0, i)),
        ],
        out_specs=pl.BlockSpec((levels, fields, block), lambda i: (0, 0, i)),
        cost_estimate=pl.CostEstimate(
            flops=12 * levels * levels * fields * cells,
            bytes_accessed=8 * levels * fields * cells,
            transcendentals=0,
        ),
    )(ocean_mixing, ocean_mixing[:, 0:1], state_by_level, forcing, sea_mask.reshape(1, cells))


def top_level_kernel(row_ref, x_ref, out_ref):
    total = row_ref[0] * x_ref[0]
    for level in range(1, x_ref.shape[0]):
        total = total + row_ref[level] * x_ref[level]
    out_ref[...] = total


def top_level_mix(first_row, state_by_level, block=2048):
    levels, fields, cells = state_by_level.shape
    return pl.pallas_call(
        top_level_kernel,
        grid=(cells // block,),
        out_shape=jax.ShapeDtypeStruct((fields, cells), jnp.float32),
        in_specs=[
            pl.BlockSpec(memory_space=pltpu.SMEM),
            pl.BlockSpec((levels, fields, block), lambda i: (0, 0, i)),
        ],
        out_specs=pl.BlockSpec((fields, block), lambda i: (0, i)),
        cost_estimate=pl.CostEstimate(
            flops=2 * levels * fields * cells,
            bytes_accessed=4 * (levels + 1) * fields * cells,
            transcendentals=0,
        ),
    )(first_row, state_by_level)


def lane_scatter_kernel(order_ref, keys_ref, last_ref, present_ref, val_ref, out_ref):
    order = order_ref[...]
    keys = keys_ref[...]
    last = last_ref[...]
    present = present_ref[...] > 0
    position = lax.broadcasted_iota(jnp.int32, keys.shape, 1)
    links = []
    shift = 1
    while shift < keys.shape[1]:
        joined = (position >= shift) & (pltpu.roll(keys, shift, 1) == keys)
        links.append((shift, joined))
        shift *= 2
    for field in range(val_ref.shape[0]):
        run = jnp.take_along_axis(val_ref[field], order, axis=1, mode="promise_in_bounds")
        for shift, joined in links:
            run = jnp.where(joined, run + pltpu.roll(run, shift, 1), run)
        picked = jnp.take_along_axis(run, last, axis=1, mode="promise_in_bounds")
        out_ref[field] = jnp.where(present, picked, 0.0)


def lane_scatter(values, order, keys, last, present):
    return pl.pallas_call(
        lane_scatter_kernel,
        out_shape=jax.ShapeDtypeStruct(values.shape, values.dtype),
        in_specs=[pl.BlockSpec(memory_space=pltpu.VMEM)] * 5,
        out_specs=pl.BlockSpec(memory_space=pltpu.VMEM),
    )(order, keys, last, present, values)


def lane_sort_kernel(key_ref, sorted_ref):
    values = key_ref[...]
    count = values.shape[1]
    position = lax.broadcasted_iota(jnp.int32, values.shape, 1)
    block = 2
    while block <= count:
        stride = block // 2
        while stride >= 1:
            lower = (position & stride) == 0
            partner = jnp.where(
                lower, pltpu.roll(values, count - stride, 1), pltpu.roll(values, stride, 1)
            )
            keep_min = lower == ((position & block) == 0)
            values = jnp.where(
                keep_min, jnp.minimum(values, partner), jnp.maximum(values, partner)
            )
            stride //= 2
        block *= 2
    sorted_ref[...] = values


def lane_sort(keys):
    return pl.pallas_call(
        lane_sort_kernel,
        out_shape=jax.ShapeDtypeStruct(keys.shape, keys.dtype),
        in_specs=[pl.BlockSpec(memory_space=pltpu.VMEM)],
        out_specs=pl.BlockSpec(memory_space=pltpu.VMEM),
    )(keys)


def per_device(
    atmos_profiles,
    atmos_mixing,
    drag_factor,
    surface_before,
    downward_fluxes,
    land_weight,
    land_surface,
    ocean_state,
    ocean_mixing,
    sea_mask,
    exchange_slot,
    parent_column,
    ocean_weight,
    atmos_weight,
):
    comp_count = lax.axis_size("comp")
    sub_count = lax.axis_size("sub")
    devices = comp_count * sub_count
    columns = atmos_profiles.shape[2]
    intersections = exchange_slot.shape[0]
    ocean_cells = exchange_slot.shape[1]
    capacity = 2 * intersections * ocean_cells // devices
    width = min(128, capacity)
    tile_count = intersections * ocean_cells // width
    slot_tiles = devices * capacity // width
    windows = columns // width
    tile_place = exchange_slot.reshape(tile_count, width)[:, 0] // width
    placement = (tile_place[None, :] == jnp.arange(slot_tiles, dtype=jnp.int32)[:, None]).astype(
        jnp.float32
    )
    tiles_pc = parent_column.reshape(tile_count, width)
    window_of_tile = tiles_pc[:, 0] // width
    lanes = tiles_pc % width
    ranked = lane_sort(lanes * width + lax.broadcasted_iota(jnp.int32, lanes.shape, 1))
    keys, order = ranked // width, ranked % width
    at_most = jnp.sum(
        (lanes[:, None, :] <= jnp.arange(width, dtype=jnp.int32)[None, :, None]).astype(jnp.int32),
        axis=2,
    )
    present = at_most - jnp.pad(at_most[:, :-1], ((0, 0), (1, 0)))
    last = jnp.maximum(at_most - 1, 0)

    state_by_level = jnp.transpose(ocean_state, (1, 0, 2))
    base_top = top_level_mix(ocean_mixing[0], state_by_level)

    request = jnp.dot(placement, window_of_tile.astype(jnp.float32), precision=highest)
    request = (request + 0.5).astype(jnp.int32).reshape(devices, slot_tiles // devices)
    asked = lax.all_to_all(request, ("comp", "sub"), split_axis=0, concat_axis=0, tiled=True)
    asked = asked.reshape(slot_tiles)
    window_hot = (asked[:, None] == jnp.arange(windows, dtype=jnp.int32)[None, :]).astype(
        jnp.float32
    )

    fluxes = surface_fluxes(atmos_profiles, drag_factor, surface_before, downward_fluxes)
    column_forcing = forcing_rows(fluxes)
    served = jnp.einsum(
        "qw,fwl->fql", window_hot, column_forcing.reshape(4, windows, width), precision=highest
    )
    arrived = lax.all_to_all(
        served.reshape(4, devices, capacity),
        ("comp", "sub"),
        split_axis=1,
        concat_axis=1,
        tiled=True,
    )
    atmos_updated = diffuse_atmos(atmos_profiles, atmos_mixing, fluxes)
    win_local = jnp.einsum(
        "qt,fql->ftl", placement, arrived.reshape(4, slot_tiles, width), precision=highest
    )
    at_cells = lane_gather(win_local, lanes).reshape(4, intersections, ocean_cells)
    forcing = jnp.sum(ocean_weight[None] * at_cells, axis=1) / jnp.sum(ocean_weight, axis=0)[None]

    sea = sea_mask[None, :] == 1
    top = jnp.where(sea, base_top + ocean_mixing[0, 0] * forcing, state_by_level[0])
    sea_share = atmos_weight * sea_mask.astype(jnp.float32)[None, :]
    outgoing = jnp.concatenate([sea_share[None] * top[:, None, :], sea_share[None]], axis=0)
    partial = lane_scatter(outgoing.reshape(5, tile_count, width), order, keys, last, present)
    send_buffer = jnp.einsum("qt,ftc->fqc", placement, partial, precision=highest)
    returned = lax.all_to_all(
        send_buffer.reshape(5, devices, capacity),
        ("comp", "sub"),
        split_axis=1,
        concat_axis=1,
        tiled=True,
    )
    summed = jnp.einsum(
        "qw,fqc->fwc", window_hot, returned.reshape(5, slot_tiles, width), precision=highest
    ).reshape(5, columns)
    updated_by_level = ocean_update(ocean_mixing, state_by_level, forcing, sea_mask)
    ocean_updated = jnp.transpose(updated_by_level, (1, 0, 2))
    surface_state = (summed[:4] + land_weight[None] * land_surface) / (summed[4] + land_weight)[
        None
    ]
    return (atmos_updated, ocean_updated, surface_state)


def solution(mesh):
    return jax.shard_map(
        per_device,
        mesh=mesh,
        in_specs=(
            P(None, None, ("comp", "sub")),
            P(),
            P(("comp", "sub")),
            P(None, ("comp", "sub")),
            P(None, ("comp", "sub")),
            P(("comp", "sub")),
            P(None, ("comp", "sub")),
            P(None, None, ("comp", "sub")),
            P(),
            P(("comp", "sub")),
            P(None, ("comp", "sub")),
            P(None, ("comp", "sub")),
            P(None, ("comp", "sub")),
            P(None, ("comp", "sub")),
        ),
        out_specs=(
            P(None, None, ("comp", "sub")),
            P(None, None, ("comp", "sub")),
            P(None, ("comp", "sub")),
        ),
        check_vma=False,
    )
```

```python
import jax
import jax.numpy as jnp
from jax import lax
from jax.experimental import pallas as pl
from jax.experimental.pallas import tpu as pltpu
from jax.sharding import PartitionSpec as P

couple_rate = 0.5
highest = lax.Precision.HIGHEST
high = lax.Precision.HIGH


def surface_fluxes(atmos_profiles, drag_factor, surface_before, downward_fluxes):
    bottom = atmos_profiles[:, -1, :].astype(jnp.float32)
    east_gap = bottom[2] - surface_before[2]
    north_gap = bottom[3] - surface_before[3]
    wind_speed = jnp.sqrt(1.0 + east_gap * east_gap + north_gap * north_gap)
    transfer = drag_factor * wind_speed
    sensible = transfer * (surface_before[0] - bottom[0])
    latent = transfer * (surface_before[1] - bottom[1])
    return jnp.stack(
        [
            sensible,
            latent,
            transfer * east_gap,
            transfer * north_gap,
            downward_fluxes[0],
            downward_fluxes[1],
            downward_fluxes[2],
            downward_fluxes[3],
        ]
    )


def diffuse_atmos(atmos_profiles, atmos_mixing, fluxes):
    lowest = atmos_mixing[:, -1].astype(jnp.float32)
    tendency = couple_rate * jnp.stack([fluxes[0], fluxes[1], -fluxes[2], -fluxes[3]])
    result = []
    for member in range(4):
        mixed_rows = jnp.dot(
            atmos_mixing, atmos_profiles[member], preferred_element_type=jnp.float32
        )
        result.append(mixed_rows + lowest[:, None] * tendency[member][None, :])
    return jnp.stack(result).astype(jnp.bfloat16)


def forcing_rows(fluxes):
    return couple_rate * jnp.stack(
        [
            fluxes[4] + fluxes[5] - fluxes[0] - fluxes[1],
            fluxes[1] - fluxes[6] - fluxes[7],
            fluxes[2],
            fluxes[3],
        ]
    )


def lane_gather_kernel(win_ref, lanes_ref, out_ref):
    lanes = lanes_ref[...]
    for field in range(win_ref.shape[0]):
        out_ref[field] = jnp.take_along_axis(
            win_ref[field], lanes, axis=1, mode="promise_in_bounds"
        )


def lane_gather(win, lanes):
    return pl.pallas_call(
        lane_gather_kernel,
        out_shape=jax.ShapeDtypeStruct(win.shape, win.dtype),
        in_specs=[pl.BlockSpec(memory_space=pltpu.VMEM)] * 2,
        out_specs=pl.BlockSpec(memory_space=pltpu.VMEM),
    )(win, lanes)


def split_kept(values):
    upper = lax.reduce_precision(values, exponent_bits=8, mantissa_bits=7)
    return upper.astype(jnp.bfloat16), (values - upper).astype(jnp.bfloat16)


def ocean_kernel(m_ref, m0_ref, x_ref, forcing_ref, sea_ref, out_ref):
    m = m_ref[...]
    m0 = m0_ref[...]
    sea = sea_ref[...] == 1
    for field in range(x_ref.shape[1]):
        x = x_ref[:, field, :]
        mixed = jnp.dot(m, x, precision=highest, preferred_element_type=jnp.float32)
        mixed = mixed + m0 * forcing_ref[field : field + 1, :]
        out_ref[:, field, :] = jnp.where(sea, mixed, x)


def ocean_update(ocean_mixing, state_by_level, forcing, sea_mask, block=1024):
    levels, fields, cells = state_by_level.shape
    return pl.pallas_call(
        ocean_kernel,
        grid=(cells // block,),
        out_shape=jax.ShapeDtypeStruct(state_by_level.shape, jnp.float32),
        in_specs=[
            pl.BlockSpec((levels, levels), lambda i: (0, 0)),
            pl.BlockSpec((levels, 1), lambda i: (0, 0)),
            pl.BlockSpec((levels, fields, block), lambda i: (0, 0, i)),
            pl.BlockSpec((fields, block), lambda i: (0, i)),
            pl.BlockSpec((1, block), lambda i: (0, i)),
        ],
        out_specs=pl.BlockSpec((levels, fields, block), lambda i: (0, 0, i)),
        cost_estimate=pl.CostEstimate(
            flops=12 * levels * levels * fields * cells,
            bytes_accessed=8 * levels * fields * cells,
            transcendentals=0,
        ),
    )(ocean_mixing, ocean_mixing[:, 0:1], state_by_level, forcing, sea_mask.reshape(1, cells))


def top_level_kernel(row_ref, x_ref, out_ref):
    total = row_ref[0] * x_ref[0]
    for level in range(1, x_ref.shape[0]):
        total = total + row_ref[level] * x_ref[level]
    out_ref[...] = total


def top_level_mix(first_row, state_by_level, block=2048):
    levels, fields, cells = state_by_level.shape
    return pl.pallas_call(
        top_level_kernel,
        grid=(cells // block,),
        out_shape=jax.ShapeDtypeStruct((fields, cells), jnp.float32),
        in_specs=[
            pl.BlockSpec(memory_space=pltpu.SMEM),
            pl.BlockSpec((levels, fields, block), lambda i: (0, 0, i)),
        ],
        out_specs=pl.BlockSpec((fields, block), lambda i: (0, i)),
        cost_estimate=pl.CostEstimate(
            flops=2 * levels * fields * cells,
            bytes_accessed=4 * (levels + 1) * fields * cells,
            transcendentals=0,
        ),
    )(first_row, state_by_level)


def lane_scatter_kernel(order_ref, keys_ref, last_ref, present_ref, val_ref, out_ref):
    order = order_ref[...]
    keys = keys_ref[...]
    last = last_ref[...]
    present = present_ref[...] > 0
    position = lax.broadcasted_iota(jnp.int32, keys.shape, 1)
    links = []
    shift = 1
    while shift < keys.shape[1]:
        joined = (position >= shift) & (pltpu.roll(keys, shift, 1) == keys)
        links.append((shift, joined))
        shift *= 2
    for field in range(val_ref.shape[0]):
        run = jnp.take_along_axis(val_ref[field], order, axis=1, mode="promise_in_bounds")
        for shift, joined in links:
            run = jnp.where(joined, run + pltpu.roll(run, shift, 1), run)
        picked = jnp.take_along_axis(run, last, axis=1, mode="promise_in_bounds")
        out_ref[field] = jnp.where(present, picked, 0.0)


def lane_scatter(values, order, keys, last, present):
    return pl.pallas_call(
        lane_scatter_kernel,
        out_shape=jax.ShapeDtypeStruct(values.shape, values.dtype),
        in_specs=[pl.BlockSpec(memory_space=pltpu.VMEM)] * 5,
        out_specs=pl.BlockSpec(memory_space=pltpu.VMEM),
    )(order, keys, last, present, values)


def lane_sort_kernel(key_ref, sorted_ref):
    values = key_ref[...]
    count = values.shape[1]
    position = lax.broadcasted_iota(jnp.int32, values.shape, 1)
    block = 2
    while block <= count:
        stride = block // 2
        while stride >= 1:
            lower = (position & stride) == 0
            partner = jnp.where(
                lower, pltpu.roll(values, count - stride, 1), pltpu.roll(values, stride, 1)
            )
            keep_min = lower == ((position & block) == 0)
            values = jnp.where(
                keep_min, jnp.minimum(values, partner), jnp.maximum(values, partner)
            )
            stride //= 2
        block *= 2
    sorted_ref[...] = values


def lane_sort(keys):
    return pl.pallas_call(
        lane_sort_kernel,
        out_shape=jax.ShapeDtypeStruct(keys.shape, keys.dtype),
        in_specs=[pl.BlockSpec(memory_space=pltpu.VMEM)],
        out_specs=pl.BlockSpec(memory_space=pltpu.VMEM),
    )(keys)


def per_device(
    atmos_profiles,
    atmos_mixing,
    drag_factor,
    surface_before,
    downward_fluxes,
    land_weight,
    land_surface,
    ocean_state,
    ocean_mixing,
    sea_mask,
    exchange_slot,
    parent_column,
    ocean_weight,
    atmos_weight,
):
    comp_count = lax.axis_size("comp")
    sub_count = lax.axis_size("sub")
    devices = comp_count * sub_count
    columns = atmos_profiles.shape[2]
    intersections = exchange_slot.shape[0]
    ocean_cells = exchange_slot.shape[1]
    capacity = 2 * intersections * ocean_cells // devices
    width = min(128, capacity)
    tile_count = intersections * ocean_cells // width
    slot_tiles = devices * capacity // width
    windows = columns // width
    tile_place = exchange_slot.reshape(tile_count, width)[:, 0] // width
    placement = (tile_place[None, :] == jnp.arange(slot_tiles, dtype=jnp.int32)[:, None]).astype(
        jnp.float32
    )
    tiles_pc = parent_column.reshape(tile_count, width)
    window_of_tile = tiles_pc[:, 0] // width
    lanes = tiles_pc % width
    ranked = lane_sort(lanes * width + lax.broadcasted_iota(jnp.int32, lanes.shape, 1))
    keys, order = ranked // width, ranked % width
    at_most = jnp.sum(
        (lanes[:, None, :] <= jnp.arange(width, dtype=jnp.int32)[None, :, None]).astype(jnp.int32),
        axis=2,
    )
    present = at_most - jnp.pad(at_most[:, :-1], ((0, 0), (1, 0)))
    last = jnp.maximum(at_most - 1, 0)

    state_by_level = jnp.transpose(ocean_state, (1, 0, 2))
    base_top = top_level_mix(ocean_mixing[0], state_by_level)

    request = jnp.dot(placement, window_of_tile.astype(jnp.float32), precision=highest)
    request = (request + 0.5).astype(jnp.int32).reshape(devices, slot_tiles // devices)
    asked = lax.all_to_all(request, ("comp", "sub"), split_axis=0, concat_axis=0, tiled=True)
    asked = asked.reshape(slot_tiles)
    window_hot = (asked[:, None] == jnp.arange(windows, dtype=jnp.int32)[None, :]).astype(
        jnp.float32
    )

    fluxes = surface_fluxes(atmos_profiles, drag_factor, surface_before, downward_fluxes)
    column_forcing = forcing_rows(fluxes)
    served = jnp.einsum(
        "qw,fwl->fql", window_hot, column_forcing.reshape(4, windows, width), precision=highest
    )
    arrived = lax.all_to_all(
        served.reshape(4, devices, capacity),
        ("comp", "sub"),
        split_axis=1,
        concat_axis=1,
        tiled=True,
    )
    win_local = jnp.einsum(
        "qt,fql->ftl", placement, arrived.reshape(4, slot_tiles, width), precision=highest
    )
    at_cells = lane_gather(win_local, lanes).reshape(4, intersections, ocean_cells)
    forcing = jnp.sum(ocean_weight[None] * at_cells, axis=1) / jnp.sum(ocean_weight, axis=0)[None]

    sea = sea_mask[None, :] == 1
    top = jnp.where(sea, base_top + ocean_mixing[0, 0] * forcing, state_by_level[0])
    sea_share = atmos_weight * sea_mask.astype(jnp.float32)[None, :]
    outgoing = jnp.concatenate([sea_share[None] * top[:, None, :], sea_share[None]], axis=0)
    partial = lane_scatter(outgoing.reshape(5, tile_count, width), order, keys, last, present)
    send_buffer = jnp.einsum("qt,ftc->fqc", placement, partial, precision=highest)
    late_profiles, send_buffer = lax.optimization_barrier((atmos_profiles, send_buffer))
    atmos_updated = diffuse_atmos(late_profiles, atmos_mixing, fluxes)
    returned = lax.all_to_all(
        send_buffer.reshape(5, devices, capacity),
        ("comp", "sub"),
        split_axis=1,
        concat_axis=1,
        tiled=True,
    )
    summed = jnp.einsum(
        "qw,fqc->fwc", window_hot, returned.reshape(5, slot_tiles, width), precision=highest
    ).reshape(5, columns)
    updated_by_level = ocean_update(ocean_mixing, state_by_level, forcing, sea_mask)
    ocean_updated = jnp.transpose(updated_by_level, (1, 0, 2))
    surface_state = (summed[:4] + land_weight[None] * land_surface) / (summed[4] + land_weight)[
        None
    ]
    return (atmos_updated, ocean_updated, surface_state)


def solution(mesh):
    return jax.shard_map(
        per_device,
        mesh=mesh,
        in_specs=(
            P(None, None, ("comp", "sub")),
            P(),
            P(("comp", "sub")),
            P(None, ("comp", "sub")),
            P(None, ("comp", "sub")),
            P(("comp", "sub")),
            P(None, ("comp", "sub")),
            P(None, None, ("comp", "sub")),
            P(),
            P(("comp", "sub")),
            P(None, ("comp", "sub")),
            P(None, ("comp", "sub")),
            P(None, ("comp", "sub")),
            P(None, ("comp", "sub")),
        ),
        out_specs=(
            P(None, None, ("comp", "sub")),
            P(None, None, ("comp", "sub")),
            P(None, ("comp", "sub")),
        ),
        check_vma=False,
    )
```

```python
import jax
import jax.numpy as jnp
from jax import lax
from jax.experimental import pallas as pl
from jax.experimental.pallas import tpu as pltpu
from jax.sharding import PartitionSpec as P

couple_rate = 0.5
highest = lax.Precision.HIGHEST
high = lax.Precision.HIGH


def surface_fluxes(atmos_profiles, drag_factor, surface_before, downward_fluxes):
    bottom = atmos_profiles[:, -1, :].astype(jnp.float32)
    east_gap = bottom[2] - surface_before[2]
    north_gap = bottom[3] - surface_before[3]
    wind_speed = jnp.sqrt(1.0 + east_gap * east_gap + north_gap * north_gap)
    transfer = drag_factor * wind_speed
    sensible = transfer * (surface_before[0] - bottom[0])
    latent = transfer * (surface_before[1] - bottom[1])
    return jnp.stack(
        [
            sensible,
            latent,
            transfer * east_gap,
            transfer * north_gap,
            downward_fluxes[0],
            downward_fluxes[1],
            downward_fluxes[2],
            downward_fluxes[3],
        ]
    )


def diffuse_atmos(atmos_profiles, atmos_mixing, fluxes):
    lowest = atmos_mixing[:, -1].astype(jnp.float32)
    tendency = couple_rate * jnp.stack([fluxes[0], fluxes[1], -fluxes[2], -fluxes[3]])
    result = []
    for member in range(4):
        mixed_rows = jnp.dot(
            atmos_mixing, atmos_profiles[member], preferred_element_type=jnp.float32
        )
        result.append(mixed_rows + lowest[:, None] * tendency[member][None, :])
    return jnp.stack(result).astype(jnp.bfloat16)


def forcing_rows(fluxes):
    return couple_rate * jnp.stack(
        [
            fluxes[4] + fluxes[5] - fluxes[0] - fluxes[1],
            fluxes[1] - fluxes[6] - fluxes[7],
            fluxes[2],
            fluxes[3],
        ]
    )


def lane_gather_kernel(win_ref, lanes_ref, out_ref):
    lanes = lanes_ref[...]
    for field in range(win_ref.shape[0]):
        out_ref[field] = jnp.take_along_axis(
            win_ref[field], lanes, axis=1, mode="promise_in_bounds"
        )


def lane_gather(win, lanes):
    return pl.pallas_call(
        lane_gather_kernel,
        out_shape=jax.ShapeDtypeStruct(win.shape, win.dtype),
        in_specs=[pl.BlockSpec(memory_space=pltpu.VMEM)] * 2,
        out_specs=pl.BlockSpec(memory_space=pltpu.VMEM),
    )(win, lanes)


def split_kept(values):
    upper = lax.reduce_precision(values, exponent_bits=8, mantissa_bits=7)
    return upper.astype(jnp.bfloat16), (values - upper).astype(jnp.bfloat16)


def ocean_kernel(m_ref, m0_ref, x_ref, forcing_ref, sea_ref, out_ref):
    m = m_ref[...]
    m0 = m0_ref[...]
    sea = sea_ref[...] == 1
    for field in range(x_ref.shape[1]):
        x = x_ref[:, field, :]
        mixed = jnp.dot(m, x, precision=highest, preferred_element_type=jnp.float32)
        mixed = mixed + m0 * forcing_ref[field : field + 1, :]
        out_ref[:, field, :] = jnp.where(sea, mixed, x)


def ocean_update(ocean_mixing, state_by_level, forcing, sea_mask, block=1024):
    levels, fields, cells = state_by_level.shape
    return pl.pallas_call(
        ocean_kernel,
        grid=(cells // block,),
        out_shape=jax.ShapeDtypeStruct(state_by_level.shape, jnp.float32),
        in_specs=[
            pl.BlockSpec((levels, levels), lambda i: (0, 0)),
            pl.BlockSpec((levels, 1), lambda i: (0, 0)),
            pl.BlockSpec((levels, fields, block), lambda i: (0, 0, i)),
            pl.BlockSpec((fields, block), lambda i: (0, i)),
            pl.BlockSpec((1, block), lambda i: (0, i)),
        ],
        out_specs=pl.BlockSpec((levels, fields, block), lambda i: (0, 0, i)),
        cost_estimate=pl.CostEstimate(
            flops=12 * levels * levels * fields * cells,
            bytes_accessed=8 * levels * fields * cells,
            transcendentals=0,
        ),
    )(ocean_mixing, ocean_mixing[:, 0:1], state_by_level, forcing, sea_mask.reshape(1, cells))


def top_level_kernel(row_ref, x_ref, out_ref):
    total = row_ref[0] * x_ref[0]
    for level in range(1, x_ref.shape[0]):
        total = total + row_ref[level] * x_ref[level]
    out_ref[...] = total


def top_level_mix(first_row, state_by_level, block=2048):
    levels, fields, cells = state_by_level.shape
    return pl.pallas_call(
        top_level_kernel,
        grid=(cells // block,),
        out_shape=jax.ShapeDtypeStruct((fields, cells), jnp.float32),
        in_specs=[
            pl.BlockSpec(memory_space=pltpu.SMEM),
            pl.BlockSpec((levels, fields, block), lambda i: (0, 0, i)),
        ],
        out_specs=pl.BlockSpec((fields, block), lambda i: (0, i)),
        cost_estimate=pl.CostEstimate(
            flops=2 * levels * fields * cells,
            bytes_accessed=4 * (levels + 1) * fields * cells,
            transcendentals=0,
        ),
    )(first_row, state_by_level)


def lane_scatter_kernel(order_ref, keys_ref, last_ref, present_ref, val_ref, out_ref):
    order = order_ref[...]
    keys = keys_ref[...]
    last = last_ref[...]
    present = present_ref[...] > 0
    position = lax.broadcasted_iota(jnp.int32, keys.shape, 1)
    links = []
    shift = 1
    while shift < keys.shape[1]:
        joined = (position >= shift) & (pltpu.roll(keys, shift, 1) == keys)
        links.append((shift, joined))
        shift *= 2
    for field in range(val_ref.shape[0]):
        run = jnp.take_along_axis(val_ref[field], order, axis=1, mode="promise_in_bounds")
        for shift, joined in links:
            run = jnp.where(joined, run + pltpu.roll(run, shift, 1), run)
        picked = jnp.take_along_axis(run, last, axis=1, mode="promise_in_bounds")
        out_ref[field] = jnp.where(present, picked, 0.0)


def lane_scatter(values, order, keys, last, present):
    return pl.pallas_call(
        lane_scatter_kernel,
        out_shape=jax.ShapeDtypeStruct(values.shape, values.dtype),
        in_specs=[pl.BlockSpec(memory_space=pltpu.VMEM)] * 5,
        out_specs=pl.BlockSpec(memory_space=pltpu.VMEM),
    )(order, keys, last, present, values)


def lane_sort_kernel(key_ref, sorted_ref):
    values = key_ref[...]
    count = values.shape[1]
    position = lax.broadcasted_iota(jnp.int32, values.shape, 1)
    block = 2
    while block <= count:
        stride = block // 2
        while stride >= 1:
            lower = (position & stride) == 0
            partner = jnp.where(
                lower, pltpu.roll(values, count - stride, 1), pltpu.roll(values, stride, 1)
            )
            keep_min = lower == ((position & block) == 0)
            values = jnp.where(
                keep_min, jnp.minimum(values, partner), jnp.maximum(values, partner)
            )
            stride //= 2
        block *= 2
    sorted_ref[...] = values


def lane_sort(keys):
    return pl.pallas_call(
        lane_sort_kernel,
        out_shape=jax.ShapeDtypeStruct(keys.shape, keys.dtype),
        in_specs=[pl.BlockSpec(memory_space=pltpu.VMEM)],
        out_specs=pl.BlockSpec(memory_space=pltpu.VMEM),
    )(keys)


def per_device(
    atmos_profiles,
    atmos_mixing,
    drag_factor,
    surface_before,
    downward_fluxes,
    land_weight,
    land_surface,
    ocean_state,
    ocean_mixing,
    sea_mask,
    exchange_slot,
    parent_column,
    ocean_weight,
    atmos_weight,
):
    comp_count = lax.axis_size("comp")
    sub_count = lax.axis_size("sub")
    devices = comp_count * sub_count
    columns = atmos_profiles.shape[2]
    intersections = exchange_slot.shape[0]
    ocean_cells = exchange_slot.shape[1]
    capacity = 2 * intersections * ocean_cells // devices
    width = min(128, capacity)
    tile_count = intersections * ocean_cells // width
    slot_tiles = devices * capacity // width
    windows = columns // width
    tile_place = exchange_slot.reshape(tile_count, width)[:, 0] // width
    placement = (tile_place[None, :] == jnp.arange(slot_tiles, dtype=jnp.int32)[:, None]).astype(
        jnp.float32
    )
    tiles_pc = parent_column.reshape(tile_count, width)
    window_of_tile = tiles_pc[:, 0] // width
    lanes = tiles_pc % width

    state_by_level = jnp.transpose(ocean_state, (1, 0, 2))

    request = jnp.dot(placement, window_of_tile.astype(jnp.float32), precision=highest)
    request = (request + 0.5).astype(jnp.int32).reshape(devices, slot_tiles // devices)
    asked = lax.all_to_all(request, ("comp", "sub"), split_axis=0, concat_axis=0, tiled=True)
    asked = asked.reshape(slot_tiles)
    window_hot = (asked[:, None] == jnp.arange(windows, dtype=jnp.int32)[None, :]).astype(
        jnp.float32
    )

    fluxes = surface_fluxes(atmos_profiles, drag_factor, surface_before, downward_fluxes)
    column_forcing = forcing_rows(fluxes)
    served = jnp.einsum(
        "qw,fwl->fql", window_hot, column_forcing.reshape(4, windows, width), precision=highest
    )
    late_lanes, late_state, served = lax.optimization_barrier((lanes, state_by_level, served))
    base_top = top_level_mix(ocean_mixing[0], late_state)
    ranked = lane_sort(late_lanes * width + lax.broadcasted_iota(jnp.int32, late_lanes.shape, 1))
    keys, order = ranked // width, ranked % width
    at_most = jnp.sum(
        (late_lanes[:, None, :] <= jnp.arange(width, dtype=jnp.int32)[None, :, None]).astype(jnp.int32),
        axis=2,
    )
    present = at_most - jnp.pad(at_most[:, :-1], ((0, 0), (1, 0)))
    last = jnp.maximum(at_most - 1, 0)
    arrived = lax.all_to_all(
        served.reshape(4, devices, capacity),
        ("comp", "sub"),
        split_axis=1,
        concat_axis=1,
        tiled=True,
    )
    win_local = jnp.einsum(
        "qt,fql->ftl", placement, arrived.reshape(4, slot_tiles, width), precision=highest
    )
    at_cells = lane_gather(win_local, lanes).reshape(4, intersections, ocean_cells)
    forcing = jnp.sum(ocean_weight[None] * at_cells, axis=1) / jnp.sum(ocean_weight, axis=0)[None]

    sea = sea_mask[None, :] == 1
    top = jnp.where(sea, base_top + ocean_mixing[0, 0] * forcing, state_by_level[0])
    sea_share = atmos_weight * sea_mask.astype(jnp.float32)[None, :]
    outgoing = jnp.concatenate([sea_share[None] * top[:, None, :], sea_share[None]], axis=0)
    partial = lane_scatter(outgoing.reshape(5, tile_count, width), order, keys, last, present)
    send_buffer = jnp.einsum("qt,ftc->fqc", placement, partial, precision=highest)
    late_profiles, send_buffer = lax.optimization_barrier((atmos_profiles, send_buffer))
    atmos_updated = diffuse_atmos(late_profiles, atmos_mixing, fluxes)
    returned = lax.all_to_all(
        send_buffer.reshape(5, devices, capacity),
        ("comp", "sub"),
        split_axis=1,
        concat_axis=1,
        tiled=True,
    )
    summed = jnp.einsum(
        "qw,fqc->fwc", window_hot, returned.reshape(5, slot_tiles, width), precision=highest
    ).reshape(5, columns)
    updated_by_level = ocean_update(ocean_mixing, state_by_level, forcing, sea_mask)
    ocean_updated = jnp.transpose(updated_by_level, (1, 0, 2))
    surface_state = (summed[:4] + land_weight[None] * land_surface) / (summed[4] + land_weight)[
        None
    ]
    return (atmos_updated, ocean_updated, surface_state)


def solution(mesh):
    return jax.shard_map(
        per_device,
        mesh=mesh,
        in_specs=(
            P(None, None, ("comp", "sub")),
            P(),
            P(("comp", "sub")),
            P(None, ("comp", "sub")),
            P(None, ("comp", "sub")),
            P(("comp", "sub")),
            P(None, ("comp", "sub")),
            P(None, None, ("comp", "sub")),
            P(),
            P(("comp", "sub")),
            P(None, ("comp", "sub")),
            P(None, ("comp", "sub")),
            P(None, ("comp", "sub")),
            P(None, ("comp", "sub")),
        ),
        out_specs=(
            P(None, None, ("comp", "sub")),
            P(None, None, ("comp", "sub")),
            P(None, ("comp", "sub")),
        ),
        check_vma=False,
    )
```

```python
import jax
import jax.numpy as jnp
from jax import lax
from jax.experimental import pallas as pl
from jax.experimental.pallas import tpu as pltpu
from jax.sharding import PartitionSpec as P

couple_rate = 0.5
highest = lax.Precision.HIGHEST
high = lax.Precision.HIGH


def surface_fluxes(atmos_profiles, drag_factor, surface_before, downward_fluxes):
    bottom = atmos_profiles[:, -1, :].astype(jnp.float32)
    east_gap = bottom[2] - surface_before[2]
    north_gap = bottom[3] - surface_before[3]
    wind_speed = jnp.sqrt(1.0 + east_gap * east_gap + north_gap * north_gap)
    transfer = drag_factor * wind_speed
    sensible = transfer * (surface_before[0] - bottom[0])
    latent = transfer * (surface_before[1] - bottom[1])
    return jnp.stack(
        [
            sensible,
            latent,
            transfer * east_gap,
            transfer * north_gap,
            downward_fluxes[0],
            downward_fluxes[1],
            downward_fluxes[2],
            downward_fluxes[3],
        ]
    )


def diffuse_atmos(atmos_profiles, atmos_mixing, fluxes):
    lowest = atmos_mixing[:, -1].astype(jnp.float32)
    tendency = couple_rate * jnp.stack([fluxes[0], fluxes[1], -fluxes[2], -fluxes[3]])
    result = []
    for member in range(4):
        mixed_rows = jnp.dot(
            atmos_mixing, atmos_profiles[member], preferred_element_type=jnp.float32
        )
        result.append(mixed_rows + lowest[:, None] * tendency[member][None, :])
    return jnp.stack(result).astype(jnp.bfloat16)


def forcing_rows(fluxes):
    return couple_rate * jnp.stack(
        [
            fluxes[4] + fluxes[5] - fluxes[0] - fluxes[1],
            fluxes[1] - fluxes[6] - fluxes[7],
            fluxes[2],
            fluxes[3],
        ]
    )


def lane_gather_kernel(win_ref, lanes_ref, out_ref):
    lanes = lanes_ref[...]
    for field in range(win_ref.shape[0]):
        out_ref[field] = jnp.take_along_axis(
            win_ref[field], lanes, axis=1, mode="promise_in_bounds"
        )


def lane_gather(win, lanes):
    return pl.pallas_call(
        lane_gather_kernel,
        out_shape=jax.ShapeDtypeStruct(win.shape, win.dtype),
        in_specs=[pl.BlockSpec(memory_space=pltpu.VMEM)] * 2,
        out_specs=pl.BlockSpec(memory_space=pltpu.VMEM),
    )(win, lanes)


def split_kept(values):
    upper = lax.reduce_precision(values, exponent_bits=8, mantissa_bits=7)
    return upper.astype(jnp.bfloat16), (values - upper).astype(jnp.bfloat16)


def ocean_kernel(m_ref, m0_ref, x_ref, forcing_ref, sea_ref, out_ref):
    m = m_ref[...]
    m0 = m0_ref[...]
    sea = sea_ref[...] == 1
    for field in range(x_ref.shape[1]):
        x = x_ref[:, field, :]
        mixed = jnp.dot(m, x, precision=highest, preferred_element_type=jnp.float32)
        mixed = mixed + m0 * forcing_ref[field : field + 1, :]
        out_ref[:, field, :] = jnp.where(sea, mixed, x)


def ocean_update(ocean_mixing, state_by_level, forcing, sea_mask, block=1024):
    levels, fields, cells = state_by_level.shape
    return pl.pallas_call(
        ocean_kernel,
        grid=(cells // block,),
        out_shape=jax.ShapeDtypeStruct(state_by_level.shape, jnp.float32),
        in_specs=[
            pl.BlockSpec((levels, levels), lambda i: (0, 0)),
            pl.BlockSpec((levels, 1), lambda i: (0, 0)),
            pl.BlockSpec((levels, fields, block), lambda i: (0, 0, i)),
            pl.BlockSpec((fields, block), lambda i: (0, i)),
            pl.BlockSpec((1, block), lambda i: (0, i)),
        ],
        out_specs=pl.BlockSpec((levels, fields, block), lambda i: (0, 0, i)),
        cost_estimate=pl.CostEstimate(
            flops=12 * levels * levels * fields * cells,
            bytes_accessed=8 * levels * fields * cells,
            transcendentals=0,
        ),
    )(ocean_mixing, ocean_mixing[:, 0:1], state_by_level, forcing, sea_mask.reshape(1, cells))


def top_level_kernel(row_ref, x_ref, out_ref):
    total = row_ref[0] * x_ref[0]
    for level in range(1, x_ref.shape[0]):
        total = total + row_ref[level] * x_ref[level]
    out_ref[...] = total


def top_level_mix(first_row, state_by_level, block=2048):
    levels, fields, cells = state_by_level.shape
    return pl.pallas_call(
        top_level_kernel,
        grid=(cells // block,),
        out_shape=jax.ShapeDtypeStruct((fields, cells), jnp.float32),
        in_specs=[
            pl.BlockSpec(memory_space=pltpu.SMEM),
            pl.BlockSpec((levels, fields, block), lambda i: (0, 0, i)),
        ],
        out_specs=pl.BlockSpec((fields, block), lambda i: (0, i)),
        cost_estimate=pl.CostEstimate(
            flops=2 * levels * fields * cells,
            bytes_accessed=4 * (levels + 1) * fields * cells,
            transcendentals=0,
        ),
    )(first_row, state_by_level)


def lane_scatter_kernel(order_ref, keys_ref, last_ref, present_ref, val_ref, out_ref):
    order = order_ref[...]
    keys = keys_ref[...]
    last = last_ref[...]
    present = present_ref[...] > 0
    position = lax.broadcasted_iota(jnp.int32, keys.shape, 1)
    links = []
    shift = 1
    while shift < keys.shape[1]:
        joined = (position >= shift) & (pltpu.roll(keys, shift, 1) == keys)
        links.append((shift, joined))
        shift *= 2
    for field in range(val_ref.shape[0]):
        run = jnp.take_along_axis(val_ref[field], order, axis=1, mode="promise_in_bounds")
        for shift, joined in links:
            run = jnp.where(joined, run + pltpu.roll(run, shift, 1), run)
        picked = jnp.take_along_axis(run, last, axis=1, mode="promise_in_bounds")
        out_ref[field] = jnp.where(present, picked, 0.0)


def lane_scatter(values, order, keys, last, present):
    return pl.pallas_call(
        lane_scatter_kernel,
        out_shape=jax.ShapeDtypeStruct(values.shape, values.dtype),
        in_specs=[pl.BlockSpec(memory_space=pltpu.VMEM)] * 5,
        out_specs=pl.BlockSpec(memory_space=pltpu.VMEM),
    )(order, keys, last, present, values)


def lane_sort_kernel(key_ref, sorted_ref):
    values = key_ref[...]
    count = values.shape[1]
    position = lax.broadcasted_iota(jnp.int32, values.shape, 1)
    block = 2
    while block <= count:
        stride = block // 2
        while stride >= 1:
            lower = (position & stride) == 0
            partner = jnp.where(
                lower, pltpu.roll(values, count - stride, 1), pltpu.roll(values, stride, 1)
            )
            keep_min = lower == ((position & block) == 0)
            values = jnp.where(
                keep_min, jnp.minimum(values, partner), jnp.maximum(values, partner)
            )
            stride //= 2
        block *= 2
    sorted_ref[...] = values


def lane_sort(keys):
    return pl.pallas_call(
        lane_sort_kernel,
        out_shape=jax.ShapeDtypeStruct(keys.shape, keys.dtype),
        in_specs=[pl.BlockSpec(memory_space=pltpu.VMEM)],
        out_specs=pl.BlockSpec(memory_space=pltpu.VMEM),
    )(keys)


def per_device(
    atmos_profiles,
    atmos_mixing,
    drag_factor,
    surface_before,
    downward_fluxes,
    land_weight,
    land_surface,
    ocean_state,
    ocean_mixing,
    sea_mask,
    exchange_slot,
    parent_column,
    ocean_weight,
    atmos_weight,
):
    comp_count = lax.axis_size("comp")
    sub_count = lax.axis_size("sub")
    devices = comp_count * sub_count
    columns = atmos_profiles.shape[2]
    intersections = exchange_slot.shape[0]
    ocean_cells = exchange_slot.shape[1]
    capacity = 2 * intersections * ocean_cells // devices
    width = min(128, capacity)
    tile_count = intersections * ocean_cells // width
    slot_tiles = devices * capacity // width
    windows = columns // width
    tile_place = exchange_slot.reshape(tile_count, width)[:, 0] // width
    placement = (tile_place[None, :] == jnp.arange(slot_tiles, dtype=jnp.int32)[:, None]).astype(
        jnp.float32
    )
    tiles_pc = parent_column.reshape(tile_count, width)
    window_of_tile = tiles_pc[:, 0] // width
    lanes = tiles_pc % width

    state_by_level = jnp.transpose(ocean_state, (1, 0, 2))

    request = jnp.dot(placement, window_of_tile.astype(jnp.float32), precision=highest)
    request = (request + 0.5).astype(jnp.int32).reshape(devices, slot_tiles // devices)
    asked = lax.all_to_all(request, ("comp", "sub"), split_axis=0, concat_axis=0, tiled=True)
    asked = asked.reshape(slot_tiles)
    window_hot = (asked[:, None] == jnp.arange(windows, dtype=jnp.int32)[None, :]).astype(
        jnp.float32
    )

    fluxes = surface_fluxes(atmos_profiles, drag_factor, surface_before, downward_fluxes)
    column_forcing = forcing_rows(fluxes)
    served = jnp.einsum(
        "qw,fwl->qfl", window_hot, column_forcing.reshape(4, windows, width), precision=highest
    )
    late_lanes, late_state, served = lax.optimization_barrier((lanes, state_by_level, served))
    base_top = top_level_mix(ocean_mixing[0], late_state)
    ranked = lane_sort(late_lanes * width + lax.broadcasted_iota(jnp.int32, late_lanes.shape, 1))
    keys, order = ranked // width, ranked % width
    at_most = jnp.sum(
        (late_lanes[:, None, :] <= jnp.arange(width, dtype=jnp.int32)[None, :, None]).astype(jnp.int32),
        axis=2,
    )
    present = at_most - jnp.pad(at_most[:, :-1], ((0, 0), (1, 0)))
    last = jnp.maximum(at_most - 1, 0)
    arrived = lax.all_to_all(
        served.reshape(devices, -1), ("comp", "sub"), split_axis=0, concat_axis=0, tiled=True
    )
    win_local = jnp.einsum(
        "qt,qfl->ftl", placement, arrived.reshape(slot_tiles, 4, width), precision=highest
    )
    at_cells = lane_gather(win_local, lanes).reshape(4, intersections, ocean_cells)
    forcing = jnp.sum(ocean_weight[None] * at_cells, axis=1) / jnp.sum(ocean_weight, axis=0)[None]

    sea = sea_mask[None, :] == 1
    top = jnp.where(sea, base_top + ocean_mixing[0, 0] * forcing, state_by_level[0])
    sea_share = atmos_weight * sea_mask.astype(jnp.float32)[None, :]
    outgoing = jnp.concatenate([sea_share[None] * top[:, None, :], sea_share[None]], axis=0)
    partial = lane_scatter(outgoing.reshape(5, tile_count, width), order, keys, last, present)
    send_buffer = jnp.einsum("qt,ftc->qfc", placement, partial, precision=highest)
    late_profiles, send_buffer = lax.optimization_barrier((atmos_profiles, send_buffer))
    atmos_updated = diffuse_atmos(late_profiles, atmos_mixing, fluxes)
    returned = lax.all_to_all(
        send_buffer.reshape(devices, -1), ("comp", "sub"), split_axis=0, concat_axis=0, tiled=True
    )
    summed = jnp.einsum(
        "qw,qfc->fwc", window_hot, returned.reshape(slot_tiles, 5, width), precision=highest
    ).reshape(5, columns)
    updated_by_level = ocean_update(ocean_mixing, state_by_level, forcing, sea_mask)
    ocean_updated = jnp.transpose(updated_by_level, (1, 0, 2))
    surface_state = (summed[:4] + land_weight[None] * land_surface) / (summed[4] + land_weight)[
        None
    ]
    return (atmos_updated, ocean_updated, surface_state)


def solution(mesh):
    return jax.shard_map(
        per_device,
        mesh=mesh,
        in_specs=(
            P(None, None, ("comp", "sub")),
            P(),
            P(("comp", "sub")),
            P(None, ("comp", "sub")),
            P(None, ("comp", "sub")),
            P(("comp", "sub")),
            P(None, ("comp", "sub")),
            P(None, None, ("comp", "sub")),
            P(),
            P(("comp", "sub")),
            P(None, ("comp", "sub")),
            P(None, ("comp", "sub")),
            P(None, ("comp", "sub")),
            P(None, ("comp", "sub")),
        ),
        out_specs=(
            P(None, None, ("comp", "sub")),
            P(None, None, ("comp", "sub")),
            P(None, ("comp", "sub")),
        ),
        check_vma=False,
    )
```

```python
import jax
import jax.numpy as jnp
from jax import lax
from jax.experimental import pallas as pl
from jax.experimental.pallas import tpu as pltpu
from jax.sharding import PartitionSpec as P

couple_rate = 0.5
highest = lax.Precision.HIGHEST
high = lax.Precision.HIGH


def surface_fluxes(atmos_profiles, drag_factor, surface_before, downward_fluxes):
    bottom = atmos_profiles[:, -1, :].astype(jnp.float32)
    east_gap = bottom[2] - surface_before[2]
    north_gap = bottom[3] - surface_before[3]
    wind_speed = jnp.sqrt(1.0 + east_gap * east_gap + north_gap * north_gap)
    transfer = drag_factor * wind_speed
    sensible = transfer * (surface_before[0] - bottom[0])
    latent = transfer * (surface_before[1] - bottom[1])
    return jnp.stack(
        [
            sensible,
            latent,
            transfer * east_gap,
            transfer * north_gap,
            downward_fluxes[0],
            downward_fluxes[1],
            downward_fluxes[2],
            downward_fluxes[3],
        ]
    )


def atmos_kernel(mix_ref, low_ref, tend_ref, x_ref, out_ref):
    mix = mix_ref[...]
    low = low_ref[...]
    for member in range(x_ref.shape[0]):
        mixed = jnp.dot(mix, x_ref[member], preferred_element_type=jnp.float32)
        mixed = mixed + low * tend_ref[member : member + 1, :]
        out_ref[member] = mixed.astype(out_ref.dtype)


def diffuse_atmos(atmos_profiles, atmos_mixing, fluxes, block=2048):
    members, levels, columns = atmos_profiles.shape
    lowest = atmos_mixing[:, -1:].astype(jnp.float32)
    tendency = couple_rate * jnp.stack([fluxes[0], fluxes[1], -fluxes[2], -fluxes[3]])
    return pl.pallas_call(
        atmos_kernel,
        grid=(columns // block,),
        out_shape=jax.ShapeDtypeStruct(atmos_profiles.shape, jnp.bfloat16),
        in_specs=[
            pl.BlockSpec((levels, levels), lambda i: (0, 0)),
            pl.BlockSpec((levels, 1), lambda i: (0, 0)),
            pl.BlockSpec((members, block), lambda i: (0, i)),
            pl.BlockSpec((members, levels, block), lambda i: (0, 0, i)),
        ],
        out_specs=pl.BlockSpec((members, levels, block), lambda i: (0, 0, i)),
        cost_estimate=pl.CostEstimate(
            flops=2 * members * levels * levels * columns,
            bytes_accessed=4 * members * levels * columns,
            transcendentals=0,
        ),
    )(atmos_mixing, lowest, tendency, atmos_profiles)


def forcing_rows(fluxes):
    return couple_rate * jnp.stack(
        [
            fluxes[4] + fluxes[5] - fluxes[0] - fluxes[1],
            fluxes[1] - fluxes[6] - fluxes[7],
            fluxes[2],
            fluxes[3],
        ]
    )


def lane_gather_kernel(win_ref, lanes_ref, out_ref):
    lanes = lanes_ref[...]
    for field in range(win_ref.shape[0]):
        out_ref[field] = jnp.take_along_axis(
            win_ref[field], lanes, axis=1, mode="promise_in_bounds"
        )


def lane_gather(win, lanes):
    return pl.pallas_call(
        lane_gather_kernel,
        out_shape=jax.ShapeDtypeStruct(win.shape, win.dtype),
        in_specs=[pl.BlockSpec(memory_space=pltpu.VMEM)] * 2,
        out_specs=pl.BlockSpec(memory_space=pltpu.VMEM),
    )(win, lanes)


def split_kept(values):
    upper = lax.reduce_precision(values, exponent_bits=8, mantissa_bits=7)
    return upper.astype(jnp.bfloat16), (values - upper).astype(jnp.bfloat16)


def ocean_kernel(m_ref, m0_ref, x_ref, forcing_ref, sea_ref, out_ref):
    m = m_ref[...]
    m0 = m0_ref[...]
    sea = sea_ref[...] == 1
    for field in range(x_ref.shape[1]):
        x = x_ref[:, field, :]
        mixed = jnp.dot(m, x, precision=highest, preferred_element_type=jnp.float32)
        mixed = mixed + m0 * forcing_ref[field : field + 1, :]
        out_ref[:, field, :] = jnp.where(sea, mixed, x)


def ocean_update(ocean_mixing, state_by_level, forcing, sea_mask, block=1024):
    levels, fields, cells = state_by_level.shape
    return pl.pallas_call(
        ocean_kernel,
        grid=(cells // block,),
        out_shape=jax.ShapeDtypeStruct(state_by_level.shape, jnp.float32),
        in_specs=[
            pl.BlockSpec((levels, levels), lambda i: (0, 0)),
            pl.BlockSpec((levels, 1), lambda i: (0, 0)),
            pl.BlockSpec((levels, fields, block), lambda i: (0, 0, i)),
            pl.BlockSpec((fields, block), lambda i: (0, i)),
            pl.BlockSpec((1, block), lambda i: (0, i)),
        ],
        out_specs=pl.BlockSpec((levels, fields, block), lambda i: (0, 0, i)),
        cost_estimate=pl.CostEstimate(
            flops=12 * levels * levels * fields * cells,
            bytes_accessed=8 * levels * fields * cells,
            transcendentals=0,
        ),
    )(ocean_mixing, ocean_mixing[:, 0:1], state_by_level, forcing, sea_mask.reshape(1, cells))


def top_level_kernel(row_ref, x_ref, out_ref):
    total = row_ref[0] * x_ref[0]
    for level in range(1, x_ref.shape[0]):
        total = total + row_ref[level] * x_ref[level]
    out_ref[...] = total


def top_level_mix(first_row, state_by_level, block=2048):
    levels, fields, cells = state_by_level.shape
    return pl.pallas_call(
        top_level_kernel,
        grid=(cells // block,),
        out_shape=jax.ShapeDtypeStruct((fields, cells), jnp.float32),
        in_specs=[
            pl.BlockSpec(memory_space=pltpu.SMEM),
            pl.BlockSpec((levels, fields, block), lambda i: (0, 0, i)),
        ],
        out_specs=pl.BlockSpec((fields, block), lambda i: (0, i)),
        cost_estimate=pl.CostEstimate(
            flops=2 * levels * fields * cells,
            bytes_accessed=4 * (levels + 1) * fields * cells,
            transcendentals=0,
        ),
    )(first_row, state_by_level)


def lane_scatter_kernel(order_ref, keys_ref, last_ref, present_ref, val_ref, out_ref):
    order = order_ref[...]
    keys = keys_ref[...]
    last = last_ref[...]
    present = present_ref[...] > 0
    position = lax.broadcasted_iota(jnp.int32, keys.shape, 1)
    links = []
    shift = 1
    while shift < keys.shape[1]:
        joined = (position >= shift) & (pltpu.roll(keys, shift, 1) == keys)
        links.append((shift, joined))
        shift *= 2
    for field in range(val_ref.shape[0]):
        run = jnp.take_along_axis(val_ref[field], order, axis=1, mode="promise_in_bounds")
        for shift, joined in links:
            run = jnp.where(joined, run + pltpu.roll(run, shift, 1), run)
        picked = jnp.take_along_axis(run, last, axis=1, mode="promise_in_bounds")
        out_ref[field] = jnp.where(present, picked, 0.0)


def lane_scatter(values, order, keys, last, present):
    return pl.pallas_call(
        lane_scatter_kernel,
        out_shape=jax.ShapeDtypeStruct(values.shape, values.dtype),
        in_specs=[pl.BlockSpec(memory_space=pltpu.VMEM)] * 5,
        out_specs=pl.BlockSpec(memory_space=pltpu.VMEM),
    )(order, keys, last, present, values)


def lane_sort_kernel(key_ref, sorted_ref):
    values = key_ref[...]
    count = values.shape[1]
    position = lax.broadcasted_iota(jnp.int32, values.shape, 1)
    block = 2
    while block <= count:
        stride = block // 2
        while stride >= 1:
            lower = (position & stride) == 0
            partner = jnp.where(
                lower, pltpu.roll(values, count - stride, 1), pltpu.roll(values, stride, 1)
            )
            keep_min = lower == ((position & block) == 0)
            values = jnp.where(
                keep_min, jnp.minimum(values, partner), jnp.maximum(values, partner)
            )
            stride //= 2
        block *= 2
    sorted_ref[...] = values


def lane_sort(keys):
    return pl.pallas_call(
        lane_sort_kernel,
        out_shape=jax.ShapeDtypeStruct(keys.shape, keys.dtype),
        in_specs=[pl.BlockSpec(memory_space=pltpu.VMEM)],
        out_specs=pl.BlockSpec(memory_space=pltpu.VMEM),
    )(keys)


def per_device(
    atmos_profiles,
    atmos_mixing,
    drag_factor,
    surface_before,
    downward_fluxes,
    land_weight,
    land_surface,
    ocean_state,
    ocean_mixing,
    sea_mask,
    exchange_slot,
    parent_column,
    ocean_weight,
    atmos_weight,
):
    comp_count = lax.axis_size("comp")
    sub_count = lax.axis_size("sub")
    devices = comp_count * sub_count
    columns = atmos_profiles.shape[2]
    intersections = exchange_slot.shape[0]
    ocean_cells = exchange_slot.shape[1]
    capacity = 2 * intersections * ocean_cells // devices
    width = min(128, capacity)
    tile_count = intersections * ocean_cells // width
    slot_tiles = devices * capacity // width
    windows = columns // width
    tile_place = exchange_slot.reshape(tile_count, width)[:, 0] // width
    placement = (tile_place[None, :] == jnp.arange(slot_tiles, dtype=jnp.int32)[:, None]).astype(
        jnp.float32
    )
    tiles_pc = parent_column.reshape(tile_count, width)
    window_of_tile = tiles_pc[:, 0] // width
    lanes = tiles_pc % width

    state_by_level = jnp.transpose(ocean_state, (1, 0, 2))

    request = jnp.dot(placement, window_of_tile.astype(jnp.float32), precision=highest)
    request = (request + 0.5).astype(jnp.int32).reshape(devices, slot_tiles // devices)
    asked = lax.all_to_all(request, ("comp", "sub"), split_axis=0, concat_axis=0, tiled=True)
    asked = asked.reshape(slot_tiles)
    window_hot = (asked[:, None] == jnp.arange(windows, dtype=jnp.int32)[None, :]).astype(
        jnp.float32
    )

    fluxes = surface_fluxes(atmos_profiles, drag_factor, surface_before, downward_fluxes)
    column_forcing = forcing_rows(fluxes)
    served = jnp.einsum(
        "qw,fwl->qfl", window_hot, column_forcing.reshape(4, windows, width), precision=highest
    )
    late_lanes, late_state, served = lax.optimization_barrier((lanes, state_by_level, served))
    base_top = top_level_mix(ocean_mixing[0], late_state)
    ranked = lane_sort(late_lanes * width + lax.broadcasted_iota(jnp.int32, late_lanes.shape, 1))
    keys, order = ranked // width, ranked % width
    at_most = jnp.sum(
        (late_lanes[:, None, :] <= jnp.arange(width, dtype=jnp.int32)[None, :, None]).astype(jnp.int32),
        axis=2,
    )
    present = at_most - jnp.pad(at_most[:, :-1], ((0, 0), (1, 0)))
    last = jnp.maximum(at_most - 1, 0)
    arrived = lax.all_to_all(
        served.reshape(devices, -1), ("comp", "sub"), split_axis=0, concat_axis=0, tiled=True
    )
    win_local = jnp.einsum(
        "qt,qfl->ftl", placement, arrived.reshape(slot_tiles, 4, width), precision=highest
    )
    at_cells = lane_gather(win_local, lanes).reshape(4, intersections, ocean_cells)
    forcing = jnp.sum(ocean_weight[None] * at_cells, axis=1) / jnp.sum(ocean_weight, axis=0)[None]

    sea = sea_mask[None, :] == 1
    top = jnp.where(sea, base_top + ocean_mixing[0, 0] * forcing, state_by_level[0])
    sea_share = atmos_weight * sea_mask.astype(jnp.float32)[None, :]
    outgoing = jnp.concatenate([sea_share[None] * top[:, None, :], sea_share[None]], axis=0)
    partial = lane_scatter(outgoing.reshape(5, tile_count, width), order, keys, last, present)
    send_buffer = jnp.einsum("qt,ftc->qfc", placement, partial, precision=highest)
    late_profiles, send_buffer = lax.optimization_barrier((atmos_profiles, send_buffer))
    atmos_updated = diffuse_atmos(late_profiles, atmos_mixing, fluxes)
    returned = lax.all_to_all(
        send_buffer.reshape(devices, -1), ("comp", "sub"), split_axis=0, concat_axis=0, tiled=True
    )
    summed = jnp.einsum(
        "qw,qfc->fwc", window_hot, returned.reshape(slot_tiles, 5, width), precision=highest
    ).reshape(5, columns)
    updated_by_level = ocean_update(ocean_mixing, state_by_level, forcing, sea_mask)
    ocean_updated = jnp.transpose(updated_by_level, (1, 0, 2))
    surface_state = (summed[:4] + land_weight[None] * land_surface) / (summed[4] + land_weight)[
        None
    ]
    return (atmos_updated, ocean_updated, surface_state)


def solution(mesh):
    return jax.shard_map(
        per_device,
        mesh=mesh,
        in_specs=(
            P(None, None, ("comp", "sub")),
            P(),
            P(("comp", "sub")),
            P(None, ("comp", "sub")),
            P(None, ("comp", "sub")),
            P(("comp", "sub")),
            P(None, ("comp", "sub")),
            P(None, None, ("comp", "sub")),
            P(),
            P(("comp", "sub")),
            P(None, ("comp", "sub")),
            P(None, ("comp", "sub")),
            P(None, ("comp", "sub")),
            P(None, ("comp", "sub")),
        ),
        out_specs=(
            P(None, None, ("comp", "sub")),
            P(None, None, ("comp", "sub")),
            P(None, ("comp", "sub")),
        ),
        check_vma=False,
    )
```

```python
import jax
import jax.numpy as jnp
from jax import lax
from jax.experimental import pallas as pl
from jax.experimental.pallas import tpu as pltpu
from jax.sharding import PartitionSpec as P

couple_rate = 0.5
highest = lax.Precision.HIGHEST
high = lax.Precision.HIGH


def surface_fluxes(atmos_profiles, drag_factor, surface_before, downward_fluxes):
    bottom = atmos_profiles[:, -1, :].astype(jnp.float32)
    east_gap = bottom[2] - surface_before[2]
    north_gap = bottom[3] - surface_before[3]
    wind_speed = jnp.sqrt(1.0 + east_gap * east_gap + north_gap * north_gap)
    transfer = drag_factor * wind_speed
    sensible = transfer * (surface_before[0] - bottom[0])
    latent = transfer * (surface_before[1] - bottom[1])
    return jnp.stack(
        [
            sensible,
            latent,
            transfer * east_gap,
            transfer * north_gap,
            downward_fluxes[0],
            downward_fluxes[1],
            downward_fluxes[2],
            downward_fluxes[3],
        ]
    )


def atmos_kernel(mix_ref, low_ref, tend_ref, x_ref, out_ref):
    mix = mix_ref[...]
    low = low_ref[...]
    for member in range(x_ref.shape[0]):
        mixed = jnp.dot(mix, x_ref[member], preferred_element_type=jnp.float32)
        mixed = mixed + low * tend_ref[member : member + 1, :]
        out_ref[member] = mixed.astype(out_ref.dtype)


def diffuse_atmos(atmos_profiles, atmos_mixing, fluxes, block=2048):
    members, levels, columns = atmos_profiles.shape
    lowest = atmos_mixing[:, -1:].astype(jnp.float32)
    tendency = couple_rate * jnp.stack([fluxes[0], fluxes[1], -fluxes[2], -fluxes[3]])
    return pl.pallas_call(
        atmos_kernel,
        grid=(columns // block,),
        out_shape=jax.ShapeDtypeStruct(atmos_profiles.shape, jnp.bfloat16),
        in_specs=[
            pl.BlockSpec((levels, levels), lambda i: (0, 0)),
            pl.BlockSpec((levels, 1), lambda i: (0, 0)),
            pl.BlockSpec((members, block), lambda i: (0, i)),
            pl.BlockSpec((members, levels, block), lambda i: (0, 0, i)),
        ],
        out_specs=pl.BlockSpec((members, levels, block), lambda i: (0, 0, i)),
        cost_estimate=pl.CostEstimate(
            flops=2 * members * levels * levels * columns,
            bytes_accessed=4 * members * levels * columns,
            transcendentals=0,
        ),
    )(atmos_mixing, lowest, tendency, atmos_profiles)


def forcing_rows(fluxes):
    return couple_rate * jnp.stack(
        [
            fluxes[4] + fluxes[5] - fluxes[0] - fluxes[1],
            fluxes[1] - fluxes[6] - fluxes[7],
            fluxes[2],
            fluxes[3],
        ]
    )


def lane_gather_kernel(win_ref, lanes_ref, out_ref):
    lanes = lanes_ref[...]
    for field in range(win_ref.shape[0]):
        out_ref[field] = jnp.take_along_axis(
            win_ref[field], lanes, axis=1, mode="promise_in_bounds"
        )


def lane_gather(win, lanes):
    return pl.pallas_call(
        lane_gather_kernel,
        out_shape=jax.ShapeDtypeStruct(win.shape, win.dtype),
        in_specs=[pl.BlockSpec(memory_space=pltpu.VMEM)] * 2,
        out_specs=pl.BlockSpec(memory_space=pltpu.VMEM),
    )(win, lanes)


def split_kept(values):
    upper = lax.reduce_precision(values, exponent_bits=8, mantissa_bits=7)
    return upper.astype(jnp.bfloat16), (values - upper).astype(jnp.bfloat16)


def ocean_kernel(m_ref, m0_ref, x_ref, forcing_ref, sea_ref, out_ref):
    m = m_ref[...]
    m0 = m0_ref[...]
    sea = sea_ref[...] == 1
    for field in range(x_ref.shape[1]):
        x = x_ref[:, field, :]
        mixed = jnp.dot(m, x, precision=highest, preferred_element_type=jnp.float32)
        mixed = mixed + m0 * forcing_ref[field : field + 1, :]
        out_ref[:, field, :] = jnp.where(sea, mixed, x)


def ocean_update(ocean_mixing, state_by_level, forcing, sea_mask, block=1024):
    levels, fields, cells = state_by_level.shape
    return pl.pallas_call(
        ocean_kernel,
        grid=(cells // block,),
        out_shape=jax.ShapeDtypeStruct(state_by_level.shape, jnp.float32),
        in_specs=[
            pl.BlockSpec((levels, levels), lambda i: (0, 0)),
            pl.BlockSpec((levels, 1), lambda i: (0, 0)),
            pl.BlockSpec((levels, fields, block), lambda i: (0, 0, i)),
            pl.BlockSpec((fields, block), lambda i: (0, i)),
            pl.BlockSpec((1, block), lambda i: (0, i)),
        ],
        out_specs=pl.BlockSpec((levels, fields, block), lambda i: (0, 0, i)),
        cost_estimate=pl.CostEstimate(
            flops=12 * levels * levels * fields * cells,
            bytes_accessed=8 * levels * fields * cells,
            transcendentals=0,
        ),
    )(ocean_mixing, ocean_mixing[:, 0:1], state_by_level, forcing, sea_mask.reshape(1, cells))


def top_level_kernel(row_ref, x_ref, out_ref):
    total = row_ref[0] * x_ref[0]
    for level in range(1, x_ref.shape[0]):
        total = total + row_ref[level] * x_ref[level]
    out_ref[...] = total


def top_level_mix(first_row, state_by_level, block=2048):
    levels, fields, cells = state_by_level.shape
    return pl.pallas_call(
        top_level_kernel,
        grid=(cells // block,),
        out_shape=jax.ShapeDtypeStruct((fields, cells), jnp.float32),
        in_specs=[
            pl.BlockSpec(memory_space=pltpu.SMEM),
            pl.BlockSpec((levels, fields, block), lambda i: (0, 0, i)),
        ],
        out_specs=pl.BlockSpec((fields, block), lambda i: (0, i)),
        cost_estimate=pl.CostEstimate(
            flops=2 * levels * fields * cells,
            bytes_accessed=4 * (levels + 1) * fields * cells,
            transcendentals=0,
        ),
    )(first_row, state_by_level)


def lane_scatter_kernel(order_ref, keys_ref, last_ref, present_ref, val_ref, out_ref):
    order = order_ref[...]
    keys = keys_ref[...]
    last = last_ref[...]
    present = present_ref[...] > 0
    position = lax.broadcasted_iota(jnp.int32, keys.shape, 1)
    links = []
    shift = 1
    while shift < keys.shape[1]:
        joined = (position >= shift) & (pltpu.roll(keys, shift, 1) == keys)
        links.append((shift, joined))
        shift *= 2
    for field in range(val_ref.shape[0]):
        run = jnp.take_along_axis(val_ref[field], order, axis=1, mode="promise_in_bounds")
        for shift, joined in links:
            run = jnp.where(joined, run + pltpu.roll(run, shift, 1), run)
        picked = jnp.take_along_axis(run, last, axis=1, mode="promise_in_bounds")
        out_ref[field] = jnp.where(present, picked, 0.0)


def lane_scatter(values, order, keys, last, present):
    return pl.pallas_call(
        lane_scatter_kernel,
        out_shape=jax.ShapeDtypeStruct(values.shape, values.dtype),
        in_specs=[pl.BlockSpec(memory_space=pltpu.VMEM)] * 5,
        out_specs=pl.BlockSpec(memory_space=pltpu.VMEM),
    )(order, keys, last, present, values)


def lane_sort_kernel(key_ref, sorted_ref):
    values = key_ref[...]
    count = values.shape[1]
    position = lax.broadcasted_iota(jnp.int32, values.shape, 1)
    block = 2
    while block <= count:
        stride = block // 2
        while stride >= 1:
            lower = (position & stride) == 0
            partner = jnp.where(
                lower, pltpu.roll(values, count - stride, 1), pltpu.roll(values, stride, 1)
            )
            keep_min = lower == ((position & block) == 0)
            values = jnp.where(
                keep_min, jnp.minimum(values, partner), jnp.maximum(values, partner)
            )
            stride //= 2
        block *= 2
    sorted_ref[...] = values


def lane_sort(keys):
    return pl.pallas_call(
        lane_sort_kernel,
        out_shape=jax.ShapeDtypeStruct(keys.shape, keys.dtype),
        in_specs=[pl.BlockSpec(memory_space=pltpu.VMEM)],
        out_specs=pl.BlockSpec(memory_space=pltpu.VMEM),
    )(keys)


def return_prep_kernel(
    m00_ref, win_ref, lanes_ref, weight_ref, share_ref, base_ref, top0_ref, sea_ref,
    order_ref, keys_ref, last_ref, present_ref, partial_ref, forcing_ref,
):
    lanes = lanes_ref[...]
    parts = base_ref.shape[1]
    split = weight_ref.shape[0] // parts
    weight = weight_ref[...].reshape(split, parts, lanes.shape[1])
    total_weight = jnp.sum(weight, axis=0)
    share = share_ref[...]
    sea = sea_ref[...] == 1
    order = order_ref[...]
    keys = keys_ref[...]
    last = last_ref[...]
    present = present_ref[...] > 0
    position = lax.broadcasted_iota(jnp.int32, keys.shape, 1)
    links = []
    shift = 1
    while shift < keys.shape[1]:
        joined = (position >= shift) & (pltpu.roll(keys, shift, 1) == keys)
        links.append((shift, joined))
        shift *= 2

    def scatter(values):
        run = jnp.take_along_axis(values, order, axis=1, mode="promise_in_bounds")
        for step, joined in links:
            run = jnp.where(joined, run + pltpu.roll(run, step, 1), run)
        picked = jnp.take_along_axis(run, last, axis=1, mode="promise_in_bounds")
        return jnp.where(present, picked, 0.0)

    for field in range(win_ref.shape[0]):
        cells = jnp.take_along_axis(win_ref[field], lanes, axis=1, mode="promise_in_bounds")
        cells = cells.reshape(split, parts, lanes.shape[1])
        forcing = jnp.sum(weight * cells, axis=0) / total_weight
        forcing_ref[field] = forcing
        top = jnp.where(sea, base_ref[field] + m00_ref[0] * forcing, top0_ref[field])
        values = (share.reshape(split, parts, lanes.shape[1]) * top[None]).reshape(share.shape)
        partial_ref[field] = scatter(values)
    partial_ref[win_ref.shape[0]] = scatter(share)


def return_prep(m00, win, lanes, weight, share, base, top0, sea, order, keys, last, present):
    fields = win.shape[0]
    return pl.pallas_call(
        return_prep_kernel,
        out_shape=(
            jax.ShapeDtypeStruct((fields + 1,) + lanes.shape, jnp.float32),
            jax.ShapeDtypeStruct(base.shape, jnp.float32),
        ),
        in_specs=[pl.BlockSpec(memory_space=pltpu.SMEM)]
        + [pl.BlockSpec(memory_space=pltpu.VMEM)] * 11,
        out_specs=(
            pl.BlockSpec(memory_space=pltpu.VMEM),
            pl.BlockSpec(memory_space=pltpu.VMEM),
        ),
    )(m00, win, lanes, weight, share, base, top0, sea, order, keys, last, present)


def per_device(
    atmos_profiles,
    atmos_mixing,
    drag_factor,
    surface_before,
    downward_fluxes,
    land_weight,
    land_surface,
    ocean_state,
    ocean_mixing,
    sea_mask,
    exchange_slot,
    parent_column,
    ocean_weight,
    atmos_weight,
):
    comp_count = lax.axis_size("comp")
    sub_count = lax.axis_size("sub")
    devices = comp_count * sub_count
    columns = atmos_profiles.shape[2]
    intersections = exchange_slot.shape[0]
    ocean_cells = exchange_slot.shape[1]
    capacity = 2 * intersections * ocean_cells // devices
    width = min(128, capacity)
    tile_count = intersections * ocean_cells // width
    slot_tiles = devices * capacity // width
    windows = columns // width
    tile_place = exchange_slot.reshape(tile_count, width)[:, 0] // width
    placement = (tile_place[None, :] == jnp.arange(slot_tiles, dtype=jnp.int32)[:, None]).astype(
        jnp.float32
    )
    tiles_pc = parent_column.reshape(tile_count, width)
    window_of_tile = tiles_pc[:, 0] // width
    lanes = tiles_pc % width

    state_by_level = jnp.transpose(ocean_state, (1, 0, 2))

    request = jnp.dot(placement, window_of_tile.astype(jnp.float32), precision=highest)
    request = (request + 0.5).astype(jnp.int32).reshape(devices, slot_tiles // devices)
    asked = lax.all_to_all(request, ("comp", "sub"), split_axis=0, concat_axis=0, tiled=True)
    asked = asked.reshape(slot_tiles)
    window_hot = (asked[:, None] == jnp.arange(windows, dtype=jnp.int32)[None, :]).astype(
        jnp.float32
    )

    fluxes = surface_fluxes(atmos_profiles, drag_factor, surface_before, downward_fluxes)
    column_forcing = forcing_rows(fluxes)
    served = jnp.einsum(
        "qw,fwl->qfl", window_hot, column_forcing.reshape(4, windows, width), precision=highest
    )
    late_lanes, late_state, served = lax.optimization_barrier((lanes, state_by_level, served))
    base_top = top_level_mix(ocean_mixing[0], late_state)
    ranked = lane_sort(late_lanes * width + lax.broadcasted_iota(jnp.int32, late_lanes.shape, 1))
    keys, order = ranked // width, ranked % width
    at_most = jnp.sum(
        (late_lanes[:, None, :] <= jnp.arange(width, dtype=jnp.int32)[None, :, None]).astype(jnp.int32),
        axis=2,
    )
    present = at_most - jnp.pad(at_most[:, :-1], ((0, 0), (1, 0)))
    last = jnp.maximum(at_most - 1, 0)
    arrived = lax.all_to_all(
        served.reshape(devices, -1), ("comp", "sub"), split_axis=0, concat_axis=0, tiled=True
    )
    win_local = jnp.einsum(
        "qt,qfl->ftl", placement, arrived.reshape(slot_tiles, 4, width), precision=highest
    )
    parts = ocean_cells // width
    sea_share = atmos_weight * sea_mask.astype(jnp.float32)[None, :]
    partial, forcing = return_prep(
        ocean_mixing[0, 0:1],
        win_local,
        late_lanes,
        ocean_weight.reshape(tile_count, width),
        sea_share.reshape(tile_count, width),
        base_top.reshape(4, parts, width),
        late_state[0].reshape(4, parts, width),
        sea_mask.reshape(parts, width),
        order,
        keys,
        last,
        present,
    )
    forcing = forcing.reshape(4, ocean_cells)
    send_buffer = jnp.einsum("qt,ftc->qfc", placement, partial, precision=highest)
    late_profiles, send_buffer = lax.optimization_barrier((atmos_profiles, send_buffer))
    atmos_updated = diffuse_atmos(late_profiles, atmos_mixing, fluxes)
    returned = lax.all_to_all(
        send_buffer.reshape(devices, -1), ("comp", "sub"), split_axis=0, concat_axis=0, tiled=True
    )
    summed = jnp.einsum(
        "qw,qfc->fwc", window_hot, returned.reshape(slot_tiles, 5, width), precision=highest
    ).reshape(5, columns)
    updated_by_level = ocean_update(ocean_mixing, state_by_level, forcing, sea_mask)
    ocean_updated = jnp.transpose(updated_by_level, (1, 0, 2))
    surface_state = (summed[:4] + land_weight[None] * land_surface) / (summed[4] + land_weight)[
        None
    ]
    return (atmos_updated, ocean_updated, surface_state)


def solution(mesh):
    return jax.shard_map(
        per_device,
        mesh=mesh,
        in_specs=(
            P(None, None, ("comp", "sub")),
            P(),
            P(("comp", "sub")),
            P(None, ("comp", "sub")),
            P(None, ("comp", "sub")),
            P(("comp", "sub")),
            P(None, ("comp", "sub")),
            P(None, None, ("comp", "sub")),
            P(),
            P(("comp", "sub")),
            P(None, ("comp", "sub")),
            P(None, ("comp", "sub")),
            P(None, ("comp", "sub")),
            P(None, ("comp", "sub")),
        ),
        out_specs=(
            P(None, None, ("comp", "sub")),
            P(None, None, ("comp", "sub")),
            P(None, ("comp", "sub")),
        ),
        check_vma=False,
    )
```

```python
import jax
import jax.numpy as jnp
from jax import lax
from jax.experimental import pallas as pl
from jax.experimental.pallas import tpu as pltpu
from jax.sharding import PartitionSpec as P

couple_rate = 0.5
highest = lax.Precision.HIGHEST
high = lax.Precision.HIGH


def surface_fluxes(atmos_profiles, drag_factor, surface_before, downward_fluxes):
    bottom = atmos_profiles[:, -1, :].astype(jnp.float32)
    east_gap = bottom[2] - surface_before[2]
    north_gap = bottom[3] - surface_before[3]
    wind_speed = jnp.sqrt(1.0 + east_gap * east_gap + north_gap * north_gap)
    transfer = drag_factor * wind_speed
    sensible = transfer * (surface_before[0] - bottom[0])
    latent = transfer * (surface_before[1] - bottom[1])
    return jnp.stack(
        [
            sensible,
            latent,
            transfer * east_gap,
            transfer * north_gap,
            downward_fluxes[0],
            downward_fluxes[1],
            downward_fluxes[2],
            downward_fluxes[3],
        ]
    )


def atmos_kernel(mix_ref, low_ref, tend_ref, x_ref, out_ref):
    mix = mix_ref[...]
    low = low_ref[...]
    for member in range(x_ref.shape[0]):
        mixed = jnp.dot(mix, x_ref[member], preferred_element_type=jnp.float32)
        mixed = mixed + low * tend_ref[member : member + 1, :]
        out_ref[member] = mixed.astype(out_ref.dtype)


def diffuse_atmos(atmos_profiles, atmos_mixing, fluxes, block=2048):
    members, levels, columns = atmos_profiles.shape
    lowest = atmos_mixing[:, -1:].astype(jnp.float32)
    tendency = couple_rate * jnp.stack([fluxes[0], fluxes[1], -fluxes[2], -fluxes[3]])
    return pl.pallas_call(
        atmos_kernel,
        grid=(columns // block,),
        out_shape=jax.ShapeDtypeStruct(atmos_profiles.shape, jnp.bfloat16),
        in_specs=[
            pl.BlockSpec((levels, levels), lambda i: (0, 0)),
            pl.BlockSpec((levels, 1), lambda i: (0, 0)),
            pl.BlockSpec((members, block), lambda i: (0, i)),
            pl.BlockSpec((members, levels, block), lambda i: (0, 0, i)),
        ],
        out_specs=pl.BlockSpec((members, levels, block), lambda i: (0, 0, i)),
        cost_estimate=pl.CostEstimate(
            flops=2 * members * levels * levels * columns,
            bytes_accessed=4 * members * levels * columns,
            transcendentals=0,
        ),
    )(atmos_mixing, lowest, tendency, atmos_profiles)


def forcing_rows(fluxes):
    return couple_rate * jnp.stack(
        [
            fluxes[4] + fluxes[5] - fluxes[0] - fluxes[1],
            fluxes[1] - fluxes[6] - fluxes[7],
            fluxes[2],
            fluxes[3],
        ]
    )


def lane_gather_kernel(win_ref, lanes_ref, out_ref):
    lanes = lanes_ref[...]
    for field in range(win_ref.shape[0]):
        out_ref[field] = jnp.take_along_axis(
            win_ref[field], lanes, axis=1, mode="promise_in_bounds"
        )


def lane_gather(win, lanes):
    return pl.pallas_call(
        lane_gather_kernel,
        out_shape=jax.ShapeDtypeStruct(win.shape, win.dtype),
        in_specs=[pl.BlockSpec(memory_space=pltpu.VMEM)] * 2,
        out_specs=pl.BlockSpec(memory_space=pltpu.VMEM),
    )(win, lanes)


def split_kept(values):
    upper = lax.reduce_precision(values, exponent_bits=8, mantissa_bits=7)
    return upper.astype(jnp.bfloat16), (values - upper).astype(jnp.bfloat16)


def ocean_kernel(m_ref, m0_ref, x_ref, forcing_ref, sea_ref, out_ref):
    m = m_ref[...]
    m0 = m0_ref[...]
    sea = sea_ref[...] == 1
    for field in range(x_ref.shape[1]):
        x = x_ref[:, field, :]
        mixed = jnp.dot(m, x, precision=highest, preferred_element_type=jnp.float32)
        mixed = mixed + m0 * forcing_ref[field : field + 1, :]
        out_ref[:, field, :] = jnp.where(sea, mixed, x)


def ocean_update(ocean_mixing, state_by_level, forcing, sea_mask, block=2048):
    levels, fields, cells = state_by_level.shape
    return pl.pallas_call(
        ocean_kernel,
        grid=(cells // block,),
        out_shape=jax.ShapeDtypeStruct(state_by_level.shape, jnp.float32),
        in_specs=[
            pl.BlockSpec((levels, levels), lambda i: (0, 0)),
            pl.BlockSpec((levels, 1), lambda i: (0, 0)),
            pl.BlockSpec((levels, fields, block), lambda i: (0, 0, i)),
            pl.BlockSpec((fields, block), lambda i: (0, i)),
            pl.BlockSpec((1, block), lambda i: (0, i)),
        ],
        out_specs=pl.BlockSpec((levels, fields, block), lambda i: (0, 0, i)),
        cost_estimate=pl.CostEstimate(
            flops=12 * levels * levels * fields * cells,
            bytes_accessed=8 * levels * fields * cells,
            transcendentals=0,
        ),
    )(ocean_mixing, ocean_mixing[:, 0:1], state_by_level, forcing, sea_mask.reshape(1, cells))


def top_level_kernel(row_ref, x_ref, out_ref):
    total = row_ref[0] * x_ref[0]
    for level in range(1, x_ref.shape[0]):
        total = total + row_ref[level] * x_ref[level]
    out_ref[...] = total


def top_level_mix(first_row, state_by_level, block=4096):
    levels, fields, cells = state_by_level.shape
    return pl.pallas_call(
        top_level_kernel,
        grid=(cells // block,),
        out_shape=jax.ShapeDtypeStruct((fields, cells), jnp.float32),
        in_specs=[
            pl.BlockSpec(memory_space=pltpu.SMEM),
            pl.BlockSpec((levels, fields, block), lambda i: (0, 0, i)),
        ],
        out_specs=pl.BlockSpec((fields, block), lambda i: (0, i)),
        cost_estimate=pl.CostEstimate(
            flops=2 * levels * fields * cells,
            bytes_accessed=4 * (levels + 1) * fields * cells,
            transcendentals=0,
        ),
    )(first_row, state_by_level)


def lane_scatter_kernel(order_ref, keys_ref, last_ref, present_ref, val_ref, out_ref):
    order = order_ref[...]
    keys = keys_ref[...]
    last = last_ref[...]
    present = present_ref[...] > 0
    position = lax.broadcasted_iota(jnp.int32, keys.shape, 1)
    links = []
    shift = 1
    while shift < keys.shape[1]:
        joined = (position >= shift) & (pltpu.roll(keys, shift, 1) == keys)
        links.append((shift, joined))
        shift *= 2
    for field in range(val_ref.shape[0]):
        run = jnp.take_along_axis(val_ref[field], order, axis=1, mode="promise_in_bounds")
        for shift, joined in links:
            run = jnp.where(joined, run + pltpu.roll(run, shift, 1), run)
        picked = jnp.take_along_axis(run, last, axis=1, mode="promise_in_bounds")
        out_ref[field] = jnp.where(present, picked, 0.0)


def lane_scatter(values, order, keys, last, present):
    return pl.pallas_call(
        lane_scatter_kernel,
        out_shape=jax.ShapeDtypeStruct(values.shape, values.dtype),
        in_specs=[pl.BlockSpec(memory_space=pltpu.VMEM)] * 5,
        out_specs=pl.BlockSpec(memory_space=pltpu.VMEM),
    )(order, keys, last, present, values)


def lane_sort_kernel(key_ref, sorted_ref):
    values = key_ref[...]
    count = values.shape[1]
    position = lax.broadcasted_iota(jnp.int32, values.shape, 1)
    block = 2
    while block <= count:
        stride = block // 2
        while stride >= 1:
            lower = (position & stride) == 0
            partner = jnp.where(
                lower, pltpu.roll(values, count - stride, 1), pltpu.roll(values, stride, 1)
            )
            keep_min = lower == ((position & block) == 0)
            values = jnp.where(
                keep_min, jnp.minimum(values, partner), jnp.maximum(values, partner)
            )
            stride //= 2
        block *= 2
    sorted_ref[...] = values


def lane_sort(keys):
    return pl.pallas_call(
        lane_sort_kernel,
        out_shape=jax.ShapeDtypeStruct(keys.shape, keys.dtype),
        in_specs=[pl.BlockSpec(memory_space=pltpu.VMEM)],
        out_specs=pl.BlockSpec(memory_space=pltpu.VMEM),
    )(keys)


def return_prep_kernel(
    m00_ref, win_ref, lanes_ref, weight_ref, share_ref, base_ref, top0_ref, sea_ref,
    order_ref, keys_ref, last_ref, present_ref, partial_ref, forcing_ref,
):
    lanes = lanes_ref[...]
    parts = base_ref.shape[1]
    split = weight_ref.shape[0] // parts
    weight = weight_ref[...].reshape(split, parts, lanes.shape[1])
    total_weight = jnp.sum(weight, axis=0)
    share = share_ref[...]
    sea = sea_ref[...] == 1
    order = order_ref[...]
    keys = keys_ref[...]
    last = last_ref[...]
    present = present_ref[...] > 0
    position = lax.broadcasted_iota(jnp.int32, keys.shape, 1)
    links = []
    shift = 1
    while shift < keys.shape[1]:
        joined = (position >= shift) & (pltpu.roll(keys, shift, 1) == keys)
        links.append((shift, joined))
        shift *= 2

    def scatter(values):
        run = jnp.take_along_axis(values, order, axis=1, mode="promise_in_bounds")
        for step, joined in links:
            run = jnp.where(joined, run + pltpu.roll(run, step, 1), run)
        picked = jnp.take_along_axis(run, last, axis=1, mode="promise_in_bounds")
        return jnp.where(present, picked, 0.0)

    for field in range(win_ref.shape[0]):
        cells = jnp.take_along_axis(win_ref[field], lanes, axis=1, mode="promise_in_bounds")
        cells = cells.reshape(split, parts, lanes.shape[1])
        forcing = jnp.sum(weight * cells, axis=0) / total_weight
        forcing_ref[field] = forcing
        top = jnp.where(sea, base_ref[field] + m00_ref[0] * forcing, top0_ref[field])
        values = (share.reshape(split, parts, lanes.shape[1]) * top[None]).reshape(share.shape)
        partial_ref[field] = scatter(values)
    partial_ref[win_ref.shape[0]] = scatter(share)


def return_prep(m00, win, lanes, weight, share, base, top0, sea, order, keys, last, present):
    fields = win.shape[0]
    return pl.pallas_call(
        return_prep_kernel,
        out_shape=(
            jax.ShapeDtypeStruct((fields + 1,) + lanes.shape, jnp.float32),
            jax.ShapeDtypeStruct(base.shape, jnp.float32),
        ),
        in_specs=[pl.BlockSpec(memory_space=pltpu.SMEM)]
        + [pl.BlockSpec(memory_space=pltpu.VMEM)] * 11,
        out_specs=(
            pl.BlockSpec(memory_space=pltpu.VMEM),
            pl.BlockSpec(memory_space=pltpu.VMEM),
        ),
    )(m00, win, lanes, weight, share, base, top0, sea, order, keys, last, present)


def per_device(
    atmos_profiles,
    atmos_mixing,
    drag_factor,
    surface_before,
    downward_fluxes,
    land_weight,
    land_surface,
    ocean_state,
    ocean_mixing,
    sea_mask,
    exchange_slot,
    parent_column,
    ocean_weight,
    atmos_weight,
):
    comp_count = lax.axis_size("comp")
    sub_count = lax.axis_size("sub")
    devices = comp_count * sub_count
    columns = atmos_profiles.shape[2]
    intersections = exchange_slot.shape[0]
    ocean_cells = exchange_slot.shape[1]
    capacity = 2 * intersections * ocean_cells // devices
    width = min(128, capacity)
    tile_count = intersections * ocean_cells // width
    slot_tiles = devices * capacity // width
    windows = columns // width
    tile_place = exchange_slot.reshape(tile_count, width)[:, 0] // width
    placement = (tile_place[None, :] == jnp.arange(slot_tiles, dtype=jnp.int32)[:, None]).astype(
        jnp.float32
    )
    tiles_pc = parent_column.reshape(tile_count, width)
    window_of_tile = tiles_pc[:, 0] // width
    lanes = tiles_pc % width

    state_by_level = jnp.transpose(ocean_state, (1, 0, 2))

    request = jnp.dot(placement, window_of_tile.astype(jnp.float32), precision=highest)
    request = (request + 0.5).astype(jnp.int32).reshape(devices, slot_tiles // devices)
    asked = lax.all_to_all(request, ("comp", "sub"), split_axis=0, concat_axis=0, tiled=True)
    asked = asked.reshape(slot_tiles)
    window_hot = (asked[:, None] == jnp.arange(windows, dtype=jnp.int32)[None, :]).astype(
        jnp.float32
    )

    fluxes = surface_fluxes(atmos_profiles, drag_factor, surface_before, downward_fluxes)
    column_forcing = forcing_rows(fluxes)
    served = jnp.einsum(
        "qw,fwl->qfl", window_hot, column_forcing.reshape(4, windows, width), precision=highest
    )
    late_lanes, late_state, served = lax.optimization_barrier((lanes, state_by_level, served))
    base_top = top_level_mix(ocean_mixing[0], late_state)
    ranked = lane_sort(late_lanes * width + lax.broadcasted_iota(jnp.int32, late_lanes.shape, 1))
    keys, order = ranked // width, ranked % width
    at_most = jnp.sum(
        (late_lanes[:, None, :] <= jnp.arange(width, dtype=jnp.int32)[None, :, None]).astype(jnp.int32),
        axis=2,
    )
    present = at_most - jnp.pad(at_most[:, :-1], ((0, 0), (1, 0)))
    last = jnp.maximum(at_most - 1, 0)
    arrived = lax.all_to_all(
        served.reshape(devices, -1), ("comp", "sub"), split_axis=0, concat_axis=0, tiled=True
    )
    win_local = jnp.einsum(
        "qt,qfl->ftl", placement, arrived.reshape(slot_tiles, 4, width), precision=highest
    )
    parts = ocean_cells // width
    sea_share = atmos_weight * sea_mask.astype(jnp.float32)[None, :]
    partial, forcing = return_prep(
        ocean_mixing[0, 0:1],
        win_local,
        late_lanes,
        ocean_weight.reshape(tile_count, width),
        sea_share.reshape(tile_count, width),
        base_top.reshape(4, parts, width),
        late_state[0].reshape(4, parts, width),
        sea_mask.reshape(parts, width),
        order,
        keys,
        last,
        present,
    )
    forcing = forcing.reshape(4, ocean_cells)
    send_buffer = jnp.einsum("qt,ftc->qfc", placement, partial, precision=highest)
    late_profiles, send_buffer = lax.optimization_barrier((atmos_profiles, send_buffer))
    atmos_updated = diffuse_atmos(late_profiles, atmos_mixing, fluxes)
    returned = lax.all_to_all(
        send_buffer.reshape(devices, -1), ("comp", "sub"), split_axis=0, concat_axis=0, tiled=True
    )
    summed = jnp.einsum(
        "qw,qfc->fwc", window_hot, returned.reshape(slot_tiles, 5, width), precision=highest
    ).reshape(5, columns)
    updated_by_level = ocean_update(ocean_mixing, state_by_level, forcing, sea_mask)
    ocean_updated = jnp.transpose(updated_by_level, (1, 0, 2))
    surface_state = (summed[:4] + land_weight[None] * land_surface) / (summed[4] + land_weight)[
        None
    ]
    return (atmos_updated, ocean_updated, surface_state)


def solution(mesh):
    return jax.shard_map(
        per_device,
        mesh=mesh,
        in_specs=(
            P(None, None, ("comp", "sub")),
            P(),
            P(("comp", "sub")),
            P(None, ("comp", "sub")),
            P(None, ("comp", "sub")),
            P(("comp", "sub")),
            P(None, ("comp", "sub")),
            P(None, None, ("comp", "sub")),
            P(),
            P(("comp", "sub")),
            P(None, ("comp", "sub")),
            P(None, ("comp", "sub")),
            P(None, ("comp", "sub")),
            P(None, ("comp", "sub")),
        ),
        out_specs=(
            P(None, None, ("comp", "sub")),
            P(None, None, ("comp", "sub")),
            P(None, ("comp", "sub")),
        ),
        check_vma=False,
    )
```

```python
import jax
import jax.numpy as jnp
from jax import lax
from jax.experimental import pallas as pl
from jax.experimental.pallas import tpu as pltpu
from jax.sharding import PartitionSpec as P

couple_rate = 0.5
highest = lax.Precision.HIGHEST
high = lax.Precision.HIGH


def surface_fluxes(atmos_profiles, drag_factor, surface_before, downward_fluxes):
    bottom = atmos_profiles[:, -1, :].astype(jnp.float32)
    east_gap = bottom[2] - surface_before[2]
    north_gap = bottom[3] - surface_before[3]
    wind_speed = jnp.sqrt(1.0 + east_gap * east_gap + north_gap * north_gap)
    transfer = drag_factor * wind_speed
    sensible = transfer * (surface_before[0] - bottom[0])
    latent = transfer * (surface_before[1] - bottom[1])
    return jnp.stack(
        [
            sensible,
            latent,
            transfer * east_gap,
            transfer * north_gap,
            downward_fluxes[0],
            downward_fluxes[1],
            downward_fluxes[2],
            downward_fluxes[3],
        ]
    )


def atmos_kernel(mix_ref, low_ref, tend_ref, x_ref, out_ref):
    mix = mix_ref[...]
    low = low_ref[...]
    for member in range(x_ref.shape[0]):
        mixed = jnp.dot(mix, x_ref[member], preferred_element_type=jnp.float32)
        mixed = mixed + low * tend_ref[member : member + 1, :]
        out_ref[member] = mixed.astype(out_ref.dtype)


def diffuse_atmos(atmos_profiles, atmos_mixing, fluxes, block=2048):
    members, levels, columns = atmos_profiles.shape
    lowest = atmos_mixing[:, -1:].astype(jnp.float32)
    tendency = couple_rate * jnp.stack([fluxes[0], fluxes[1], -fluxes[2], -fluxes[3]])
    return pl.pallas_call(
        atmos_kernel,
        grid=(columns // block,),
        out_shape=jax.ShapeDtypeStruct(atmos_profiles.shape, jnp.bfloat16),
        in_specs=[
            pl.BlockSpec((levels, levels), lambda i: (0, 0)),
            pl.BlockSpec((levels, 1), lambda i: (0, 0)),
            pl.BlockSpec((members, block), lambda i: (0, i)),
            pl.BlockSpec((members, levels, block), lambda i: (0, 0, i)),
        ],
        out_specs=pl.BlockSpec((members, levels, block), lambda i: (0, 0, i)),
        cost_estimate=pl.CostEstimate(
            flops=2 * members * levels * levels * columns,
            bytes_accessed=4 * members * levels * columns,
            transcendentals=0,
        ),
    )(atmos_mixing, lowest, tendency, atmos_profiles)


def forcing_rows(fluxes):
    return couple_rate * jnp.stack(
        [
            fluxes[4] + fluxes[5] - fluxes[0] - fluxes[1],
            fluxes[1] - fluxes[6] - fluxes[7],
            fluxes[2],
            fluxes[3],
        ]
    )


def lane_gather_kernel(win_ref, lanes_ref, out_ref):
    lanes = lanes_ref[...]
    for field in range(win_ref.shape[0]):
        out_ref[field] = jnp.take_along_axis(
            win_ref[field], lanes, axis=1, mode="promise_in_bounds"
        )


def lane_gather(win, lanes):
    return pl.pallas_call(
        lane_gather_kernel,
        out_shape=jax.ShapeDtypeStruct(win.shape, win.dtype),
        in_specs=[pl.BlockSpec(memory_space=pltpu.VMEM)] * 2,
        out_specs=pl.BlockSpec(memory_space=pltpu.VMEM),
    )(win, lanes)


def split_kept(values):
    upper = lax.reduce_precision(values, exponent_bits=8, mantissa_bits=7)
    return upper.astype(jnp.bfloat16), (values - upper).astype(jnp.bfloat16)


def ocean_kernel(m_ref, m0_ref, x_ref, forcing_ref, sea_ref, out_ref):
    m = m_ref[...]
    m0 = m0_ref[...]
    sea = sea_ref[...] == 1
    for field in range(x_ref.shape[1]):
        x = x_ref[:, field, :]
        mixed = jnp.dot(m, x, precision=highest, preferred_element_type=jnp.float32)
        mixed = mixed + m0 * forcing_ref[field : field + 1, :]
        out_ref[:, field, :] = jnp.where(sea, mixed, x)


def ocean_update(ocean_mixing, state_by_level, forcing, sea_mask, block=2048):
    levels, fields, cells = state_by_level.shape
    return pl.pallas_call(
        ocean_kernel,
        grid=(cells // block,),
        out_shape=jax.ShapeDtypeStruct(state_by_level.shape, jnp.float32),
        in_specs=[
            pl.BlockSpec((levels, levels), lambda i: (0, 0)),
            pl.BlockSpec((levels, 1), lambda i: (0, 0)),
            pl.BlockSpec((levels, fields, block), lambda i: (0, 0, i)),
            pl.BlockSpec((fields, block), lambda i: (0, i)),
            pl.BlockSpec((1, block), lambda i: (0, i)),
        ],
        out_specs=pl.BlockSpec((levels, fields, block), lambda i: (0, 0, i)),
        cost_estimate=pl.CostEstimate(
            flops=12 * levels * levels * fields * cells,
            bytes_accessed=8 * levels * fields * cells,
            transcendentals=0,
        ),
    )(ocean_mixing, ocean_mixing[:, 0:1], state_by_level, forcing, sea_mask.reshape(1, cells))


def top_level_kernel(row_ref, x_ref, out_ref):
    total = row_ref[0] * x_ref[0]
    for level in range(1, x_ref.shape[0]):
        total = total + row_ref[level] * x_ref[level]
    out_ref[...] = total


def top_level_mix(first_row, state_by_level, block=4096):
    levels, fields, cells = state_by_level.shape
    return pl.pallas_call(
        top_level_kernel,
        grid=(cells // block,),
        out_shape=jax.ShapeDtypeStruct((fields, cells), jnp.float32),
        in_specs=[
            pl.BlockSpec(memory_space=pltpu.SMEM),
            pl.BlockSpec((levels, fields, block), lambda i: (0, 0, i)),
        ],
        out_specs=pl.BlockSpec((fields, block), lambda i: (0, i)),
        cost_estimate=pl.CostEstimate(
            flops=2 * levels * fields * cells,
            bytes_accessed=4 * (levels + 1) * fields * cells,
            transcendentals=0,
        ),
    )(first_row, state_by_level)


def lane_scatter_kernel(order_ref, keys_ref, last_ref, present_ref, val_ref, out_ref):
    order = order_ref[...]
    keys = keys_ref[...]
    last = last_ref[...]
    present = present_ref[...] > 0
    position = lax.broadcasted_iota(jnp.int32, keys.shape, 1)
    links = []
    shift = 1
    while shift < keys.shape[1]:
        joined = (position >= shift) & (pltpu.roll(keys, shift, 1) == keys)
        links.append((shift, joined))
        shift *= 2
    for field in range(val_ref.shape[0]):
        run = jnp.take_along_axis(val_ref[field], order, axis=1, mode="promise_in_bounds")
        for shift, joined in links:
            run = jnp.where(joined, run + pltpu.roll(run, shift, 1), run)
        picked = jnp.take_along_axis(run, last, axis=1, mode="promise_in_bounds")
        out_ref[field] = jnp.where(present, picked, 0.0)


def lane_scatter(values, order, keys, last, present):
    return pl.pallas_call(
        lane_scatter_kernel,
        out_shape=jax.ShapeDtypeStruct(values.shape, values.dtype),
        in_specs=[pl.BlockSpec(memory_space=pltpu.VMEM)] * 5,
        out_specs=pl.BlockSpec(memory_space=pltpu.VMEM),
    )(order, keys, last, present, values)


def lane_sort_kernel(key_ref, sorted_ref, present_ref, last_ref):
    values = key_ref[...]
    count = values.shape[1]
    position = lax.broadcasted_iota(jnp.int32, values.shape, 1)
    block = 2
    while block <= count:
        stride = block // 2
        while stride >= 1:
            lower = (position & stride) == 0
            partner = jnp.where(
                lower, pltpu.roll(values, count - stride, 1), pltpu.roll(values, stride, 1)
            )
            keep_min = lower == ((position & block) == 0)
            values = jnp.where(
                keep_min, jnp.minimum(values, partner), jnp.maximum(values, partner)
            )
            stride //= 2
        block *= 2
    sorted_ref[...] = values
    lanes = values // count
    below = jnp.zeros_like(position)
    step = count // 2
    while step >= 1:
        probe = jnp.take_along_axis(lanes, below + (step - 1), axis=1, mode="promise_in_bounds")
        below = jnp.where(probe <= position, below + step, below)
        step //= 2
    probe = jnp.take_along_axis(lanes, below, axis=1, mode="promise_in_bounds")
    below = jnp.where(probe <= position, below + 1, below)
    earlier = jnp.where(position >= 1, pltpu.roll(below, 1, 1), 0)
    present_ref[...] = below - earlier
    last_ref[...] = jnp.maximum(below - 1, 0)


def lane_sort(keys):
    return pl.pallas_call(
        lane_sort_kernel,
        out_shape=(jax.ShapeDtypeStruct(keys.shape, keys.dtype),) * 3,
        in_specs=[pl.BlockSpec(memory_space=pltpu.VMEM)],
        out_specs=(pl.BlockSpec(memory_space=pltpu.VMEM),) * 3,
    )(keys)


def return_prep_kernel(
    m00_ref, win_ref, lanes_ref, weight_ref, share_ref, base_ref, top0_ref, sea_ref,
    order_ref, keys_ref, last_ref, present_ref, partial_ref, forcing_ref,
):
    lanes = lanes_ref[...]
    parts = base_ref.shape[1]
    split = weight_ref.shape[0] // parts
    weight = weight_ref[...].reshape(split, parts, lanes.shape[1])
    total_weight = jnp.sum(weight, axis=0)
    share = share_ref[...]
    sea = sea_ref[...] == 1
    order = order_ref[...]
    keys = keys_ref[...]
    last = last_ref[...]
    present = present_ref[...] > 0
    position = lax.broadcasted_iota(jnp.int32, keys.shape, 1)
    links = []
    shift = 1
    while shift < keys.shape[1]:
        joined = (position >= shift) & (pltpu.roll(keys, shift, 1) == keys)
        links.append((shift, joined))
        shift *= 2

    def scatter(values):
        run = jnp.take_along_axis(values, order, axis=1, mode="promise_in_bounds")
        for step, joined in links:
            run = jnp.where(joined, run + pltpu.roll(run, step, 1), run)
        picked = jnp.take_along_axis(run, last, axis=1, mode="promise_in_bounds")
        return jnp.where(present, picked, 0.0)

    for field in range(win_ref.shape[0]):
        cells = jnp.take_along_axis(win_ref[field], lanes, axis=1, mode="promise_in_bounds")
        cells = cells.reshape(split, parts, lanes.shape[1])
        forcing = jnp.sum(weight * cells, axis=0) / total_weight
        forcing_ref[field] = forcing
        top = jnp.where(sea, base_ref[field] + m00_ref[0] * forcing, top0_ref[field])
        values = (share.reshape(split, parts, lanes.shape[1]) * top[None]).reshape(share.shape)
        partial_ref[field] = scatter(values)
    partial_ref[win_ref.shape[0]] = scatter(share)


def return_prep(m00, win, lanes, weight, share, base, top0, sea, order, keys, last, present):
    fields = win.shape[0]
    return pl.pallas_call(
        return_prep_kernel,
        out_shape=(
            jax.ShapeDtypeStruct((fields + 1,) + lanes.shape, jnp.float32),
            jax.ShapeDtypeStruct(base.shape, jnp.float32),
        ),
        in_specs=[pl.BlockSpec(memory_space=pltpu.SMEM)]
        + [pl.BlockSpec(memory_space=pltpu.VMEM)] * 11,
        out_specs=(
            pl.BlockSpec(memory_space=pltpu.VMEM),
            pl.BlockSpec(memory_space=pltpu.VMEM),
        ),
    )(m00, win, lanes, weight, share, base, top0, sea, order, keys, last, present)


def per_device(
    atmos_profiles,
    atmos_mixing,
    drag_factor,
    surface_before,
    downward_fluxes,
    land_weight,
    land_surface,
    ocean_state,
    ocean_mixing,
    sea_mask,
    exchange_slot,
    parent_column,
    ocean_weight,
    atmos_weight,
):
    comp_count = lax.axis_size("comp")
    sub_count = lax.axis_size("sub")
    devices = comp_count * sub_count
    columns = atmos_profiles.shape[2]
    intersections = exchange_slot.shape[0]
    ocean_cells = exchange_slot.shape[1]
    capacity = 2 * intersections * ocean_cells // devices
    width = min(128, capacity)
    tile_count = intersections * ocean_cells // width
    slot_tiles = devices * capacity // width
    windows = columns // width
    tile_place = exchange_slot.reshape(tile_count, width)[:, 0] // width
    placement = (tile_place[None, :] == jnp.arange(slot_tiles, dtype=jnp.int32)[:, None]).astype(
        jnp.float32
    )
    tiles_pc = parent_column.reshape(tile_count, width)
    window_of_tile = tiles_pc[:, 0] // width
    lanes = tiles_pc % width

    state_by_level = jnp.transpose(ocean_state, (1, 0, 2))

    request = jnp.dot(placement, window_of_tile.astype(jnp.float32), precision=highest)
    request = (request + 0.5).astype(jnp.int32).reshape(devices, slot_tiles // devices)
    asked = lax.all_to_all(request, ("comp", "sub"), split_axis=0, concat_axis=0, tiled=True)
    asked = asked.reshape(slot_tiles)
    window_hot = (asked[:, None] == jnp.arange(windows, dtype=jnp.int32)[None, :]).astype(
        jnp.float32
    )

    fluxes = surface_fluxes(atmos_profiles, drag_factor, surface_before, downward_fluxes)
    column_forcing = forcing_rows(fluxes)
    served = jnp.einsum(
        "qw,fwl->qfl", window_hot, column_forcing.reshape(4, windows, width), precision=highest
    )
    late_lanes, late_state, served = lax.optimization_barrier((lanes, state_by_level, served))
    base_top = top_level_mix(ocean_mixing[0], late_state)
    ranked, present, last = lane_sort(
        late_lanes * width + lax.broadcasted_iota(jnp.int32, late_lanes.shape, 1)
    )
    keys, order = ranked // width, ranked % width
    arrived = lax.all_to_all(
        served.reshape(devices, -1), ("comp", "sub"), split_axis=0, concat_axis=0, tiled=True
    )
    win_local = jnp.einsum(
        "qt,qfl->ftl", placement, arrived.reshape(slot_tiles, 4, width), precision=highest
    )
    parts = ocean_cells // width
    sea_share = atmos_weight * sea_mask.astype(jnp.float32)[None, :]
    partial, forcing = return_prep(
        ocean_mixing[0, 0:1],
        win_local,
        late_lanes,
        ocean_weight.reshape(tile_count, width),
        sea_share.reshape(tile_count, width),
        base_top.reshape(4, parts, width),
        late_state[0].reshape(4, parts, width),
        sea_mask.reshape(parts, width),
        order,
        keys,
        last,
        present,
    )
    forcing = forcing.reshape(4, ocean_cells)
    send_buffer = jnp.einsum("qt,ftc->qfc", placement, partial, precision=highest)
    late_profiles, send_buffer = lax.optimization_barrier((atmos_profiles, send_buffer))
    atmos_updated = diffuse_atmos(late_profiles, atmos_mixing, fluxes)
    returned = lax.all_to_all(
        send_buffer.reshape(devices, -1), ("comp", "sub"), split_axis=0, concat_axis=0, tiled=True
    )
    summed = jnp.einsum(
        "qw,qfc->fwc", window_hot, returned.reshape(slot_tiles, 5, width), precision=highest
    ).reshape(5, columns)
    updated_by_level = ocean_update(ocean_mixing, state_by_level, forcing, sea_mask)
    ocean_updated = jnp.transpose(updated_by_level, (1, 0, 2))
    surface_state = (summed[:4] + land_weight[None] * land_surface) / (summed[4] + land_weight)[
        None
    ]
    return (atmos_updated, ocean_updated, surface_state)


def solution(mesh):
    return jax.shard_map(
        per_device,
        mesh=mesh,
        in_specs=(
            P(None, None, ("comp", "sub")),
            P(),
            P(("comp", "sub")),
            P(None, ("comp", "sub")),
            P(None, ("comp", "sub")),
            P(("comp", "sub")),
            P(None, ("comp", "sub")),
            P(None, None, ("comp", "sub")),
            P(),
            P(("comp", "sub")),
            P(None, ("comp", "sub")),
            P(None, ("comp", "sub")),
            P(None, ("comp", "sub")),
            P(None, ("comp", "sub")),
        ),
        out_specs=(
            P(None, None, ("comp", "sub")),
            P(None, None, ("comp", "sub")),
            P(None, ("comp", "sub")),
        ),
        check_vma=False,
    )
```

```python
import jax
import jax.numpy as jnp
from jax import lax
from jax.experimental import pallas as pl
from jax.experimental.pallas import tpu as pltpu
from jax.sharding import PartitionSpec as P

couple_rate = 0.5
highest = lax.Precision.HIGHEST
high = lax.Precision.HIGH


def surface_fluxes(atmos_profiles, drag_factor, surface_before, downward_fluxes):
    bottom = atmos_profiles[:, -1, :].astype(jnp.float32)
    east_gap = bottom[2] - surface_before[2]
    north_gap = bottom[3] - surface_before[3]
    wind_speed = jnp.sqrt(1.0 + east_gap * east_gap + north_gap * north_gap)
    transfer = drag_factor * wind_speed
    sensible = transfer * (surface_before[0] - bottom[0])
    latent = transfer * (surface_before[1] - bottom[1])
    return jnp.stack(
        [
            sensible,
            latent,
            transfer * east_gap,
            transfer * north_gap,
            downward_fluxes[0],
            downward_fluxes[1],
            downward_fluxes[2],
            downward_fluxes[3],
        ]
    )


def atmos_kernel(mix_ref, low_ref, tend_ref, x_ref, out_ref):
    mix = mix_ref[...]
    low = low_ref[...]
    for member in range(x_ref.shape[0]):
        mixed = jnp.dot(mix, x_ref[member], preferred_element_type=jnp.float32)
        mixed = mixed + low * tend_ref[member : member + 1, :]
        out_ref[member] = mixed.astype(out_ref.dtype)


def diffuse_atmos(atmos_profiles, atmos_mixing, fluxes, block=4096):
    members, levels, columns = atmos_profiles.shape
    lowest = atmos_mixing[:, -1:].astype(jnp.float32)
    tendency = couple_rate * jnp.stack([fluxes[0], fluxes[1], -fluxes[2], -fluxes[3]])
    return pl.pallas_call(
        atmos_kernel,
        grid=(columns // block,),
        out_shape=jax.ShapeDtypeStruct(atmos_profiles.shape, jnp.bfloat16),
        in_specs=[
            pl.BlockSpec((levels, levels), lambda i: (0, 0)),
            pl.BlockSpec((levels, 1), lambda i: (0, 0)),
            pl.BlockSpec((members, block), lambda i: (0, i)),
            pl.BlockSpec((members, levels, block), lambda i: (0, 0, i)),
        ],
        out_specs=pl.BlockSpec((members, levels, block), lambda i: (0, 0, i)),
        cost_estimate=pl.CostEstimate(
            flops=2 * members * levels * levels * columns,
            bytes_accessed=4 * members * levels * columns,
            transcendentals=0,
        ),
    )(atmos_mixing, lowest, tendency, atmos_profiles)


def forcing_rows(fluxes):
    return couple_rate * jnp.stack(
        [
            fluxes[4] + fluxes[5] - fluxes[0] - fluxes[1],
            fluxes[1] - fluxes[6] - fluxes[7],
            fluxes[2],
            fluxes[3],
        ]
    )


def lane_gather_kernel(win_ref, lanes_ref, out_ref):
    lanes = lanes_ref[...]
    for field in range(win_ref.shape[0]):
        out_ref[field] = jnp.take_along_axis(
            win_ref[field], lanes, axis=1, mode="promise_in_bounds"
        )


def lane_gather(win, lanes):
    return pl.pallas_call(
        lane_gather_kernel,
        out_shape=jax.ShapeDtypeStruct(win.shape, win.dtype),
        in_specs=[pl.BlockSpec(memory_space=pltpu.VMEM)] * 2,
        out_specs=pl.BlockSpec(memory_space=pltpu.VMEM),
    )(win, lanes)


def split_kept(values):
    upper = lax.reduce_precision(values, exponent_bits=8, mantissa_bits=7)
    return upper.astype(jnp.bfloat16), (values - upper).astype(jnp.bfloat16)


def ocean_kernel(m_ref, m0_ref, x_ref, forcing_ref, sea_ref, out_ref):
    m = m_ref[...]
    m0 = m0_ref[...]
    sea = sea_ref[...] == 1
    for field in range(x_ref.shape[1]):
        x = x_ref[:, field, :]
        mixed = jnp.dot(m, x, precision=highest, preferred_element_type=jnp.float32)
        mixed = mixed + m0 * forcing_ref[field : field + 1, :]
        out_ref[:, field, :] = jnp.where(sea, mixed, x)


def ocean_update(ocean_mixing, state_by_level, forcing, sea_mask, block=4096):
    levels, fields, cells = state_by_level.shape
    return pl.pallas_call(
        ocean_kernel,
        grid=(cells // block,),
        out_shape=jax.ShapeDtypeStruct(state_by_level.shape, jnp.float32),
        in_specs=[
            pl.BlockSpec((levels, levels), lambda i: (0, 0)),
            pl.BlockSpec((levels, 1), lambda i: (0, 0)),
            pl.BlockSpec((levels, fields, block), lambda i: (0, 0, i)),
            pl.BlockSpec((fields, block), lambda i: (0, i)),
            pl.BlockSpec((1, block), lambda i: (0, i)),
        ],
        out_specs=pl.BlockSpec((levels, fields, block), lambda i: (0, 0, i)),
        cost_estimate=pl.CostEstimate(
            flops=12 * levels * levels * fields * cells,
            bytes_accessed=8 * levels * fields * cells,
            transcendentals=0,
        ),
    )(ocean_mixing, ocean_mixing[:, 0:1], state_by_level, forcing, sea_mask.reshape(1, cells))


def top_level_kernel(row_ref, x_ref, out_ref):
    total = row_ref[0] * x_ref[0]
    for level in range(1, x_ref.shape[0]):
        total = total + row_ref[level] * x_ref[level]
    out_ref[...] = total


def top_level_mix(first_row, state_by_level, block=4096):
    levels, fields, cells = state_by_level.shape
    return pl.pallas_call(
        top_level_kernel,
        grid=(cells // block,),
        out_shape=jax.ShapeDtypeStruct((fields, cells), jnp.float32),
        in_specs=[
            pl.BlockSpec(memory_space=pltpu.SMEM),
            pl.BlockSpec((levels, fields, block), lambda i: (0, 0, i)),
        ],
        out_specs=pl.BlockSpec((fields, block), lambda i: (0, i)),
        cost_estimate=pl.CostEstimate(
            flops=2 * levels * fields * cells,
            bytes_accessed=4 * (levels + 1) * fields * cells,
            transcendentals=0,
        ),
    )(first_row, state_by_level)


def lane_scatter_kernel(order_ref, keys_ref, last_ref, present_ref, val_ref, out_ref):
    order = order_ref[...]
    keys = keys_ref[...]
    last = last_ref[...]
    present = present_ref[...] > 0
    position = lax.broadcasted_iota(jnp.int32, keys.shape, 1)
    links = []
    shift = 1
    while shift < keys.shape[1]:
        joined = (position >= shift) & (pltpu.roll(keys, shift, 1) == keys)
        links.append((shift, joined))
        shift *= 2
    for field in range(val_ref.shape[0]):
        run = jnp.take_along_axis(val_ref[field], order, axis=1, mode="promise_in_bounds")
        for shift, joined in links:
            run = jnp.where(joined, run + pltpu.roll(run, shift, 1), run)
        picked = jnp.take_along_axis(run, last, axis=1, mode="promise_in_bounds")
        out_ref[field] = jnp.where(present, picked, 0.0)


def lane_scatter(values, order, keys, last, present):
    return pl.pallas_call(
        lane_scatter_kernel,
        out_shape=jax.ShapeDtypeStruct(values.shape, values.dtype),
        in_specs=[pl.BlockSpec(memory_space=pltpu.VMEM)] * 5,
        out_specs=pl.BlockSpec(memory_space=pltpu.VMEM),
    )(order, keys, last, present, values)


def lane_sort_kernel(key_ref, sorted_ref, present_ref, last_ref):
    values = key_ref[...]
    count = values.shape[1]
    position = lax.broadcasted_iota(jnp.int32, values.shape, 1)
    block = 2
    while block <= count:
        stride = block // 2
        while stride >= 1:
            lower = (position & stride) == 0
            partner = jnp.where(
                lower, pltpu.roll(values, count - stride, 1), pltpu.roll(values, stride, 1)
            )
            keep_min = lower == ((position & block) == 0)
            values = jnp.where(
                keep_min, jnp.minimum(values, partner), jnp.maximum(values, partner)
            )
            stride //= 2
        block *= 2
    sorted_ref[...] = values
    lanes = values // count
    below = jnp.zeros_like(position)
    step = count // 2
    while step >= 1:
        probe = jnp.take_along_axis(lanes, below + (step - 1), axis=1, mode="promise_in_bounds")
        below = jnp.where(probe <= position, below + step, below)
        step //= 2
    probe = jnp.take_along_axis(lanes, below, axis=1, mode="promise_in_bounds")
    below = jnp.where(probe <= position, below + 1, below)
    earlier = jnp.where(position >= 1, pltpu.roll(below, 1, 1), 0)
    present_ref[...] = below - earlier
    last_ref[...] = jnp.maximum(below - 1, 0)


def lane_sort(keys):
    return pl.pallas_call(
        lane_sort_kernel,
        out_shape=(jax.ShapeDtypeStruct(keys.shape, keys.dtype),) * 3,
        in_specs=[pl.BlockSpec(memory_space=pltpu.VMEM)],
        out_specs=(pl.BlockSpec(memory_space=pltpu.VMEM),) * 3,
    )(keys)


def return_prep_kernel(
    m00_ref, win_ref, lanes_ref, weight_ref, share_ref, base_ref, top0_ref, sea_ref,
    order_ref, keys_ref, last_ref, present_ref, partial_ref, forcing_ref,
):
    lanes = lanes_ref[...]
    parts = base_ref.shape[1]
    split = weight_ref.shape[0] // parts
    weight = weight_ref[...].reshape(split, parts, lanes.shape[1])
    total_weight = jnp.sum(weight, axis=0)
    share = share_ref[...]
    sea = sea_ref[...] == 1
    order = order_ref[...]
    keys = keys_ref[...]
    last = last_ref[...]
    present = present_ref[...] > 0
    position = lax.broadcasted_iota(jnp.int32, keys.shape, 1)
    links = []
    shift = 1
    while shift < keys.shape[1]:
        joined = (position >= shift) & (pltpu.roll(keys, shift, 1) == keys)
        links.append((shift, joined))
        shift *= 2

    def scatter(values):
        run = jnp.take_along_axis(values, order, axis=1, mode="promise_in_bounds")
        for step, joined in links:
            run = jnp.where(joined, run + pltpu.roll(run, step, 1), run)
        picked = jnp.take_along_axis(run, last, axis=1, mode="promise_in_bounds")
        return jnp.where(present, picked, 0.0)

    for field in range(win_ref.shape[0]):
        cells = jnp.take_along_axis(win_ref[field], lanes, axis=1, mode="promise_in_bounds")
        cells = cells.reshape(split, parts, lanes.shape[1])
        forcing = jnp.sum(weight * cells, axis=0) / total_weight
        forcing_ref[field] = forcing
        top = jnp.where(sea, base_ref[field] + m00_ref[0] * forcing, top0_ref[field])
        values = (share.reshape(split, parts, lanes.shape[1]) * top[None]).reshape(share.shape)
        partial_ref[field] = scatter(values)
    partial_ref[win_ref.shape[0]] = scatter(share)


def return_prep(m00, win, lanes, weight, share, base, top0, sea, order, keys, last, present):
    fields = win.shape[0]
    return pl.pallas_call(
        return_prep_kernel,
        out_shape=(
            jax.ShapeDtypeStruct((fields + 1,) + lanes.shape, jnp.float32),
            jax.ShapeDtypeStruct(base.shape, jnp.float32),
        ),
        in_specs=[pl.BlockSpec(memory_space=pltpu.SMEM)]
        + [pl.BlockSpec(memory_space=pltpu.VMEM)] * 11,
        out_specs=(
            pl.BlockSpec(memory_space=pltpu.VMEM),
            pl.BlockSpec(memory_space=pltpu.VMEM),
        ),
    )(m00, win, lanes, weight, share, base, top0, sea, order, keys, last, present)


def per_device(
    atmos_profiles,
    atmos_mixing,
    drag_factor,
    surface_before,
    downward_fluxes,
    land_weight,
    land_surface,
    ocean_state,
    ocean_mixing,
    sea_mask,
    exchange_slot,
    parent_column,
    ocean_weight,
    atmos_weight,
):
    comp_count = lax.axis_size("comp")
    sub_count = lax.axis_size("sub")
    devices = comp_count * sub_count
    columns = atmos_profiles.shape[2]
    intersections = exchange_slot.shape[0]
    ocean_cells = exchange_slot.shape[1]
    capacity = 2 * intersections * ocean_cells // devices
    width = min(128, capacity)
    tile_count = intersections * ocean_cells // width
    slot_tiles = devices * capacity // width
    windows = columns // width
    tile_place = exchange_slot.reshape(tile_count, width)[:, 0] // width
    placement = (tile_place[None, :] == jnp.arange(slot_tiles, dtype=jnp.int32)[:, None]).astype(
        jnp.float32
    )
    tiles_pc = parent_column.reshape(tile_count, width)
    window_of_tile = tiles_pc[:, 0] // width
    lanes = tiles_pc % width

    state_by_level = jnp.transpose(ocean_state, (1, 0, 2))

    request = jnp.dot(placement, window_of_tile.astype(jnp.float32), precision=highest)
    request = (request + 0.5).astype(jnp.int32).reshape(devices, slot_tiles // devices)
    asked = lax.all_to_all(request, ("comp", "sub"), split_axis=0, concat_axis=0, tiled=True)
    asked = asked.reshape(slot_tiles)
    window_hot = (asked[:, None] == jnp.arange(windows, dtype=jnp.int32)[None, :]).astype(
        jnp.float32
    )

    fluxes = surface_fluxes(atmos_profiles, drag_factor, surface_before, downward_fluxes)
    column_forcing = forcing_rows(fluxes)
    served = jnp.einsum(
        "qw,fwl->qfl", window_hot, column_forcing.reshape(4, windows, width), precision=highest
    )
    late_lanes, late_state, served = lax.optimization_barrier((lanes, state_by_level, served))
    base_top = top_level_mix(ocean_mixing[0], late_state)
    ranked, present, last = lane_sort(
        late_lanes * width + lax.broadcasted_iota(jnp.int32, late_lanes.shape, 1)
    )
    keys, order = ranked // width, ranked % width
    arrived = lax.all_to_all(
        served.reshape(devices, -1), ("comp", "sub"), split_axis=0, concat_axis=0, tiled=True
    )
    win_local = jnp.einsum(
        "qt,qfl->ftl", placement, arrived.reshape(slot_tiles, 4, width), precision=highest
    )
    parts = ocean_cells // width
    sea_share = atmos_weight * sea_mask.astype(jnp.float32)[None, :]
    partial, forcing = return_prep(
        ocean_mixing[0, 0:1],
        win_local,
        late_lanes,
        ocean_weight.reshape(tile_count, width),
        sea_share.reshape(tile_count, width),
        base_top.reshape(4, parts, width),
        late_state[0].reshape(4, parts, width),
        sea_mask.reshape(parts, width),
        order,
        keys,
        last,
        present,
    )
    forcing = forcing.reshape(4, ocean_cells)
    send_buffer = jnp.einsum("qt,ftc->qfc", placement, partial, precision=highest)
    late_profiles, send_buffer = lax.optimization_barrier((atmos_profiles, send_buffer))
    atmos_updated = diffuse_atmos(late_profiles, atmos_mixing, fluxes)
    returned = lax.all_to_all(
        send_buffer.reshape(devices, -1), ("comp", "sub"), split_axis=0, concat_axis=0, tiled=True
    )
    summed = jnp.einsum(
        "qw,qfc->fwc", window_hot, returned.reshape(slot_tiles, 5, width), precision=highest
    ).reshape(5, columns)
    updated_by_level = ocean_update(ocean_mixing, state_by_level, forcing, sea_mask)
    ocean_updated = jnp.transpose(updated_by_level, (1, 0, 2))
    surface_state = (summed[:4] + land_weight[None] * land_surface) / (summed[4] + land_weight)[
        None
    ]
    return (atmos_updated, ocean_updated, surface_state)


def solution(mesh):
    return jax.shard_map(
        per_device,
        mesh=mesh,
        in_specs=(
            P(None, None, ("comp", "sub")),
            P(),
            P(("comp", "sub")),
            P(None, ("comp", "sub")),
            P(None, ("comp", "sub")),
            P(("comp", "sub")),
            P(None, ("comp", "sub")),
            P(None, None, ("comp", "sub")),
            P(),
            P(("comp", "sub")),
            P(None, ("comp", "sub")),
            P(None, ("comp", "sub")),
            P(None, ("comp", "sub")),
            P(None, ("comp", "sub")),
        ),
        out_specs=(
            P(None, None, ("comp", "sub")),
            P(None, None, ("comp", "sub")),
            P(None, ("comp", "sub")),
        ),
        check_vma=False,
    )
```

```python
import jax
import jax.numpy as jnp
from jax import lax
from jax.experimental import pallas as pl
from jax.experimental.pallas import tpu as pltpu
from jax.sharding import PartitionSpec as P

couple_rate = 0.5
highest = lax.Precision.HIGHEST
high = lax.Precision.HIGH


def surface_fluxes(atmos_profiles, drag_factor, surface_before, downward_fluxes):
    bottom = atmos_profiles[:, -1, :].astype(jnp.float32)
    east_gap = bottom[2] - surface_before[2]
    north_gap = bottom[3] - surface_before[3]
    wind_speed = jnp.sqrt(1.0 + east_gap * east_gap + north_gap * north_gap)
    transfer = drag_factor * wind_speed
    sensible = transfer * (surface_before[0] - bottom[0])
    latent = transfer * (surface_before[1] - bottom[1])
    return jnp.stack(
        [
            sensible,
            latent,
            transfer * east_gap,
            transfer * north_gap,
            downward_fluxes[0],
            downward_fluxes[1],
            downward_fluxes[2],
            downward_fluxes[3],
        ]
    )


def atmos_kernel(mix_ref, low_ref, tend_ref, x_ref, out_ref):
    mix = mix_ref[...]
    low = low_ref[...]
    for member in range(x_ref.shape[0]):
        mixed = jnp.dot(mix, x_ref[member], preferred_element_type=jnp.float32)
        mixed = mixed + low * tend_ref[member : member + 1, :]
        out_ref[member] = mixed.astype(out_ref.dtype)


def diffuse_atmos(atmos_profiles, atmos_mixing, fluxes, block=2048):
    members, levels, columns = atmos_profiles.shape
    lowest = atmos_mixing[:, -1:].astype(jnp.float32)
    tendency = couple_rate * jnp.stack([fluxes[0], fluxes[1], -fluxes[2], -fluxes[3]])
    return pl.pallas_call(
        atmos_kernel,
        grid=(columns // block,),
        out_shape=jax.ShapeDtypeStruct(atmos_profiles.shape, jnp.bfloat16),
        in_specs=[
            pl.BlockSpec((levels, levels), lambda i: (0, 0)),
            pl.BlockSpec((levels, 1), lambda i: (0, 0)),
            pl.BlockSpec((members, block), lambda i: (0, i)),
            pl.BlockSpec((members, levels, block), lambda i: (0, 0, i)),
        ],
        out_specs=pl.BlockSpec((members, levels, block), lambda i: (0, 0, i)),
        cost_estimate=pl.CostEstimate(
            flops=2 * members * levels * levels * columns,
            bytes_accessed=4 * members * levels * columns,
            transcendentals=0,
        ),
    )(atmos_mixing, lowest, tendency, atmos_profiles)


def forcing_rows(fluxes):
    return couple_rate * jnp.stack(
        [
            fluxes[4] + fluxes[5] - fluxes[0] - fluxes[1],
            fluxes[1] - fluxes[6] - fluxes[7],
            fluxes[2],
            fluxes[3],
        ]
    )


def lane_gather_kernel(win_ref, lanes_ref, out_ref):
    lanes = lanes_ref[...]
    for field in range(win_ref.shape[0]):
        out_ref[field] = jnp.take_along_axis(
            win_ref[field], lanes, axis=1, mode="promise_in_bounds"
        )


def lane_gather(win, lanes):
    return pl.pallas_call(
        lane_gather_kernel,
        out_shape=jax.ShapeDtypeStruct(win.shape, win.dtype),
        in_specs=[pl.BlockSpec(memory_space=pltpu.VMEM)] * 2,
        out_specs=pl.BlockSpec(memory_space=pltpu.VMEM),
    )(win, lanes)


def split_kept(values):
    upper = lax.reduce_precision(values, exponent_bits=8, mantissa_bits=7)
    return upper.astype(jnp.bfloat16), (values - upper).astype(jnp.bfloat16)


def ocean_kernel(m_ref, m0_ref, x_ref, forcing_ref, sea_ref, out_ref):
    m = m_ref[...]
    m0 = m0_ref[...]
    sea = sea_ref[...] == 1
    for field in range(x_ref.shape[1]):
        x = x_ref[:, field, :]
        mixed = jnp.dot(m, x, precision=highest, preferred_element_type=jnp.float32)
        mixed = mixed + m0 * forcing_ref[field : field + 1, :]
        out_ref[:, field, :] = jnp.where(sea, mixed, x)


def ocean_update(ocean_mixing, state_by_level, forcing, sea_mask, block=2048):
    levels, fields, cells = state_by_level.shape
    return pl.pallas_call(
        ocean_kernel,
        grid=(cells // block,),
        out_shape=jax.ShapeDtypeStruct(state_by_level.shape, jnp.float32),
        in_specs=[
            pl.BlockSpec((levels, levels), lambda i: (0, 0)),
            pl.BlockSpec((levels, 1), lambda i: (0, 0)),
            pl.BlockSpec((levels, fields, block), lambda i: (0, 0, i)),
            pl.BlockSpec((fields, block), lambda i: (0, i)),
            pl.BlockSpec((1, block), lambda i: (0, i)),
        ],
        out_specs=pl.BlockSpec((levels, fields, block), lambda i: (0, 0, i)),
        cost_estimate=pl.CostEstimate(
            flops=12 * levels * levels * fields * cells,
            bytes_accessed=8 * levels * fields * cells,
            transcendentals=0,
        ),
    )(ocean_mixing, ocean_mixing[:, 0:1], state_by_level, forcing, sea_mask.reshape(1, cells))


def top_level_kernel(row_ref, x_ref, out_ref):
    total = row_ref[0] * x_ref[0]
    for level in range(1, x_ref.shape[0]):
        total = total + row_ref[level] * x_ref[level]
    out_ref[...] = total


def top_level_mix(first_row, state_by_level, block=4096):
    levels, fields, cells = state_by_level.shape
    return pl.pallas_call(
        top_level_kernel,
        grid=(cells // block,),
        out_shape=jax.ShapeDtypeStruct((fields, cells), jnp.float32),
        in_specs=[
            pl.BlockSpec(memory_space=pltpu.SMEM),
            pl.BlockSpec((levels, fields, block), lambda i: (0, 0, i)),
        ],
        out_specs=pl.BlockSpec((fields, block), lambda i: (0, i)),
        cost_estimate=pl.CostEstimate(
            flops=2 * levels * fields * cells,
            bytes_accessed=4 * (levels + 1) * fields * cells,
            transcendentals=0,
        ),
    )(first_row, state_by_level)


def lane_scatter_kernel(order_ref, keys_ref, last_ref, present_ref, val_ref, out_ref):
    order = order_ref[...]
    keys = keys_ref[...]
    last = last_ref[...]
    present = present_ref[...] > 0
    position = lax.broadcasted_iota(jnp.int32, keys.shape, 1)
    links = []
    shift = 1
    while shift < keys.shape[1]:
        joined = (position >= shift) & (pltpu.roll(keys, shift, 1) == keys)
        links.append((shift, joined))
        shift *= 2
    for field in range(val_ref.shape[0]):
        run = jnp.take_along_axis(val_ref[field], order, axis=1, mode="promise_in_bounds")
        for shift, joined in links:
            run = jnp.where(joined, run + pltpu.roll(run, shift, 1), run)
        picked = jnp.take_along_axis(run, last, axis=1, mode="promise_in_bounds")
        out_ref[field] = jnp.where(present, picked, 0.0)


def lane_scatter(values, order, keys, last, present):
    return pl.pallas_call(
        lane_scatter_kernel,
        out_shape=jax.ShapeDtypeStruct(values.shape, values.dtype),
        in_specs=[pl.BlockSpec(memory_space=pltpu.VMEM)] * 5,
        out_specs=pl.BlockSpec(memory_space=pltpu.VMEM),
    )(order, keys, last, present, values)


def lane_sort_kernel(key_ref, sorted_ref, present_ref, last_ref):
    values = key_ref[...]
    count = values.shape[1]
    position = lax.broadcasted_iota(jnp.int32, values.shape, 1)
    block = 2
    while block <= count:
        stride = block // 2
        while stride >= 1:
            lower = (position & stride) == 0
            partner = jnp.where(
                lower, pltpu.roll(values, count - stride, 1), pltpu.roll(values, stride, 1)
            )
            keep_min = lower == ((position & block) == 0)
            values = jnp.where(
                keep_min, jnp.minimum(values, partner), jnp.maximum(values, partner)
            )
            stride //= 2
        block *= 2
    sorted_ref[...] = values
    lanes = values // count
    below = jnp.zeros_like(position)
    step = count // 2
    while step >= 1:
        probe = jnp.take_along_axis(lanes, below + (step - 1), axis=1, mode="promise_in_bounds")
        below = jnp.where(probe <= position, below + step, below)
        step //= 2
    probe = jnp.take_along_axis(lanes, below, axis=1, mode="promise_in_bounds")
    below = jnp.where(probe <= position, below + 1, below)
    earlier = jnp.where(position >= 1, pltpu.roll(below, 1, 1), 0)
    present_ref[...] = below - earlier
    last_ref[...] = jnp.maximum(below - 1, 0)


def lane_sort(keys):
    return pl.pallas_call(
        lane_sort_kernel,
        out_shape=(jax.ShapeDtypeStruct(keys.shape, keys.dtype),) * 3,
        in_specs=[pl.BlockSpec(memory_space=pltpu.VMEM)],
        out_specs=(pl.BlockSpec(memory_space=pltpu.VMEM),) * 3,
    )(keys)


def return_prep_kernel(
    m00_ref, win_ref, lanes_ref, weight_ref, share_ref, base_ref, top0_ref, sea_ref,
    order_ref, keys_ref, last_ref, present_ref, partial_ref, forcing_ref,
):
    lanes = lanes_ref[...]
    parts = base_ref.shape[1]
    split = weight_ref.shape[0] // parts
    weight = weight_ref[...].reshape(split, parts, lanes.shape[1])
    total_weight = jnp.sum(weight, axis=0)
    share = share_ref[...]
    sea = sea_ref[...] == 1
    order = order_ref[...]
    keys = keys_ref[...]
    last = last_ref[...]
    present = present_ref[...] > 0
    position = lax.broadcasted_iota(jnp.int32, keys.shape, 1)
    links = []
    shift = 1
    while shift < keys.shape[1]:
        joined = (position >= shift) & (pltpu.roll(keys, shift, 1) == keys)
        links.append((shift, joined))
        shift *= 2

    def scatter(values):
        run = jnp.take_along_axis(values, order, axis=1, mode="promise_in_bounds")
        for step, joined in links:
            run = jnp.where(joined, run + pltpu.roll(run, step, 1), run)
        picked = jnp.take_along_axis(run, last, axis=1, mode="promise_in_bounds")
        return jnp.where(present, picked, 0.0)

    for field in range(win_ref.shape[0]):
        cells = jnp.take_along_axis(win_ref[field], lanes, axis=1, mode="promise_in_bounds")
        cells = cells.reshape(split, parts, lanes.shape[1])
        forcing = jnp.sum(weight * cells, axis=0) / total_weight
        forcing_ref[field] = forcing
        top = jnp.where(sea, base_ref[field] + m00_ref[0] * forcing, top0_ref[field])
        values = (share.reshape(split, parts, lanes.shape[1]) * top[None]).reshape(share.shape)
        partial_ref[field] = scatter(values)
    partial_ref[win_ref.shape[0]] = scatter(share)


def return_prep(m00, win, lanes, weight, share, base, top0, sea, order, keys, last, present):
    fields = win.shape[0]
    return pl.pallas_call(
        return_prep_kernel,
        out_shape=(
            jax.ShapeDtypeStruct((fields + 1,) + lanes.shape, jnp.float32),
            jax.ShapeDtypeStruct(base.shape, jnp.float32),
        ),
        in_specs=[pl.BlockSpec(memory_space=pltpu.SMEM)]
        + [pl.BlockSpec(memory_space=pltpu.VMEM)] * 11,
        out_specs=(
            pl.BlockSpec(memory_space=pltpu.VMEM),
            pl.BlockSpec(memory_space=pltpu.VMEM),
        ),
    )(m00, win, lanes, weight, share, base, top0, sea, order, keys, last, present)


def per_device(
    atmos_profiles,
    atmos_mixing,
    drag_factor,
    surface_before,
    downward_fluxes,
    land_weight,
    land_surface,
    ocean_state,
    ocean_mixing,
    sea_mask,
    exchange_slot,
    parent_column,
    ocean_weight,
    atmos_weight,
):
    comp_count = lax.axis_size("comp")
    sub_count = lax.axis_size("sub")
    devices = comp_count * sub_count
    columns = atmos_profiles.shape[2]
    intersections = exchange_slot.shape[0]
    ocean_cells = exchange_slot.shape[1]
    capacity = 2 * intersections * ocean_cells // devices
    width = min(128, capacity)
    tile_count = intersections * ocean_cells // width
    slot_tiles = devices * capacity // width
    windows = columns // width
    tile_place = exchange_slot.reshape(tile_count, width)[:, 0] // width
    placement = (tile_place[None, :] == jnp.arange(slot_tiles, dtype=jnp.int32)[:, None]).astype(
        jnp.float32
    )
    tiles_pc = parent_column.reshape(tile_count, width)
    window_of_tile = tiles_pc[:, 0] // width
    lanes = tiles_pc % width

    state_by_level = jnp.transpose(ocean_state, (1, 0, 2))

    request = jnp.dot(placement, window_of_tile.astype(jnp.float32), precision=highest)
    request = (request + 0.5).astype(jnp.int32).reshape(devices, slot_tiles // devices)
    asked = lax.all_to_all(request, ("comp", "sub"), split_axis=0, concat_axis=0, tiled=True)
    asked = asked.reshape(slot_tiles)
    window_hot = (asked[:, None] == jnp.arange(windows, dtype=jnp.int32)[None, :]).astype(
        jnp.float32
    )

    fluxes = surface_fluxes(atmos_profiles, drag_factor, surface_before, downward_fluxes)
    column_forcing = forcing_rows(fluxes)
    served = jnp.einsum(
        "qw,fwl->qfl", window_hot, column_forcing.reshape(4, windows, width), precision=highest
    )
    late_lanes, late_state, served = lax.optimization_barrier((lanes, state_by_level, served))
    base_top = top_level_mix(ocean_mixing[0], late_state)
    ranked, present, last = lane_sort(
        late_lanes * width + lax.broadcasted_iota(jnp.int32, late_lanes.shape, 1)
    )
    keys, order = ranked // width, ranked % width
    arrived = lax.all_to_all(
        served.reshape(devices, -1, width), ("comp", "sub"), split_axis=0, concat_axis=0, tiled=True
    )
    win_local = jnp.einsum(
        "qt,qfl->ftl", placement, arrived.reshape(slot_tiles, 4, width), precision=highest
    )
    parts = ocean_cells // width
    sea_share = atmos_weight * sea_mask.astype(jnp.float32)[None, :]
    partial, forcing = return_prep(
        ocean_mixing[0, 0:1],
        win_local,
        late_lanes,
        ocean_weight.reshape(tile_count, width),
        sea_share.reshape(tile_count, width),
        base_top.reshape(4, parts, width),
        late_state[0].reshape(4, parts, width),
        sea_mask.reshape(parts, width),
        order,
        keys,
        last,
        present,
    )
    forcing = forcing.reshape(4, ocean_cells)
    send_buffer = jnp.einsum("qt,ftc->qfc", placement, partial, precision=highest)
    late_profiles, send_buffer = lax.optimization_barrier((atmos_profiles, send_buffer))
    atmos_updated = diffuse_atmos(late_profiles, atmos_mixing, fluxes)
    returned = lax.all_to_all(
        send_buffer.reshape(devices, -1, width), ("comp", "sub"), split_axis=0, concat_axis=0, tiled=True
    )
    summed = jnp.einsum(
        "qw,qfc->fwc", window_hot, returned.reshape(slot_tiles, 5, width), precision=highest
    ).reshape(5, columns)
    updated_by_level = ocean_update(ocean_mixing, state_by_level, forcing, sea_mask)
    ocean_updated = jnp.transpose(updated_by_level, (1, 0, 2))
    surface_state = (summed[:4] + land_weight[None] * land_surface) / (summed[4] + land_weight)[
        None
    ]
    return (atmos_updated, ocean_updated, surface_state)


def solution(mesh):
    return jax.shard_map(
        per_device,
        mesh=mesh,
        in_specs=(
            P(None, None, ("comp", "sub")),
            P(),
            P(("comp", "sub")),
            P(None, ("comp", "sub")),
            P(None, ("comp", "sub")),
            P(("comp", "sub")),
            P(None, ("comp", "sub")),
            P(None, None, ("comp", "sub")),
            P(),
            P(("comp", "sub")),
            P(None, ("comp", "sub")),
            P(None, ("comp", "sub")),
            P(None, ("comp", "sub")),
            P(None, ("comp", "sub")),
        ),
        out_specs=(
            P(None, None, ("comp", "sub")),
            P(None, None, ("comp", "sub")),
            P(None, ("comp", "sub")),
        ),
        check_vma=False,
    )
```

```python
import jax
import jax.numpy as jnp
from jax import lax
from jax.experimental import pallas as pl
from jax.experimental.pallas import tpu as pltpu
from jax.sharding import PartitionSpec as P

couple_rate = 0.5
highest = lax.Precision.HIGHEST
high = lax.Precision.HIGH


def surface_fluxes(atmos_profiles, drag_factor, surface_before, downward_fluxes):
    bottom = atmos_profiles[:, -1, :].astype(jnp.float32)
    east_gap = bottom[2] - surface_before[2]
    north_gap = bottom[3] - surface_before[3]
    wind_speed = jnp.sqrt(1.0 + east_gap * east_gap + north_gap * north_gap)
    transfer = drag_factor * wind_speed
    sensible = transfer * (surface_before[0] - bottom[0])
    latent = transfer * (surface_before[1] - bottom[1])
    return jnp.stack(
        [
            sensible,
            latent,
            transfer * east_gap,
            transfer * north_gap,
            downward_fluxes[0],
            downward_fluxes[1],
            downward_fluxes[2],
            downward_fluxes[3],
        ]
    )


def atmos_kernel(mix_ref, low_ref, tend_ref, x_ref, out_ref):
    mix = mix_ref[...]
    low = low_ref[...]
    for member in range(x_ref.shape[0]):
        mixed = jnp.dot(mix, x_ref[member], preferred_element_type=jnp.float32)
        mixed = mixed + low * tend_ref[member : member + 1, :]
        out_ref[member] = mixed.astype(out_ref.dtype)


def diffuse_atmos(atmos_profiles, atmos_mixing, fluxes, block=2048):
    members, levels, columns = atmos_profiles.shape
    lowest = atmos_mixing[:, -1:].astype(jnp.float32)
    tendency = couple_rate * jnp.stack([fluxes[0], fluxes[1], -fluxes[2], -fluxes[3]])
    return pl.pallas_call(
        atmos_kernel,
        grid=(columns // block,),
        out_shape=jax.ShapeDtypeStruct(atmos_profiles.shape, jnp.bfloat16),
        in_specs=[
            pl.BlockSpec((levels, levels), lambda i: (0, 0)),
            pl.BlockSpec((levels, 1), lambda i: (0, 0)),
            pl.BlockSpec((members, block), lambda i: (0, i)),
            pl.BlockSpec((members, levels, block), lambda i: (0, 0, i)),
        ],
        out_specs=pl.BlockSpec((members, levels, block), lambda i: (0, 0, i)),
        cost_estimate=pl.CostEstimate(
            flops=2 * members * levels * levels * columns,
            bytes_accessed=4 * members * levels * columns,
            transcendentals=0,
        ),
    )(atmos_mixing, lowest, tendency, atmos_profiles)


def forcing_rows(fluxes):
    return couple_rate * jnp.stack(
        [
            fluxes[4] + fluxes[5] - fluxes[0] - fluxes[1],
            fluxes[1] - fluxes[6] - fluxes[7],
            fluxes[2],
            fluxes[3],
        ]
    )


def lane_gather_kernel(win_ref, lanes_ref, out_ref):
    lanes = lanes_ref[...]
    for field in range(win_ref.shape[0]):
        out_ref[field] = jnp.take_along_axis(
            win_ref[field], lanes, axis=1, mode="promise_in_bounds"
        )


def lane_gather(win, lanes):
    return pl.pallas_call(
        lane_gather_kernel,
        out_shape=jax.ShapeDtypeStruct(win.shape, win.dtype),
        in_specs=[pl.BlockSpec(memory_space=pltpu.VMEM)] * 2,
        out_specs=pl.BlockSpec(memory_space=pltpu.VMEM),
    )(win, lanes)


def split_kept(values):
    upper = lax.reduce_precision(values, exponent_bits=8, mantissa_bits=7)
    return upper.astype(jnp.bfloat16), (values - upper).astype(jnp.bfloat16)


def ocean_kernel(m_ref, m0_ref, x_ref, forcing_ref, sea_ref, out_ref):
    m = m_ref[...]
    m0 = m0_ref[...]
    sea = sea_ref[...] == 1
    for field in range(x_ref.shape[1]):
        x = x_ref[:, field, :]
        mixed = jnp.dot(m, x, precision=highest, preferred_element_type=jnp.float32)
        mixed = mixed + m0 * forcing_ref[field : field + 1, :]
        out_ref[:, field, :] = jnp.where(sea, mixed, x)


def ocean_update(ocean_mixing, state_by_level, forcing, sea_mask, block=2048):
    levels, fields, cells = state_by_level.shape
    return pl.pallas_call(
        ocean_kernel,
        grid=(cells // block,),
        out_shape=jax.ShapeDtypeStruct(state_by_level.shape, jnp.float32),
        in_specs=[
            pl.BlockSpec((levels, levels), lambda i: (0, 0)),
            pl.BlockSpec((levels, 1), lambda i: (0, 0)),
            pl.BlockSpec((levels, fields, block), lambda i: (0, 0, i)),
            pl.BlockSpec((fields, block), lambda i: (0, i)),
            pl.BlockSpec((1, block), lambda i: (0, i)),
        ],
        out_specs=pl.BlockSpec((levels, fields, block), lambda i: (0, 0, i)),
        cost_estimate=pl.CostEstimate(
            flops=12 * levels * levels * fields * cells,
            bytes_accessed=8 * levels * fields * cells,
            transcendentals=0,
        ),
    )(ocean_mixing, ocean_mixing[:, 0:1], state_by_level, forcing, sea_mask.reshape(1, cells))


def top_level_kernel(row_ref, x_ref, out_ref):
    total = row_ref[0] * x_ref[0]
    for level in range(1, x_ref.shape[0]):
        total = total + row_ref[level] * x_ref[level]
    out_ref[...] = total


def top_level_mix(first_row, state_by_level, block=4096):
    levels, fields, cells = state_by_level.shape
    return pl.pallas_call(
        top_level_kernel,
        grid=(cells // block,),
        out_shape=jax.ShapeDtypeStruct((fields, cells), jnp.float32),
        in_specs=[
            pl.BlockSpec(memory_space=pltpu.SMEM),
            pl.BlockSpec((levels, fields, block), lambda i: (0, 0, i)),
        ],
        out_specs=pl.BlockSpec((fields, block), lambda i: (0, i)),
        cost_estimate=pl.CostEstimate(
            flops=2 * levels * fields * cells,
            bytes_accessed=4 * (levels + 1) * fields * cells,
            transcendentals=0,
        ),
    )(first_row, state_by_level)


def lane_scatter_kernel(order_ref, keys_ref, last_ref, present_ref, val_ref, out_ref):
    order = order_ref[...]
    keys = keys_ref[...]
    last = last_ref[...]
    present = present_ref[...] > 0
    position = lax.broadcasted_iota(jnp.int32, keys.shape, 1)
    links = []
    shift = 1
    while shift < keys.shape[1]:
        joined = (position >= shift) & (pltpu.roll(keys, shift, 1) == keys)
        links.append((shift, joined))
        shift *= 2
    for field in range(val_ref.shape[0]):
        run = jnp.take_along_axis(val_ref[field], order, axis=1, mode="promise_in_bounds")
        for shift, joined in links:
            run = jnp.where(joined, run + pltpu.roll(run, shift, 1), run)
        picked = jnp.take_along_axis(run, last, axis=1, mode="promise_in_bounds")
        out_ref[field] = jnp.where(present, picked, 0.0)


def lane_scatter(values, order, keys, last, present):
    return pl.pallas_call(
        lane_scatter_kernel,
        out_shape=jax.ShapeDtypeStruct(values.shape, values.dtype),
        in_specs=[pl.BlockSpec(memory_space=pltpu.VMEM)] * 5,
        out_specs=pl.BlockSpec(memory_space=pltpu.VMEM),
    )(order, keys, last, present, values)


def lane_sort_kernel(key_ref, sorted_ref, present_ref, last_ref):
    values = key_ref[...]
    count = values.shape[1]
    position = lax.broadcasted_iota(jnp.int32, values.shape, 1)
    block = 2
    while block <= count:
        stride = block // 2
        while stride >= 1:
            lower = (position & stride) == 0
            partner = jnp.where(
                lower, pltpu.roll(values, count - stride, 1), pltpu.roll(values, stride, 1)
            )
            keep_min = lower == ((position & block) == 0)
            values = jnp.where(
                keep_min, jnp.minimum(values, partner), jnp.maximum(values, partner)
            )
            stride //= 2
        block *= 2
    sorted_ref[...] = values
    lanes = values // count
    below = jnp.zeros_like(position)
    step = count // 2
    while step >= 1:
        probe = jnp.take_along_axis(lanes, below + (step - 1), axis=1, mode="promise_in_bounds")
        below = jnp.where(probe <= position, below + step, below)
        step //= 2
    probe = jnp.take_along_axis(lanes, below, axis=1, mode="promise_in_bounds")
    below = jnp.where(probe <= position, below + 1, below)
    earlier = jnp.where(position >= 1, pltpu.roll(below, 1, 1), 0)
    present_ref[...] = below - earlier
    last_ref[...] = jnp.maximum(below - 1, 0)


def lane_sort(keys):
    return pl.pallas_call(
        lane_sort_kernel,
        out_shape=(jax.ShapeDtypeStruct(keys.shape, keys.dtype),) * 3,
        in_specs=[pl.BlockSpec(memory_space=pltpu.VMEM)],
        out_specs=(pl.BlockSpec(memory_space=pltpu.VMEM),) * 3,
    )(keys)


def return_prep_kernel(
    m00_ref, win_ref, lanes_ref, weight_ref, share_ref, base_ref, top0_ref, sea_ref,
    order_ref, keys_ref, last_ref, present_ref, partial_ref, forcing_ref,
):
    lanes = lanes_ref[...]
    parts = base_ref.shape[1]
    split = weight_ref.shape[0] // parts
    weight = weight_ref[...].reshape(split, parts, lanes.shape[1])
    total_weight = jnp.sum(weight, axis=0)
    share = share_ref[...]
    sea = sea_ref[...] == 1
    order = order_ref[...]
    keys = keys_ref[...]
    last = last_ref[...]
    present = present_ref[...] > 0
    position = lax.broadcasted_iota(jnp.int32, keys.shape, 1)
    links = []
    shift = 1
    while shift < keys.shape[1]:
        joined = (position >= shift) & (pltpu.roll(keys, shift, 1) == keys)
        links.append((shift, joined))
        shift *= 2

    def scatter(values):
        run = jnp.take_along_axis(values, order, axis=1, mode="promise_in_bounds")
        for step, joined in links:
            run = jnp.where(joined, run + pltpu.roll(run, step, 1), run)
        picked = jnp.take_along_axis(run, last, axis=1, mode="promise_in_bounds")
        return jnp.where(present, picked, 0.0)

    for field in range(win_ref.shape[0]):
        cells = jnp.take_along_axis(win_ref[field], lanes, axis=1, mode="promise_in_bounds")
        cells = cells.reshape(split, parts, lanes.shape[1])
        forcing = jnp.sum(weight * cells, axis=0) / total_weight
        forcing_ref[field] = forcing
        top = jnp.where(sea, base_ref[field] + m00_ref[0] * forcing, top0_ref[field])
        values = (share.reshape(split, parts, lanes.shape[1]) * top[None]).reshape(share.shape)
        partial_ref[field] = scatter(values)
    partial_ref[win_ref.shape[0]] = scatter(share)


def return_prep(m00, win, lanes, weight, share, base, top0, sea, order, keys, last, present):
    fields = win.shape[0]
    return pl.pallas_call(
        return_prep_kernel,
        out_shape=(
            jax.ShapeDtypeStruct((fields + 1,) + lanes.shape, jnp.float32),
            jax.ShapeDtypeStruct(base.shape, jnp.float32),
        ),
        in_specs=[pl.BlockSpec(memory_space=pltpu.SMEM)]
        + [pl.BlockSpec(memory_space=pltpu.VMEM)] * 11,
        out_specs=(
            pl.BlockSpec(memory_space=pltpu.VMEM),
            pl.BlockSpec(memory_space=pltpu.VMEM),
        ),
    )(m00, win, lanes, weight, share, base, top0, sea, order, keys, last, present)


def per_device(
    atmos_profiles,
    atmos_mixing,
    drag_factor,
    surface_before,
    downward_fluxes,
    land_weight,
    land_surface,
    ocean_state,
    ocean_mixing,
    sea_mask,
    exchange_slot,
    parent_column,
    ocean_weight,
    atmos_weight,
):
    comp_count = lax.axis_size("comp")
    sub_count = lax.axis_size("sub")
    devices = comp_count * sub_count
    columns = atmos_profiles.shape[2]
    intersections = exchange_slot.shape[0]
    ocean_cells = exchange_slot.shape[1]
    capacity = 2 * intersections * ocean_cells // devices
    width = min(128, capacity)
    tile_count = intersections * ocean_cells // width
    slot_tiles = devices * capacity // width
    windows = columns // width
    tile_place = exchange_slot.reshape(tile_count, width)[:, 0] // width
    placement = (tile_place[None, :] == jnp.arange(slot_tiles, dtype=jnp.int32)[:, None]).astype(
        jnp.float32
    )
    tiles_pc = parent_column.reshape(tile_count, width)
    window_of_tile = tiles_pc[:, 0] // width
    lanes = tiles_pc % width

    state_by_level = jnp.transpose(ocean_state, (1, 0, 2))

    request = jnp.dot(placement, window_of_tile.astype(jnp.float32), precision=highest)
    request = (request + 0.5).astype(jnp.int32).reshape(devices, slot_tiles // devices)
    asked = lax.all_to_all(request, ("comp", "sub"), split_axis=0, concat_axis=0, tiled=True)
    asked = asked.reshape(slot_tiles)
    ranked, present, last = lane_sort(
        lanes * width + lax.broadcasted_iota(jnp.int32, lanes.shape, 1)
    )
    ranked, present, last, asked = lax.optimization_barrier((ranked, present, last, asked))
    keys, order = ranked // width, ranked % width
    window_hot = (asked[:, None] == jnp.arange(windows, dtype=jnp.int32)[None, :]).astype(
        jnp.float32
    )

    fluxes = surface_fluxes(atmos_profiles, drag_factor, surface_before, downward_fluxes)
    column_forcing = forcing_rows(fluxes)
    served = jnp.einsum(
        "qw,fwl->qfl", window_hot, column_forcing.reshape(4, windows, width), precision=highest
    )
    late_lanes, late_state, served = lax.optimization_barrier((lanes, state_by_level, served))
    base_top = top_level_mix(ocean_mixing[0], late_state)
    arrived = lax.all_to_all(
        served.reshape(devices, -1), ("comp", "sub"), split_axis=0, concat_axis=0, tiled=True
    )
    win_local = jnp.einsum(
        "qt,qfl->ftl", placement, arrived.reshape(slot_tiles, 4, width), precision=highest
    )
    parts = ocean_cells // width
    sea_share = atmos_weight * sea_mask.astype(jnp.float32)[None, :]
    partial, forcing = return_prep(
        ocean_mixing[0, 0:1],
        win_local,
        late_lanes,
        ocean_weight.reshape(tile_count, width),
        sea_share.reshape(tile_count, width),
        base_top.reshape(4, parts, width),
        late_state[0].reshape(4, parts, width),
        sea_mask.reshape(parts, width),
        order,
        keys,
        last,
        present,
    )
    forcing = forcing.reshape(4, ocean_cells)
    send_buffer = jnp.einsum("qt,ftc->qfc", placement, partial, precision=highest)
    late_profiles, send_buffer = lax.optimization_barrier((atmos_profiles, send_buffer))
    atmos_updated = diffuse_atmos(late_profiles, atmos_mixing, fluxes)
    returned = lax.all_to_all(
        send_buffer.reshape(devices, -1), ("comp", "sub"), split_axis=0, concat_axis=0, tiled=True
    )
    summed = jnp.einsum(
        "qw,qfc->fwc", window_hot, returned.reshape(slot_tiles, 5, width), precision=highest
    ).reshape(5, columns)
    updated_by_level = ocean_update(ocean_mixing, state_by_level, forcing, sea_mask)
    ocean_updated = jnp.transpose(updated_by_level, (1, 0, 2))
    surface_state = (summed[:4] + land_weight[None] * land_surface) / (summed[4] + land_weight)[
        None
    ]
    return (atmos_updated, ocean_updated, surface_state)


def solution(mesh):
    return jax.shard_map(
        per_device,
        mesh=mesh,
        in_specs=(
            P(None, None, ("comp", "sub")),
            P(),
            P(("comp", "sub")),
            P(None, ("comp", "sub")),
            P(None, ("comp", "sub")),
            P(("comp", "sub")),
            P(None, ("comp", "sub")),
            P(None, None, ("comp", "sub")),
            P(),
            P(("comp", "sub")),
            P(None, ("comp", "sub")),
            P(None, ("comp", "sub")),
            P(None, ("comp", "sub")),
            P(None, ("comp", "sub")),
        ),
        out_specs=(
            P(None, None, ("comp", "sub")),
            P(None, None, ("comp", "sub")),
            P(None, ("comp", "sub")),
        ),
        check_vma=False,
    )
```

```python
import jax
import jax.numpy as jnp
from jax import lax
from jax.experimental import pallas as pl
from jax.experimental.pallas import tpu as pltpu
from jax.sharding import PartitionSpec as P

couple_rate = 0.5
highest = lax.Precision.HIGHEST
high = lax.Precision.HIGH


def surface_fluxes(atmos_profiles, drag_factor, surface_before, downward_fluxes):
    bottom = atmos_profiles[:, -1, :].astype(jnp.float32)
    east_gap = bottom[2] - surface_before[2]
    north_gap = bottom[3] - surface_before[3]
    wind_speed = jnp.sqrt(1.0 + east_gap * east_gap + north_gap * north_gap)
    transfer = drag_factor * wind_speed
    sensible = transfer * (surface_before[0] - bottom[0])
    latent = transfer * (surface_before[1] - bottom[1])
    return jnp.stack(
        [
            sensible,
            latent,
            transfer * east_gap,
            transfer * north_gap,
            downward_fluxes[0],
            downward_fluxes[1],
            downward_fluxes[2],
            downward_fluxes[3],
        ]
    )


def atmos_kernel(mix_ref, low_ref, tend_ref, x_ref, out_ref):
    mix = mix_ref[...]
    low = low_ref[...]
    for member in range(x_ref.shape[0]):
        mixed = jnp.dot(mix, x_ref[member], preferred_element_type=jnp.float32)
        mixed = mixed + low * tend_ref[member : member + 1, :]
        out_ref[member] = mixed.astype(out_ref.dtype)


def diffuse_atmos(atmos_profiles, atmos_mixing, fluxes, block=1024):
    members, levels, columns = atmos_profiles.shape
    lowest = atmos_mixing[:, -1:].astype(jnp.float32)
    tendency = couple_rate * jnp.stack([fluxes[0], fluxes[1], -fluxes[2], -fluxes[3]])
    return pl.pallas_call(
        atmos_kernel,
        grid=(columns // block,),
        out_shape=jax.ShapeDtypeStruct(atmos_profiles.shape, jnp.bfloat16),
        in_specs=[
            pl.BlockSpec((levels, levels), lambda i: (0, 0)),
            pl.BlockSpec((levels, 1), lambda i: (0, 0)),
            pl.BlockSpec((members, block), lambda i: (0, i)),
            pl.BlockSpec((members, levels, block), lambda i: (0, 0, i)),
        ],
        out_specs=pl.BlockSpec((members, levels, block), lambda i: (0, 0, i)),
        cost_estimate=pl.CostEstimate(
            flops=2 * members * levels * levels * columns,
            bytes_accessed=4 * members * levels * columns,
            transcendentals=0,
        ),
    )(atmos_mixing, lowest, tendency, atmos_profiles)


def forcing_rows(fluxes):
    return couple_rate * jnp.stack(
        [
            fluxes[4] + fluxes[5] - fluxes[0] - fluxes[1],
            fluxes[1] - fluxes[6] - fluxes[7],
            fluxes[2],
            fluxes[3],
        ]
    )


def lane_gather_kernel(win_ref, lanes_ref, out_ref):
    lanes = lanes_ref[...]
    for field in range(win_ref.shape[0]):
        out_ref[field] = jnp.take_along_axis(
            win_ref[field], lanes, axis=1, mode="promise_in_bounds"
        )


def lane_gather(win, lanes):
    return pl.pallas_call(
        lane_gather_kernel,
        out_shape=jax.ShapeDtypeStruct(win.shape, win.dtype),
        in_specs=[pl.BlockSpec(memory_space=pltpu.VMEM)] * 2,
        out_specs=pl.BlockSpec(memory_space=pltpu.VMEM),
    )(win, lanes)


def split_kept(values):
    upper = lax.reduce_precision(values, exponent_bits=8, mantissa_bits=7)
    return upper.astype(jnp.bfloat16), (values - upper).astype(jnp.bfloat16)


def ocean_kernel(m_ref, m0_ref, x_ref, forcing_ref, sea_ref, out_ref):
    m = m_ref[...]
    m0 = m0_ref[...]
    sea = sea_ref[...] == 1
    for field in range(x_ref.shape[1]):
        x = x_ref[:, field, :]
        mixed = jnp.dot(m, x, precision=highest, preferred_element_type=jnp.float32)
        mixed = mixed + m0 * forcing_ref[field : field + 1, :]
        out_ref[:, field, :] = jnp.where(sea, mixed, x)


def ocean_update(ocean_mixing, state_by_level, forcing, sea_mask, block=2048):
    levels, fields, cells = state_by_level.shape
    return pl.pallas_call(
        ocean_kernel,
        grid=(cells // block,),
        out_shape=jax.ShapeDtypeStruct(state_by_level.shape, jnp.float32),
        in_specs=[
            pl.BlockSpec((levels, levels), lambda i: (0, 0)),
            pl.BlockSpec((levels, 1), lambda i: (0, 0)),
            pl.BlockSpec((levels, fields, block), lambda i: (0, 0, i)),
            pl.BlockSpec((fields, block), lambda i: (0, i)),
            pl.BlockSpec((1, block), lambda i: (0, i)),
        ],
        out_specs=pl.BlockSpec((levels, fields, block), lambda i: (0, 0, i)),
        cost_estimate=pl.CostEstimate(
            flops=12 * levels * levels * fields * cells,
            bytes_accessed=8 * levels * fields * cells,
            transcendentals=0,
        ),
    )(ocean_mixing, ocean_mixing[:, 0:1], state_by_level, forcing, sea_mask.reshape(1, cells))


def top_level_kernel(row_ref, x_ref, out_ref):
    total = row_ref[0] * x_ref[0]
    for level in range(1, x_ref.shape[0]):
        total = total + row_ref[level] * x_ref[level]
    out_ref[...] = total


def top_level_mix(first_row, state_by_level, block=4096):
    levels, fields, cells = state_by_level.shape
    return pl.pallas_call(
        top_level_kernel,
        grid=(cells // block,),
        out_shape=jax.ShapeDtypeStruct((fields, cells), jnp.float32),
        in_specs=[
            pl.BlockSpec(memory_space=pltpu.SMEM),
            pl.BlockSpec((levels, fields, block), lambda i: (0, 0, i)),
        ],
        out_specs=pl.BlockSpec((fields, block), lambda i: (0, i)),
        cost_estimate=pl.CostEstimate(
            flops=2 * levels * fields * cells,
            bytes_accessed=4 * (levels + 1) * fields * cells,
            transcendentals=0,
        ),
    )(first_row, state_by_level)


def lane_scatter_kernel(order_ref, keys_ref, last_ref, present_ref, val_ref, out_ref):
    order = order_ref[...]
    keys = keys_ref[...]
    last = last_ref[...]
    present = present_ref[...] > 0
    position = lax.broadcasted_iota(jnp.int32, keys.shape, 1)
    links = []
    shift = 1
    while shift < keys.shape[1]:
        joined = (position >= shift) & (pltpu.roll(keys, shift, 1) == keys)
        links.append((shift, joined))
        shift *= 2
    for field in range(val_ref.shape[0]):
        run = jnp.take_along_axis(val_ref[field], order, axis=1, mode="promise_in_bounds")
        for shift, joined in links:
            run = jnp.where(joined, run + pltpu.roll(run, shift, 1), run)
        picked = jnp.take_along_axis(run, last, axis=1, mode="promise_in_bounds")
        out_ref[field] = jnp.where(present, picked, 0.0)


def lane_scatter(values, order, keys, last, present):
    return pl.pallas_call(
        lane_scatter_kernel,
        out_shape=jax.ShapeDtypeStruct(values.shape, values.dtype),
        in_specs=[pl.BlockSpec(memory_space=pltpu.VMEM)] * 5,
        out_specs=pl.BlockSpec(memory_space=pltpu.VMEM),
    )(order, keys, last, present, values)


def lane_sort_kernel(key_ref, sorted_ref, present_ref, last_ref):
    values = key_ref[...]
    count = values.shape[1]
    position = lax.broadcasted_iota(jnp.int32, values.shape, 1)
    block = 2
    while block <= count:
        stride = block // 2
        while stride >= 1:
            lower = (position & stride) == 0
            partner = jnp.where(
                lower, pltpu.roll(values, count - stride, 1), pltpu.roll(values, stride, 1)
            )
            keep_min = lower == ((position & block) == 0)
            values = jnp.where(
                keep_min, jnp.minimum(values, partner), jnp.maximum(values, partner)
            )
            stride //= 2
        block *= 2
    sorted_ref[...] = values
    lanes = values // count
    below = jnp.zeros_like(position)
    step = count // 2
    while step >= 1:
        probe = jnp.take_along_axis(lanes, below + (step - 1), axis=1, mode="promise_in_bounds")
        below = jnp.where(probe <= position, below + step, below)
        step //= 2
    probe = jnp.take_along_axis(lanes, below, axis=1, mode="promise_in_bounds")
    below = jnp.where(probe <= position, below + 1, below)
    earlier = jnp.where(position >= 1, pltpu.roll(below, 1, 1), 0)
    present_ref[...] = below - earlier
    last_ref[...] = jnp.maximum(below - 1, 0)


def lane_sort(keys):
    return pl.pallas_call(
        lane_sort_kernel,
        out_shape=(jax.ShapeDtypeStruct(keys.shape, keys.dtype),) * 3,
        in_specs=[pl.BlockSpec(memory_space=pltpu.VMEM)],
        out_specs=(pl.BlockSpec(memory_space=pltpu.VMEM),) * 3,
    )(keys)


def return_prep_kernel(
    m00_ref, win_ref, lanes_ref, weight_ref, share_ref, base_ref, top0_ref, sea_ref,
    order_ref, keys_ref, last_ref, present_ref, partial_ref, forcing_ref,
):
    lanes = lanes_ref[...]
    parts = base_ref.shape[1]
    split = weight_ref.shape[0] // parts
    weight = weight_ref[...].reshape(split, parts, lanes.shape[1])
    total_weight = jnp.sum(weight, axis=0)
    share = share_ref[...]
    sea = sea_ref[...] == 1
    order = order_ref[...]
    keys = keys_ref[...]
    last = last_ref[...]
    present = present_ref[...] > 0
    position = lax.broadcasted_iota(jnp.int32, keys.shape, 1)
    links = []
    shift = 1
    while shift < keys.shape[1]:
        joined = (position >= shift) & (pltpu.roll(keys, shift, 1) == keys)
        links.append((shift, joined))
        shift *= 2

    def scatter(values):
        run = jnp.take_along_axis(values, order, axis=1, mode="promise_in_bounds")
        for step, joined in links:
            run = jnp.where(joined, run + pltpu.roll(run, step, 1), run)
        picked = jnp.take_along_axis(run, last, axis=1, mode="promise_in_bounds")
        return jnp.where(present, picked, 0.0)

    for field in range(win_ref.shape[0]):
        cells = jnp.take_along_axis(win_ref[field], lanes, axis=1, mode="promise_in_bounds")
        cells = cells.reshape(split, parts, lanes.shape[1])
        forcing = jnp.sum(weight * cells, axis=0) / total_weight
        forcing_ref[field] = forcing
        top = jnp.where(sea, base_ref[field] + m00_ref[0] * forcing, top0_ref[field])
        values = (share.reshape(split, parts, lanes.shape[1]) * top[None]).reshape(share.shape)
        partial_ref[field] = scatter(values)
    partial_ref[win_ref.shape[0]] = scatter(share)


def return_prep(m00, win, lanes, weight, share, base, top0, sea, order, keys, last, present):
    fields = win.shape[0]
    return pl.pallas_call(
        return_prep_kernel,
        out_shape=(
            jax.ShapeDtypeStruct((fields + 1,) + lanes.shape, jnp.float32),
            jax.ShapeDtypeStruct(base.shape, jnp.float32),
        ),
        in_specs=[pl.BlockSpec(memory_space=pltpu.SMEM)]
        + [pl.BlockSpec(memory_space=pltpu.VMEM)] * 11,
        out_specs=(
            pl.BlockSpec(memory_space=pltpu.VMEM),
            pl.BlockSpec(memory_space=pltpu.VMEM),
        ),
    )(m00, win, lanes, weight, share, base, top0, sea, order, keys, last, present)


def per_device(
    atmos_profiles,
    atmos_mixing,
    drag_factor,
    surface_before,
    downward_fluxes,
    land_weight,
    land_surface,
    ocean_state,
    ocean_mixing,
    sea_mask,
    exchange_slot,
    parent_column,
    ocean_weight,
    atmos_weight,
):
    comp_count = lax.axis_size("comp")
    sub_count = lax.axis_size("sub")
    devices = comp_count * sub_count
    columns = atmos_profiles.shape[2]
    intersections = exchange_slot.shape[0]
    ocean_cells = exchange_slot.shape[1]
    capacity = 2 * intersections * ocean_cells // devices
    width = min(128, capacity)
    tile_count = intersections * ocean_cells // width
    slot_tiles = devices * capacity // width
    windows = columns // width
    tile_place = exchange_slot.reshape(tile_count, width)[:, 0] // width
    placement = (tile_place[None, :] == jnp.arange(slot_tiles, dtype=jnp.int32)[:, None]).astype(
        jnp.float32
    )
    tiles_pc = parent_column.reshape(tile_count, width)
    window_of_tile = tiles_pc[:, 0] // width
    lanes = tiles_pc % width

    state_by_level = jnp.transpose(ocean_state, (1, 0, 2))

    request = jnp.dot(placement, window_of_tile.astype(jnp.float32), precision=highest)
    request = (request + 0.5).astype(jnp.int32).reshape(devices, slot_tiles // devices)
    asked = lax.all_to_all(request, ("comp", "sub"), split_axis=0, concat_axis=0, tiled=True)
    asked = asked.reshape(slot_tiles)
    window_hot = (asked[:, None] == jnp.arange(windows, dtype=jnp.int32)[None, :]).astype(
        jnp.float32
    )

    fluxes = surface_fluxes(atmos_profiles, drag_factor, surface_before, downward_fluxes)
    column_forcing = forcing_rows(fluxes)
    served = jnp.einsum(
        "qw,fwl->qfl", window_hot, column_forcing.reshape(4, windows, width), precision=highest
    )
    late_lanes, late_state, served = lax.optimization_barrier((lanes, state_by_level, served))
    base_top = top_level_mix(ocean_mixing[0], late_state)
    ranked, present, last = lane_sort(
        late_lanes * width + lax.broadcasted_iota(jnp.int32, late_lanes.shape, 1)
    )
    keys, order = ranked // width, ranked % width
    arrived = lax.all_to_all(
        served.reshape(devices, -1), ("comp", "sub"), split_axis=0, concat_axis=0, tiled=True
    )
    win_local = jnp.einsum(
        "qt,qfl->ftl", placement, arrived.reshape(slot_tiles, 4, width), precision=highest
    )
    parts = ocean_cells // width
    sea_share = atmos_weight * sea_mask.astype(jnp.float32)[None, :]
    partial, forcing = return_prep(
        ocean_mixing[0, 0:1],
        win_local,
        late_lanes,
        ocean_weight.reshape(tile_count, width),
        sea_share.reshape(tile_count, width),
        base_top.reshape(4, parts, width),
        late_state[0].reshape(4, parts, width),
        sea_mask.reshape(parts, width),
        order,
        keys,
        last,
        present,
    )
    forcing = forcing.reshape(4, ocean_cells)
    send_buffer = jnp.einsum("qt,ftc->qfc", placement, partial, precision=highest)
    late_profiles, send_buffer = lax.optimization_barrier((atmos_profiles, send_buffer))
    atmos_updated = diffuse_atmos(late_profiles, atmos_mixing, fluxes)
    returned = lax.all_to_all(
        send_buffer.reshape(devices, -1), ("comp", "sub"), split_axis=0, concat_axis=0, tiled=True
    )
    summed = jnp.einsum(
        "qw,qfc->fwc", window_hot, returned.reshape(slot_tiles, 5, width), precision=highest
    ).reshape(5, columns)
    updated_by_level = ocean_update(ocean_mixing, state_by_level, forcing, sea_mask)
    ocean_updated = jnp.transpose(updated_by_level, (1, 0, 2))
    surface_state = (summed[:4] + land_weight[None] * land_surface) / (summed[4] + land_weight)[
        None
    ]
    return (atmos_updated, ocean_updated, surface_state)


def solution(mesh):
    return jax.shard_map(
        per_device,
        mesh=mesh,
        in_specs=(
            P(None, None, ("comp", "sub")),
            P(),
            P(("comp", "sub")),
            P(None, ("comp", "sub")),
            P(None, ("comp", "sub")),
            P(("comp", "sub")),
            P(None, ("comp", "sub")),
            P(None, None, ("comp", "sub")),
            P(),
            P(("comp", "sub")),
            P(None, ("comp", "sub")),
            P(None, ("comp", "sub")),
            P(None, ("comp", "sub")),
            P(None, ("comp", "sub")),
        ),
        out_specs=(
            P(None, None, ("comp", "sub")),
            P(None, None, ("comp", "sub")),
            P(None, ("comp", "sub")),
        ),
        check_vma=False,
    )
```
